32 devices in a mesh: fsdp: 8 (over y, x, core), seq: 4 (over z).
Axes of the slice: x: 2, y: 2, z: 4, core: 2. Of those that a mesh axis runs over, the one named last changes fastest.
Arguments:
- tokens: bfloat16 [8192, 768], P(('fsdp', 'seq')), may hold values from -6 to 6
- memory: bfloat16 [8, 20, 768], P('fsdp'), may hold values from -6 to 6
- lengths: int32 [8], P('fsdp'), may hold values from 256 to 1004, as said below
- w_qkv: bfloat16 [2, 768, 2304], P(None, 'fsdp'), may hold values from -0.21875 to 0.21875
- b_qv: bfloat16 [2, 1536], P(None, 'fsdp'), may hold values from -1.5 to 1.5
- w_out: bfloat16 [2, 768, 768], P(None, 'fsdp'), may hold values from -2 to 2
- b_out: bfloat16 [2, 768], P(None, 'fsdp'), may hold values from -1.5 to 1.5
- gain_attn: bfloat16 [2, 768], P(None, 'fsdp'), may hold values from 0.5 to 1.5
- shift_attn: bfloat16 [2, 768], P(None, 'fsdp'), may hold values from -1.5 to 1.5
- w_up: bfloat16 [2, 768, 3072], P(None, 'fsdp'), may hold values from -0.21875 to 0.21875
- b_up: bfloat16 [2, 3072], P(None, 'fsdp'), may hold values from -1.5 to 1.5
- w_down: bfloat16 [2, 3072, 768], P(None, 'fsdp'), may hold values from -0.109375 to 0.109375
- b_down: bfloat16 [2, 768], P(None, 'fsdp'), may hold values from -1.5 to 1.5
- gain_ffn: bfloat16 [2, 768], P(None, 'fsdp'), may hold values from 0.5 to 1.5
- shift_ffn: bfloat16 [2, 768], P(None, 'fsdp'), may hold values from -1.5 to 1.5
- cotangent: float32 [8192, 768], P(('fsdp', 'seq')), may hold values from -6 to 6
Outputs:
- result: float32 [8192, 768], P(('fsdp', 'seq'))
- grad_tokens: float32 [8192, 768], P(('fsdp', 'seq'))
- grad_memory: float32 [8, 20, 768], P('fsdp')
- grad_w_qkv: float32 [2, 768, 2304], P(None, 'fsdp')
- grad_b_qv: float32 [2, 1536], P(None, 'fsdp')
- grad_w_out: float32 [2, 768, 768], P(None, 'fsdp')
- grad_b_out: float32 [2, 768], P(None, 'fsdp')
- grad_gain_attn: float32 [2, 768], P(None, 'fsdp')
- grad_shift_attn: float32 [2, 768], P(None, 'fsdp')
- grad_w_up: float32 [2, 768, 3072], P(None, 'fsdp')
- grad_b_up: float32 [2, 3072], P(None, 'fsdp')
- grad_w_down: float32 [2, 3072, 768], P(None, 'fsdp')
- grad_b_down: float32 [2, 768], P(None, 'fsdp')
- grad_gain_ffn: float32 [2, 768], P(None, 'fsdp')
- grad_shift_ffn: float32 [2, 768], P(None, 'fsdp')
The draws below stay inside these ranges and needn't reach their ends.
Inputs may be any that keep to these rules, and one draw needn't show every extreme that they name: `lengths`: one sequence has exactly 1004 token rows and another exactly 256.
All inputs are finite; a program needn't handle non-finite values.
Results may differ from the reference program's by a relative error of at most 0.018.
Values may be sent and summed in bfloat16 or wider, within the bound.
A program may use at most 192 MiB of HBM per device.

```python
import math
import jax
import jax.numpy as jnp
from jax import lax

D = 768
HEADS = 12
HD = 64
FF = 3072
MEM = 10
LAYERS = 2
SEQ_LEN = 1024
SEQS = 8
ROWS = 8192


def draw_lengths(key, part):
    shortest = SEQ_LEN // 4
    longest = SEQ_LEN - 2 * MEM
    key_value, key_order = jax.random.split(key)
    values = jax.random.randint(key_value, (SEQS,), shortest, longest + 1)
    shuffled = jax.random.permutation(key_order, SEQS)
    seq_index = jnp.arange(SEQS)
    values = jnp.where(seq_index == shuffled[0], longest, values)
    values = jnp.where(seq_index == shuffled[1], shortest, values)
    return values.astype(jnp.int32)


def block_scale(key, extent, cuts, low, largest):
    def one(dim, parts):
        draws = jax.random.uniform(jax.random.fold_in(jax.random.fold_in(key, 6), dim), (parts,), jnp.float32, low / len(cuts), largest / len(cuts))
        return jnp.repeat(jnp.exp(draws), extent[dim] // parts).reshape((-1,) + (1,) * (len(extent) - dim - 1))

    loudness = one(*cuts[0])
    for cut in cuts[1:]:
        loudness = loudness * one(*cut)
    return loudness


def bell_draw(rng, extent, width, reach, cuts=(), kind=jnp.bfloat16):
    loudness = block_scale(rng, extent, cuts, -0.22, 0.18) if cuts else 1.0
    array = jax.random.normal(rng, extent, jnp.float32) * width * loudness
    return jnp.minimum(jnp.maximum(array, -reach), reach).astype(kind)


def setup_inputs(seed: int = 0) -> dict:
    splits = jax.random.split(jax.random.key(seed), 17)
    return {
        "tokens": bell_draw(splits[0], (ROWS, D), 1.0, 6.0, ((0, 32),)),
        "memory": bell_draw(splits[1], (SEQS, 2 * MEM, D), 1.0, 6.0, ((0, 8),)),
        "lengths": draw_lengths(jax.random.fold_in(splits[16], 71), 0),
        "w_qkv": bell_draw(splits[3], (LAYERS, D, 3 * D), D ** -0.5, 0.21875, ((1, 8),)),
        "b_qv": bell_draw(splits[4], (LAYERS, 2 * D), 0.25, 1.5, ((1, 8),)),
        "w_out": bell_draw(splits[5], (LAYERS, D, D), (max(8, D * 8 // SEQ_LEN)) ** -0.5, 2.0, ((1, 8),)),
        "b_out": bell_draw(splits[6], (LAYERS, D), 0.25, 1.5, ((1, 8),)),
        "gain_attn": jnp.clip(1.0 + 0.1 * jax.random.normal(splits[7], (LAYERS, D), jnp.float32), 0.5, 1.5).astype(jnp.bfloat16),
        "shift_attn": bell_draw(splits[8], (LAYERS, D), 0.25, 1.5, ((1, 8),)),
        "w_up": bell_draw(splits[9], (LAYERS, D, FF), D ** -0.5, 0.21875, ((1, 8),)),
        "b_up": bell_draw(splits[10], (LAYERS, FF), 0.25, 1.5, ((1, 8),)),
        "w_down": bell_draw(splits[11], (LAYERS, FF, D), FF ** -0.5, 0.109375, ((1, 8),)),
        "b_down": bell_draw(splits[12], (LAYERS, D), 0.25, 1.5, ((1, 8),)),
        "gain_ffn": jnp.clip(1.0 + 0.1 * jax.random.normal(splits[13], (LAYERS, D), jnp.float32), 0.5, 1.5).astype(jnp.bfloat16),
        "shift_ffn": bell_draw(splits[14], (LAYERS, D), 0.25, 1.5, ((1, 8),)),
        "cotangent": bell_draw(splits[15], (ROWS, D), 1.0, 6.0, ((0, 32),), jnp.float32),
    }


@jax.custom_vjp
def low(v):
    return lax.optimization_barrier(v.astype(jnp.bfloat16)).astype(jnp.float32)

@jax.custom_vjp
def low_back(v):
    return v

def low_keep(v):
    return (low(v), None)

def low_pass(kept, grad):
    return (grad,)

def back_keep(v):
    return (v, None)

def back_low(kept, grad):
    return (low(grad),)
low.defvjp(low_keep, low_pass)
low_back.defvjp(back_keep, back_low)
norm_eps = 1e-12
masked_score = -1e+30

def matmul(left, right):
    return jnp.dot(left, right, precision=lax.Precision.HIGHEST)

def norm_rows(values, gain_vec, shift_vec):
    row_mean = lax.optimization_barrier(jnp.mean(values, axis=-1, keepdims=True))
    centred = values - row_mean
    variance = lax.optimization_barrier(jnp.mean(centred * centred, axis=-1, keepdims=True))
    return centred * lax.rsqrt(variance + norm_eps) * gain_vec + shift_vec

def attention(queries, keys_all, values_all, key_live):
    total_rows = queries.shape[0]
    block_rows = math.gcd(total_rows, 512)
    block_count = total_rows // block_rows
    score_scale = HD ** (-0.5)

    def one_block(query_block):
        scores = jnp.einsum('qhd,khd->hqk', query_block, keys_all, precision=lax.Precision.HIGHEST) * score_scale
        scores = low_back(scores)
        scores = jnp.where(key_live[None, None, :], scores, masked_score)
        top_score = lax.optimization_barrier(jnp.max(scores, axis=-1, keepdims=True))
        exponent = jnp.exp(scores - top_score)
        probability = low(exponent / lax.optimization_barrier(jnp.sum(exponent, axis=-1, keepdims=True)))
        return jnp.einsum('hqk,khd->qhd', probability, values_all, precision=lax.Precision.HIGHEST)
    blocks = queries.reshape(block_count, block_rows, queries.shape[1], queries.shape[2])
    context = lax.map(jax.checkpoint(one_block), blocks)
    return context.reshape(queries.shape)

def encoder_layer(hidden, params, key_live):
    w_qkv, b_qv, w_out, b_out, gain_attn, shift_attn, w_up, b_up, w_down, b_down, gain_ffn, shift_ffn = params
    total_rows = hidden.shape[0]
    bias_full = jnp.concatenate([b_qv[:D], jnp.zeros((D,), jnp.float32), b_qv[D:]])
    projected = low(low_back(matmul(low(hidden), w_qkv) + bias_full))
    split_heads = projected.reshape(total_rows, 3, HEADS, HD)
    context = attention(split_heads[:, 0], split_heads[:, 1], split_heads[:, 2], key_live)
    context = low(low_back(context.reshape(total_rows, D)))
    attended = low_back(matmul(context, w_out) + b_out)
    normed = norm_rows(hidden + attended, gain_attn, shift_attn)
    pre_gelu = low_back(matmul(low(normed), w_up) + b_up)
    active = low(jax.nn.gelu(pre_gelu, approximate=False))
    branch_out = low_back(matmul(active, w_down) + b_down)
    return norm_rows(normed + branch_out, gain_ffn, shift_ffn)

def reference(tokens, memory, lengths, w_qkv, b_qv, w_out, b_out, gain_attn, shift_attn, w_up, b_up, w_down, b_down, gain_ffn, shift_ffn, cotangent):
    weights = tuple((item.astype(jnp.float32) for item in (w_qkv, b_qv, w_out, b_out, gain_attn, shift_attn, w_up, b_up, w_down, b_down, gain_ffn, shift_ffn)))
    token_rows = tokens.astype(jnp.float32).reshape(SEQS, SEQ_LEN, D)
    memory_rows = memory.astype(jnp.float32)
    grad_rows = cotangent.reshape(SEQS, SEQ_LEN, D)
    positions = jnp.arange(SEQ_LEN, dtype=jnp.int32)
    memory_slots = jnp.arange(2 * MEM, dtype=jnp.int32)

    def one_sequence(totals, inputs):
        token_seq, memory_seq, length, grad_out = inputs
        live_rows = positions < length + 2 * MEM
        token_live = (positions >= MEM) & (positions < length + MEM)
        targets = jnp.where(memory_slots < MEM, memory_slots, length + memory_slots)
        select = (positions[:, None] == targets[None, :]).astype(jnp.float32)

        def forward(token_in, memory_in, params):
            hidden = jnp.where(token_live[:, None], token_in, 0.0) + matmul(select, memory_in)
            for layer_index in range(LAYERS):
                hidden = encoder_layer(hidden, tuple((stacked[layer_index] for stacked in params)), live_rows)
            return jnp.where(live_rows[:, None], hidden, 0.0)
        output, pullback = jax.vjp(forward, token_seq, memory_seq, weights)
        grad_token, grad_mem, grad_params = pullback(grad_out)
        totals = jax.tree.map(lambda a, b: a + b, totals, grad_params)
        return (totals, (output, grad_token, grad_mem))
    zero_grads = jax.tree.map(jnp.zeros_like, weights)
    totals, (outputs, grad_token, grad_mem) = lax.scan(one_sequence, zero_grads, (token_rows, memory_rows, lengths, grad_rows))
    return (outputs.reshape(ROWS, D), grad_token.reshape(ROWS, D), grad_mem, totals[0], totals[1], totals[2], totals[3], totals[4], totals[5], totals[6], totals[7], totals[8], totals[9], totals[10], totals[11])
```

```python
import math

import jax
import jax.numpy as jnp
from jax import lax
from jax.sharding import PartitionSpec as P

D = 768
HEADS = 12
HD = 64
MEM = 10
LAYERS = 2


norm_eps = 1e-12
masked_score = -1e30


def norm_rows(values, gain_vec, shift_vec):
    row_mean = jnp.mean(values, axis=-1, keepdims=True)
    centred = values - row_mean
    variance = jnp.mean(centred * centred, axis=-1, keepdims=True)
    return centred * lax.rsqrt(variance + norm_eps) * gain_vec + shift_vec


def gelu_exact(values):
    return jax.nn.gelu(values, approximate=False)


def gather_layer(stacks, layer_index):
    (
        w_qkv,
        b_qv,
        w_out,
        b_out,
        gain_attn,
        shift_attn,
        w_up,
        b_up,
        w_down,
        b_down,
        gain_ffn,
        shift_ffn,
    ) = tuple((stacked[layer_index] for stacked in stacks))
    return (
        lax.all_gather(w_qkv, "fsdp", axis=0, tiled=True),
        lax.all_gather(b_qv, "fsdp", axis=0, tiled=True),
        lax.all_gather(w_out, "fsdp", axis=0, tiled=True),
        lax.all_gather(b_out, "fsdp", axis=0, tiled=True),
        lax.all_gather(gain_attn, "fsdp", axis=0, tiled=True),
        lax.all_gather(shift_attn, "fsdp", axis=0, tiled=True),
        lax.all_gather(w_up, "fsdp", axis=0, tiled=True),
        lax.all_gather(b_up, "fsdp", axis=0, tiled=True),
        lax.all_gather(w_down, "fsdp", axis=0, tiled=True),
        lax.all_gather(b_down, "fsdp", axis=0, tiled=True),
        lax.all_gather(gain_ffn, "fsdp", axis=0, tiled=True),
        lax.all_gather(shift_ffn, "fsdp", axis=0, tiled=True),
    )


def attend_forward(queries, keys_all, values_all, key_live):
    total_rows, local_heads = (queries.shape[0], queries.shape[1])
    block_rows = math.gcd(total_rows, 512)
    block_count = total_rows // block_rows
    score_scale = HD ** (-0.5)

    def one_block(query_block):
        scores = (
            jnp.einsum("qhd,khd->hqk", query_block, keys_all, preferred_element_type=jnp.float32)
            * score_scale
        )
        scores = jnp.where(key_live[None, None, :], scores, masked_score)
        top_score = jnp.max(scores, axis=-1, keepdims=True)
        exponent = jnp.exp(scores - top_score)
        row_total = jnp.sum(exponent, axis=-1, keepdims=True)
        probability = (exponent / row_total).astype(jnp.bfloat16)
        context = jnp.einsum(
            "hqk,khd->qhd", probability, values_all, preferred_element_type=jnp.float32
        )
        return (context.astype(jnp.bfloat16), (top_score + jnp.log(row_total))[..., 0])

    blocks = queries.reshape(block_count, block_rows, local_heads, HD)
    context, log_total = lax.map(one_block, blocks)
    return (context.reshape(total_rows, local_heads, HD), log_total)


def attend_backward(queries, keys_all, values_all, grad_context, log_total, key_live):
    total_rows, local_heads = (queries.shape[0], queries.shape[1])
    block_rows = math.gcd(total_rows, 512)
    block_count = total_rows // block_rows
    score_scale = HD ** (-0.5)

    def one_block(running, inputs):
        grad_keys, grad_values = running
        query_block, grad_block, log_block = inputs
        scores = (
            jnp.einsum("qhd,khd->hqk", query_block, keys_all, preferred_element_type=jnp.float32)
            * score_scale
        )
        scores = jnp.where(key_live[None, None, :], scores, masked_score)
        probability = jnp.exp(scores - log_block[:, :, None])
        grad_prob = jnp.einsum(
            "qhd,khd->hqk", grad_block, values_all, preferred_element_type=jnp.float32
        )
        grad_values = grad_values + jnp.einsum(
            "hqk,qhd->khd",
            probability.astype(jnp.bfloat16),
            grad_block,
            preferred_element_type=jnp.float32,
        )
        inner_sum = jnp.sum(grad_prob * probability, axis=-1, keepdims=True)
        grad_scores = (probability * (grad_prob - inner_sum)).astype(jnp.bfloat16)
        grad_query = (
            jnp.einsum("hqk,khd->qhd", grad_scores, keys_all, preferred_element_type=jnp.float32)
            * score_scale
        )
        grad_keys = (
            grad_keys
            + jnp.einsum(
                "hqk,qhd->khd", grad_scores, query_block, preferred_element_type=jnp.float32
            )
            * score_scale
        )
        return ((grad_keys, grad_values), grad_query)

    zero_keys = jnp.zeros((total_rows, local_heads, HD), jnp.float32)
    shaped = (
        queries.reshape(block_count, block_rows, local_heads, HD),
        grad_context.reshape(block_count, block_rows, local_heads, HD),
        log_total,
    )
    (grad_keys, grad_values), grad_queries = lax.scan(one_block, (zero_keys, zero_keys), shaped)
    return (grad_queries.reshape(total_rows, local_heads, HD), grad_keys, grad_values)


def layer_forward(hidden, weights, key_live):
    (
        w_qkv,
        b_qv,
        w_out,
        b_out,
        gain_attn,
        shift_attn,
        w_up,
        b_up,
        w_down,
        b_down,
        gain_ffn,
        shift_ffn,
    ) = weights
    local_rows = hidden.shape[0]
    groups = lax.axis_size("seq")
    local_heads = HEADS // groups
    bias_qv = b_qv.astype(jnp.float32)
    bias_full = jnp.concatenate([bias_qv[:D], jnp.zeros((D,), jnp.float32), bias_qv[D:]])
    hidden_low = hidden.astype(jnp.bfloat16)
    projected = (jnp.dot(hidden_low, w_qkv, preferred_element_type=jnp.float32) + bias_full).astype(
        jnp.bfloat16
    )
    by_head = lax.all_to_all(
        projected.reshape(local_rows, 3, groups, local_heads, HD),
        "seq",
        split_axis=2,
        concat_axis=0,
        tiled=True,
    )
    context, log_total = attend_forward(
        by_head[:, 0, 0], by_head[:, 1, 0], by_head[:, 2, 0], key_live
    )
    ctx_rows = lax.all_to_all(
        context.reshape(local_rows * groups, 1, local_heads, HD),
        "seq",
        split_axis=0,
        concat_axis=1,
        tiled=True,
    ).reshape(local_rows, D)
    attended = jnp.dot(ctx_rows, w_out, preferred_element_type=jnp.float32) + b_out.astype(
        jnp.float32
    )
    residual_one = hidden + attended
    normed = norm_rows(residual_one, gain_attn.astype(jnp.float32), shift_attn.astype(jnp.float32))
    pre_gelu = jnp.dot(
        normed.astype(jnp.bfloat16), w_up, preferred_element_type=jnp.float32
    ) + b_up.astype(jnp.float32)
    active = gelu_exact(pre_gelu).astype(jnp.bfloat16)
    branch_out = jnp.dot(active, w_down, preferred_element_type=jnp.float32) + b_down.astype(
        jnp.float32
    )
    residual_two = normed + branch_out
    output = norm_rows(residual_two, gain_ffn.astype(jnp.float32), shift_ffn.astype(jnp.float32))
    stored = (
        hidden,
        by_head,
        log_total,
        ctx_rows,
        residual_one,
        normed,
        pre_gelu,
        active,
        residual_two,
    )
    return (output, stored)


def layer_backward(grad_output, weights, stored, key_live):
    (
        w_qkv,
        b_qv,
        w_out,
        b_out,
        gain_attn,
        shift_attn,
        w_up,
        b_up,
        w_down,
        b_down,
        gain_ffn,
        shift_ffn,
    ) = weights
    hidden, by_head, log_total, ctx_rows, residual_one, normed, pre_gelu, active, residual_two = (
        stored
    )
    local_rows = hidden.shape[0]
    groups = lax.axis_size("seq")
    local_heads = HEADS // groups
    ffn_pull = jax.vjp(
        norm_rows, residual_two, gain_ffn.astype(jnp.float32), shift_ffn.astype(jnp.float32)
    )[1]
    grad_two, grad_gain_ffn, grad_shift_ffn = ffn_pull(grad_output)
    grad_branch = grad_two.astype(jnp.bfloat16)
    grad_b_down = jnp.sum(grad_branch.astype(jnp.float32), axis=0)
    grad_w_down = jnp.einsum("rf,rd->fd", active, grad_branch, preferred_element_type=jnp.float32)
    grad_active = jnp.einsum("rd,fd->rf", grad_branch, w_down, preferred_element_type=jnp.float32)
    gelu_pull = jax.vjp(gelu_exact, pre_gelu)[1]
    grad_pre = gelu_pull(grad_active)[0].astype(jnp.bfloat16)
    grad_b_up = jnp.sum(grad_pre.astype(jnp.float32), axis=0)
    normed_low = normed.astype(jnp.bfloat16)
    grad_w_up = jnp.einsum("rd,rf->df", normed_low, grad_pre, preferred_element_type=jnp.float32)
    grad_normed = (
        jnp.einsum("rf,df->rd", grad_pre, w_up, preferred_element_type=jnp.float32) + grad_two
    )
    attn_pull = jax.vjp(
        norm_rows, residual_one, gain_attn.astype(jnp.float32), shift_attn.astype(jnp.float32)
    )[1]
    grad_one, grad_gain_attn, grad_shift_attn = attn_pull(grad_normed)
    grad_attended = grad_one.astype(jnp.bfloat16)
    grad_b_out = jnp.sum(grad_attended.astype(jnp.float32), axis=0)
    grad_w_out = jnp.einsum(
        "rk,rd->kd", ctx_rows, grad_attended, preferred_element_type=jnp.float32
    )
    grad_ctx = jnp.einsum(
        "rd,kd->rk", grad_attended, w_out, preferred_element_type=jnp.float32
    ).astype(jnp.bfloat16)
    grad_heads = lax.all_to_all(
        grad_ctx.reshape(local_rows, groups, local_heads, HD),
        "seq",
        split_axis=1,
        concat_axis=0,
        tiled=True,
    )
    grad_queries, grad_keys, grad_values = attend_backward(
        by_head[:, 0, 0], by_head[:, 1, 0], by_head[:, 2, 0], grad_heads[:, 0], log_total, key_live
    )
    grad_stack = jnp.stack([grad_queries, grad_keys, grad_values], axis=1).astype(jnp.bfloat16)[
        :, :, None
    ]
    grad_projected = lax.all_to_all(
        grad_stack, "seq", split_axis=0, concat_axis=2, tiled=True
    ).reshape(local_rows, 3 * D)
    grad_sums = jnp.sum(grad_projected.astype(jnp.float32), axis=0)
    grad_b_qv = jnp.concatenate([grad_sums[:D], grad_sums[2 * D :]])
    hidden_low = hidden.astype(jnp.bfloat16)
    grad_w_qkv = jnp.einsum(
        "rd,re->de", hidden_low, grad_projected, preferred_element_type=jnp.float32
    )
    grad_hidden = (
        jnp.einsum("re,de->rd", grad_projected, w_qkv, preferred_element_type=jnp.float32)
        + grad_one
    )
    weight_grads = (
        grad_w_qkv,
        grad_b_qv,
        grad_w_out,
        grad_b_out,
        grad_gain_attn,
        grad_shift_attn,
        grad_w_up,
        grad_b_up,
        grad_w_down,
        grad_b_down,
        grad_gain_ffn,
        grad_shift_ffn,
    )
    return (grad_hidden, weight_grads)


def fsdp_layer_sum(weight_grads):
    (
        grad_w_qkv,
        grad_b_qv,
        grad_w_out,
        grad_b_out,
        grad_gain_attn,
        grad_shift_attn,
        grad_w_up,
        grad_b_up,
        grad_w_down,
        grad_b_down,
        grad_gain_ffn,
        grad_shift_ffn,
    ) = weight_grads
    return (
        lax.psum_scatter(grad_w_qkv.astype(jnp.bfloat16), "fsdp", scatter_dimension=0, tiled=True),
        lax.psum_scatter(grad_b_qv.astype(jnp.bfloat16), "fsdp", scatter_dimension=0, tiled=True),
        lax.psum_scatter(grad_w_out.astype(jnp.bfloat16), "fsdp", scatter_dimension=0, tiled=True),
        lax.psum_scatter(grad_b_out.astype(jnp.bfloat16), "fsdp", scatter_dimension=0, tiled=True),
        lax.psum_scatter(grad_gain_attn.astype(jnp.bfloat16), "fsdp", scatter_dimension=0, tiled=True),
        lax.psum_scatter(grad_shift_attn.astype(jnp.bfloat16), "fsdp", scatter_dimension=0, tiled=True),
        lax.psum_scatter(grad_w_up.astype(jnp.bfloat16), "fsdp", scatter_dimension=0, tiled=True),
        lax.psum_scatter(grad_b_up.astype(jnp.bfloat16), "fsdp", scatter_dimension=0, tiled=True),
        lax.psum_scatter(grad_w_down.astype(jnp.bfloat16), "fsdp", scatter_dimension=0, tiled=True),
        lax.psum_scatter(grad_b_down.astype(jnp.bfloat16), "fsdp", scatter_dimension=0, tiled=True),
        lax.psum_scatter(grad_gain_ffn.astype(jnp.bfloat16), "fsdp", scatter_dimension=0, tiled=True),
        lax.psum_scatter(grad_shift_ffn.astype(jnp.bfloat16), "fsdp", scatter_dimension=0, tiled=True),
    )


def seq_total_sum(shard_grads, grad_memory):
    (
        grad_w_qkv,
        grad_b_qv,
        grad_w_out,
        grad_b_out,
        grad_gain_attn,
        grad_shift_attn,
        grad_w_up,
        grad_b_up,
        grad_w_down,
        grad_b_down,
        grad_gain_ffn,
        grad_shift_ffn,
    ) = shard_grads
    pieces = (
        lax.psum_scatter(
            grad_w_qkv.astype(jnp.bfloat16), "seq", scatter_dimension=2, tiled=True
        ).astype(jnp.float32),
        lax.psum_scatter(
            grad_w_out.astype(jnp.bfloat16), "seq", scatter_dimension=2, tiled=True
        ).astype(jnp.float32),
        lax.psum_scatter(
            grad_w_up.astype(jnp.bfloat16), "seq", scatter_dimension=2, tiled=True
        ).astype(jnp.float32),
        lax.psum_scatter(
            grad_w_down.astype(jnp.bfloat16), "seq", scatter_dimension=2, tiled=True
        ).astype(jnp.float32),
    )
    matrices = (
        lax.all_gather(pieces[0].astype(jnp.bfloat16), "seq", axis=2, tiled=True).astype(
            jnp.float32
        ),
        lax.all_gather(pieces[1].astype(jnp.bfloat16), "seq", axis=2, tiled=True).astype(
            jnp.float32
        ),
        lax.all_gather(pieces[2].astype(jnp.bfloat16), "seq", axis=2, tiled=True).astype(
            jnp.float32
        ),
        lax.all_gather(pieces[3].astype(jnp.bfloat16), "seq", axis=2, tiled=True).astype(
            jnp.float32
        ),
    )
    smalls = (
        lax.psum(grad_b_qv.astype(jnp.bfloat16), "seq").astype(jnp.float32),
        lax.psum(grad_b_out.astype(jnp.bfloat16), "seq").astype(jnp.float32),
        lax.psum(grad_gain_attn.astype(jnp.bfloat16), "seq").astype(jnp.float32),
        lax.psum(grad_shift_attn.astype(jnp.bfloat16), "seq").astype(jnp.float32),
        lax.psum(grad_b_up.astype(jnp.bfloat16), "seq").astype(jnp.float32),
        lax.psum(grad_b_down.astype(jnp.bfloat16), "seq").astype(jnp.float32),
        lax.psum(grad_gain_ffn.astype(jnp.bfloat16), "seq").astype(jnp.float32),
        lax.psum(grad_shift_ffn.astype(jnp.bfloat16), "seq").astype(jnp.float32),
        lax.psum(grad_memory.astype(jnp.bfloat16), "seq").astype(jnp.float32),
    )
    weights_sum = (
        matrices[0],
        smalls[0],
        matrices[1],
        smalls[1],
        smalls[2],
        smalls[3],
        matrices[2],
        smalls[4],
        matrices[3],
        smalls[5],
        smalls[6],
        smalls[7],
    )
    return (weights_sum, smalls[8])


def body(
    tokens,
    memory,
    lengths,
    w_qkv,
    b_qv,
    w_out,
    b_out,
    gain_attn,
    shift_attn,
    w_up,
    b_up,
    w_down,
    b_down,
    gain_ffn,
    shift_ffn,
    cotangent,
):
    local_rows = tokens.shape[0]
    groups = lax.axis_size("seq")
    seq_place = lax.axis_index("seq")
    length = lengths[0]
    positions = seq_place * local_rows + jnp.arange(local_rows, dtype=jnp.int32)
    key_live = jnp.arange(local_rows * groups, dtype=jnp.int32) < length + 2 * MEM
    row_live = (positions < length + 2 * MEM)[:, None]
    token_live = ((positions >= MEM) & (positions < length + MEM))[:, None]
    memory_slots = jnp.arange(2 * MEM, dtype=jnp.int32)
    targets = jnp.where(memory_slots < MEM, memory_slots, length + memory_slots)
    select = positions[:, None] == targets[None, :]
    hidden = jnp.where(token_live, tokens.astype(jnp.float32), 0.0) + jnp.dot(
        select.astype(jnp.bfloat16), memory[0], preferred_element_type=jnp.float32
    )
    stacks = (
        w_qkv,
        b_qv,
        w_out,
        b_out,
        gain_attn,
        shift_attn,
        w_up,
        b_up,
        w_down,
        b_down,
        gain_ffn,
        shift_ffn,
    )
    kept = []
    for layer_index in range(LAYERS):
        weights = gather_layer(stacks, layer_index)
        hidden, stored = layer_forward(hidden, weights, key_live)
        kept.append((weights, stored))
    result = jnp.where(row_live, hidden, 0.0)
    grad_hidden = jnp.where(row_live, cotangent, 0.0)
    collected = []
    for layer_index in reversed(range(LAYERS)):
        weights, stored = kept[layer_index]
        grad_hidden, weight_grads = layer_backward(grad_hidden, weights, stored, key_live)
        collected.insert(0, fsdp_layer_sum(weight_grads))
    stacked_grads = tuple((jnp.stack(member) for member in zip(*collected)))
    grad_tokens = jnp.where(token_live, grad_hidden, 0.0)
    grad_memory = jnp.dot(
        select.astype(jnp.float32).T, grad_hidden, precision=lax.Precision.HIGHEST
    )[None]
    summed, memory_sum = seq_total_sum(stacked_grads, grad_memory)
    return (result, grad_tokens, memory_sum) + tuple(summed)


def solution(mesh):
    in_specs = (
        P(("fsdp", "seq"), None),
        P("fsdp", None, None),
        P("fsdp"),
        P(None, "fsdp", None),
        P(None, "fsdp"),
        P(None, "fsdp", None),
        P(None, "fsdp"),
        P(None, "fsdp"),
        P(None, "fsdp"),
        P(None, "fsdp", None),
        P(None, "fsdp"),
        P(None, "fsdp", None),
        P(None, "fsdp"),
        P(None, "fsdp"),
        P(None, "fsdp"),
        P(("fsdp", "seq"), None),
    )
    out_specs = (
        P(("fsdp", "seq"), None),
        P(("fsdp", "seq"), None),
        P("fsdp", None, None),
        P(None, "fsdp", None),
        P(None, "fsdp"),
        P(None, "fsdp", None),
        P(None, "fsdp"),
        P(None, "fsdp"),
        P(None, "fsdp"),
        P(None, "fsdp", None),
        P(None, "fsdp"),
        P(None, "fsdp", None),
        P(None, "fsdp"),
        P(None, "fsdp"),
        P(None, "fsdp"),
    )
    return jax.shard_map(body, mesh=mesh, in_specs=in_specs, out_specs=out_specs, check_vma=False)
```

```python
import functools
import math

import jax
import jax.numpy as jnp
from jax import lax
from jax.experimental import pallas as pl
from jax.experimental.pallas import tpu as pltpu
from jax.sharding import PartitionSpec as P

D = 768
HEADS = 12
HD = 64
FF = 3072
MEM = 10
LAYERS = 2
GROUP = 640
CTX = 256
MESH = pl.DeviceIdType.MESH

norm_eps = 1e-12
masked_score = -1e30


def dot(a, b):
    return jnp.dot(a, b, preferred_element_type=jnp.float32)


def dot_t(a, b):
    return lax.dot_general(a, b, (((1,), (1,)), ((), ())), preferred_element_type=jnp.float32)


def t_dot(a, b):
    return lax.dot_general(a, b, (((0,), (0,)), ((), ())), preferred_element_type=jnp.float32)


def standardize(values):
    row_mean = jnp.mean(values, axis=-1, keepdims=True)
    centred = values - row_mean
    variance = jnp.mean(centred * centred, axis=-1, keepdims=True)
    scale = lax.rsqrt(variance + norm_eps)
    return centred * scale, scale


B_OUT, GAIN_A, SHIFT_A, B_UP, B_DOWN, GAIN_F, SHIFT_F, VECS = 0, 1, 2, 3, 7, 8, 9, 10


def forward_kernel(
    n, g, *refs
):
    (
        x0_ref, mask_ref, bqkv_ref, vec_ref, sq_ref, so_ref, su_ref, sd_ref,
        y_ref, fq_ref, fo_ref, fu_ref, fd_ref, xb_out, heads_out, lse_out, ctx_out, r1_out, pre_out, act_out, r2_out,
        wq, wo, wu, wd, x_s, xb, heads, lse, ctx, r1, pre, act, r2, acc_s, nb_s, qkv_send, ctx_send,
        w_send, w_recv, c_send, c_recv, own_sem, q_send_sem, q_recv_sem, k_send_sem, k_recv_sem, save_sem,
    ) = refs
    f, s = lax.axis_index("fsdp"), lax.axis_index("seq")
    rows = x0_ref.shape[0]
    half = n // 2
    partner = f + 1 - 2 * lax.rem(f, 2)

    barrier = pltpu.get_barrier_semaphore()
    for j in range(1, n):
        pl.semaphore_signal(barrier, 1, device_id={"fsdp": lax.rem(f + j, n), "seq": s}, device_id_type=MESH)
    for j in range(1, g):
        pl.semaphore_signal(barrier, 1, device_id={"fsdp": f, "seq": lax.rem(s + j, g)}, device_id_type=MESH)
    pl.semaphore_wait(barrier, n - 1 + g - 1)

    lands = (wq, wo, wu, wd)
    shards = (sq_ref, so_ref, su_ref, sd_ref)
    fulls = (fq_ref, fo_ref, fu_ref, fd_ref)

    def place(m, owner):
        layer, kind = divmod(m, 4)
        depth = shards[kind].shape[1]
        return lands[kind].at[layer, pl.ds(pl.multiple_of(owner * depth, depth), depth)]

    def to_chip(m, j):
        layer, kind = divmod(m, 4)
        return pltpu.make_async_remote_copy(
            src_ref=shards[kind].at[layer], dst_ref=place(m, f), send_sem=w_send.at[m, j - 1], recv_sem=w_recv.at[m, j - 1],
            device_id={"fsdp": lax.rem(f + 2 * j, n), "seq": s}, device_id_type=MESH)

    def to_core(m, j):
        owner = lax.rem(f - 2 * j + n, n)
        return pltpu.make_async_remote_copy(
            src_ref=place(m, owner), dst_ref=place(m, owner), send_sem=c_send.at[m, j], recv_sem=c_recv.at[m, j],
            device_id={"fsdp": partner, "seq": s}, device_id_type=MESH)

    def own_copy(m):
        layer, kind = divmod(m, 4)
        return pltpu.make_async_copy(shards[kind].at[layer], place(m, f), own_sem.at[m])

    def save_full(m):
        layer, kind = divmod(m, 4)
        return pltpu.make_async_copy(lands[kind].at[layer], fulls[kind].at[layer], own_sem.at[m])

    for m in range(4 * LAYERS):
        own_copy(m).start()
        for j in range(1, half):
            to_chip(m, j).start()
    for m in range(4 * LAYERS):
        own_copy(m).wait()
        to_core(m, 0).start()

    def forward_on(m):
        for j in range(1, half):
            to_chip(m, j).wait_recv()
            to_core(m, j).start()

    def need(m):
        for j in range(half):
            to_core(m, j).wait_recv()
        save_full(m).start()

    saves = []

    def save(src, dst):
        copy = pltpu.make_async_copy(src, dst, save_sem.at[len(saves)])
        copy.start()
        saves.append(copy)

    lane = lax.broadcasted_iota(jnp.int32, (rows, 128), 1)
    x_s[...] = x0_ref[...]

    for layer in range(LAYERS):
        m0 = 4 * layer
        xb[layer] = x_s[...].astype(jnp.bfloat16)
        save(xb.at[layer], xb_out.at[layer])
        forward_on(m0)
        need(m0)

        def q_copy(i):
            return pltpu.make_async_remote_copy(
                src_ref=qkv_send.at[i - 1], dst_ref=heads.at[layer, pl.ds(pl.multiple_of(s * rows, rows), rows)],
                send_sem=q_send_sem.at[layer, i - 1], recv_sem=q_recv_sem.at[layer, i - 1],
                device_id={"fsdp": f, "seq": lax.rem(s + i, g)}, device_id_type=MESH)

        def q_arrival(i):
            return pltpu.make_async_remote_copy(
                src_ref=qkv_send.at[i - 1],
                dst_ref=heads.at[layer, pl.ds(pl.multiple_of(lax.rem(s - i + g, g) * rows, rows), rows)],
                send_sem=q_send_sem.at[layer, i - 1], recv_sem=q_recv_sem.at[layer, i - 1],
                device_id={"fsdp": f, "seq": lax.rem(s + i, g)}, device_id_type=MESH)

        if layer:
            for i in range(1, g):
                pltpu.make_async_remote_copy(
                    src_ref=qkv_send.at[i - 1], dst_ref=heads.at[layer - 1, pl.ds(pl.multiple_of(s * rows, rows), rows)],
                    send_sem=q_send_sem.at[layer - 1, i - 1], recv_sem=q_recv_sem.at[layer - 1, i - 1],
                    device_id={"fsdp": f, "seq": lax.rem(s + i, g)}, device_id_type=MESH).wait_send()

        for i in list(range(1, g)) + [0]:
            group = lax.rem(s + i, g)
            columns = pl.ds(pl.multiple_of(group * GROUP, 128), GROUP)
            projected = (dot(xb[layer], wq[layer, :, columns]) + bqkv_ref[layer, group]).astype(jnp.bfloat16)
            if i:
                qkv_send[i - 1] = projected
                q_copy(i).start()
            else:
                heads[layer, pl.ds(pl.multiple_of(s * rows, rows), rows), :] = projected
        forward_on(m0 + 1)
        for i in range(1, g):
            q_arrival(i).wait_recv()
        save(heads.at[layer], heads_out.at[layer])

        def c_copy(i, b):
            return pltpu.make_async_remote_copy(
                src_ref=ctx_send.at[layer, i], dst_ref=ctx.at[layer, s],
                send_sem=k_send_sem.at[layer, i], recv_sem=k_recv_sem.at[layer, i],
                device_id={"fsdp": f, "seq": b}, device_id_type=MESH)

        def attend(i, carry):
            b = lax.rem(s + i, g)
            block = pl.ds(pl.multiple_of(b * rows, rows), rows)
            q_a = heads[layer, block, 0:128] * jnp.bfloat16(HD**-0.5)
            q_d = heads[layer, block, 384:512] * jnp.bfloat16(HD**-0.5)
            zero = jnp.zeros_like(q_a)
            outs, logs = [], []
            for h in range(3):
                if h == 2:
                    scores = dot_t(q_d, heads[layer, :, 512:640])
                else:
                    part = jnp.where(lane < 64, q_a, zero) if h == 0 else jnp.where(lane < 64, zero, q_a)
                    scores = dot_t(part, heads[layer, :, 128:256])
                scores = scores + mask_ref[...]
                top = jnp.max(scores, axis=-1, keepdims=True)
                exponent = jnp.exp(scores - top)
                total = jnp.sum(exponent, axis=-1, keepdims=True)
                values = heads[layer, :, 384:512] if h == 2 else heads[layer, :, 256:384]
                outs.append(dot(exponent.astype(jnp.bfloat16), values) * (1.0 / total))
                logs.append(top + jnp.log(total))
            lse[layer, block, :] = jnp.where(lane == 0, logs[0], jnp.where(lane == 1, logs[1], logs[2]))
            first = jnp.where(lane < 64, outs[0], outs[1]).astype(jnp.bfloat16)
            second = jnp.where(lane < 64, 0.0, outs[2]).astype(jnp.bfloat16)

            @pl.when(i < g)
            def _():
                ctx_send[layer, i, :, 0:128] = first
                ctx_send[layer, i, :, 128:256] = second
                c_copy(i, b).start()

            @pl.when(i == g)
            def _():
                ctx[layer, s, :, 0:128] = first
                ctx[layer, s, :, 128:256] = second

            return carry

        lax.fori_loop(1, g + 1, attend, 0)
        save(lse.at[layer], lse_out.at[layer])
        need(m0 + 1)
        forward_on(m0 + 2)
        for i in range(1, g):
            pltpu.make_async_remote_copy(
                src_ref=ctx_send.at[layer, i], dst_ref=ctx.at[layer, lax.rem(s - i + g, g)],
                send_sem=k_send_sem.at[layer, i], recv_sem=k_recv_sem.at[layer, i],
                device_id={"fsdp": f, "seq": lax.rem(s + i, g)}, device_id_type=MESH).wait_recv()
        save(ctx.at[layer], ctx_out.at[layer])

        total = x_s[...] + vec_ref[layer, B_OUT]
        for grp in range(g):
            base = grp * 3 * HD
            total = total + dot(ctx[layer, grp, :, 0:128], wo[layer, base : base + 128, :])
            total = total + dot(ctx[layer, grp, :, 128:256], wo[layer, base + 64 : base + 192, :])
        r1[layer] = total
        save(r1.at[layer], r1_out.at[layer])
        normed = standardize(total)[0] * vec_ref[layer, GAIN_A] + vec_ref[layer, SHIFT_A]
        nb_s[...] = normed.astype(jnp.bfloat16)
        acc_s[...] = normed + vec_ref[layer, B_DOWN]
        need(m0 + 2)
        forward_on(m0 + 3)
        need(m0 + 3)

        def ffn(c, carry):
            columns = pl.ds(pl.multiple_of(c * D, 128), D)
            up = dot(nb_s[...], wu[layer, :, columns]) + vec_ref[layer, B_UP + c]
            pre[layer, :, columns] = up
            active = (up * (lax.erf(up * (0.5**0.5)) + 1.0) * 0.5).astype(jnp.bfloat16)
            act[layer, :, columns] = active
            acc_s[...] += dot(active, wd[layer, columns, :])
            return carry

        lax.fori_loop(0, FF // D, ffn, 0)
        save(pre.at[layer], pre_out.at[layer])
        save(act.at[layer], act_out.at[layer])
        r2[layer] = acc_s[...]
        save(r2.at[layer], r2_out.at[layer])
        x_s[...] = standardize(acc_s[...])[0] * vec_ref[layer, GAIN_F] + vec_ref[layer, SHIFT_F]
    y_ref[...] = x_s[...]

    for m in range(4 * LAYERS):
        for j in range(1, half):
            to_chip(m, j).wait_send()
        for j in range(half):
            to_core(m, j).wait_send()
        save_full(m).wait()
    for i in range(1, g):
        pltpu.make_async_remote_copy(
            src_ref=qkv_send.at[i - 1], dst_ref=heads.at[LAYERS - 1, pl.ds(pl.multiple_of(s * rows, rows), rows)],
            send_sem=q_send_sem.at[LAYERS - 1, i - 1], recv_sem=q_recv_sem.at[LAYERS - 1, i - 1],
            device_id={"fsdp": f, "seq": lax.rem(s + i, g)}, device_id_type=MESH).wait_send()
    for layer in range(LAYERS):
        for i in range(1, g):
            pltpu.make_async_remote_copy(
                src_ref=ctx_send.at[layer, i], dst_ref=ctx.at[layer, s],
                send_sem=k_send_sem.at[layer, i], recv_sem=k_recv_sem.at[layer, i],
                device_id={"fsdp": f, "seq": lax.rem(s + i, g)}, device_id_type=MESH).wait_send()
    for copy in saves:
        copy.wait()


def run_forward(n, g, x0, mask, bqkv, vecs, sq, so, su, sd):
    rows, span = x0.shape[0], x0.shape[0] * g
    any_spec = pl.BlockSpec(memory_space=pl.ANY)
    vmem = pl.BlockSpec(memory_space=pltpu.VMEM)
    bf, f32 = jnp.bfloat16, jnp.float32
    half = n // 2
    shapes = [
        ((rows, D), f32, vmem),
        ((LAYERS, D, g * GROUP), bf, any_spec),
        ((LAYERS, D, D), bf, any_spec),
        ((LAYERS, D, FF), bf, any_spec),
        ((LAYERS, FF, D), bf, any_spec),
        ((LAYERS, rows, D), bf, any_spec),
        ((LAYERS, span, GROUP), bf, any_spec),
        ((LAYERS, span, 128), f32, any_spec),
        ((LAYERS, g, rows, CTX), bf, any_spec),
        ((LAYERS, rows, D), f32, any_spec),
        ((LAYERS, rows, FF), f32, any_spec),
        ((LAYERS, rows, FF), bf, any_spec),
        ((LAYERS, rows, D), f32, any_spec),
    ]
    dma = pltpu.SemaphoreType.DMA
    return pl.pallas_call(
        functools.partial(forward_kernel, n, g),
        name="forward",
        out_shape=[jax.ShapeDtypeStruct(a, b) for a, b, _ in shapes],
        in_specs=[vmem] * 4 + [any_spec] * 4,
        out_specs=[c for _, _, c in shapes],
        scratch_shapes=[
            pltpu.VMEM((LAYERS, D, g * GROUP), bf),
            pltpu.VMEM((LAYERS, D, D), bf),
            pltpu.VMEM((LAYERS, D, FF), bf),
            pltpu.VMEM((LAYERS, FF, D), bf),
            pltpu.VMEM((rows, D), f32),
            pltpu.VMEM((LAYERS, rows, D), bf),
            pltpu.VMEM((LAYERS, span, GROUP), bf),
            pltpu.VMEM((LAYERS, span, 128), f32),
            pltpu.VMEM((LAYERS, g, rows, CTX), bf),
            pltpu.VMEM((LAYERS, rows, D), f32),
            pltpu.VMEM((LAYERS, rows, FF), f32),
            pltpu.VMEM((LAYERS, rows, FF), bf),
            pltpu.VMEM((LAYERS, rows, D), f32),
            pltpu.VMEM((rows, D), f32),
            pltpu.VMEM((rows, D), bf),
            pltpu.VMEM((g - 1, rows, GROUP), bf),
            pltpu.VMEM((LAYERS, g, rows, CTX), bf),
            dma((4 * LAYERS, half - 1)),
            dma((4 * LAYERS, half - 1)),
            dma((4 * LAYERS, half)),
            dma((4 * LAYERS, half)),
            dma((4 * LAYERS,)),
            dma((LAYERS, g - 1)),
            dma((LAYERS, g - 1)),
            dma((LAYERS, g)),
            dma((LAYERS, g)),
            dma((8 * LAYERS,)),
        ],
        compiler_params=pltpu.CompilerParams(
            collective_id=0, has_side_effects=True, vmem_limit_bytes=62 * 1024 * 1024
        ),
    )(x0, mask, bqkv, vecs, sq, so, su, sd)


def group_columns(w, g):
    lead = w.shape[:-1]
    q, k, v = (w[..., i * D : (i + 1) * D].reshape(lead + (g, 3 * HD)) for i in range(3))
    return jnp.concatenate(
        [q[..., :128], k[..., :128], v[..., :128], q[..., 128:], v[..., 128:], k[..., 128:], jnp.zeros_like(k[..., 128:])], axis=-1)


def ungroup_columns(w):
    lead, g = w.shape[:-2], w.shape[-2]
    q = jnp.concatenate([w[..., 0:128], w[..., 384:448]], axis=-1).reshape(lead + (D,))
    k = jnp.concatenate([w[..., 128:256], w[..., 512:576]], axis=-1).reshape(lead + (D,))
    v = jnp.concatenate([w[..., 256:384], w[..., 448:512]], axis=-1).reshape(lead + (D,))
    return jnp.concatenate([q, k, v], axis=-1)


def gather_vectors(n, g, b_qv, b_out, gain_attn, shift_attn, b_up, b_down, gain_ffn, shift_ffn):
    width = D // n
    packed = jnp.concatenate(
        [b_qv.reshape(LAYERS, 2, width), b_out[:, None], gain_attn[:, None], shift_attn[:, None],
         b_up.reshape(LAYERS, FF // D, width), b_down[:, None], gain_ffn[:, None], shift_ffn[:, None]], axis=1)
    whole = lax.all_gather(packed, "fsdp", axis=0).astype(jnp.float32)
    b = whole[:, :, 0:2].transpose(1, 0, 2, 3).reshape(LAYERS, 2 * D)
    up = whole[:, :, 5:9].transpose(1, 0, 2, 3).reshape(LAYERS, FF // D, D)
    rest = whole.transpose(1, 2, 0, 3).reshape(LAYERS, 12, D)
    vecs = jnp.concatenate([rest[:, 2:5], up, rest[:, 9:12]], axis=1)[:, :, None]
    full = jnp.concatenate([b[:, :D], jnp.zeros_like(b[:, :D]), b[:, D:]], axis=-1)
    return group_columns(full, g)[:, :, None], vecs


def norm_rows(values, gain_vec, shift_vec):
    row_mean = jnp.mean(values, axis=-1, keepdims=True)
    centred = values - row_mean
    variance = jnp.mean(centred * centred, axis=-1, keepdims=True)
    return centred * lax.rsqrt(variance + norm_eps) * gain_vec + shift_vec


def gelu_exact(values):
    return jax.nn.gelu(values, approximate=False)


def gather_layer(stacks, layer_index):
    (
        w_qkv,
        b_qv,
        w_out,
        b_out,
        gain_attn,
        shift_attn,
        w_up,
        b_up,
        w_down,
        b_down,
        gain_ffn,
        shift_ffn,
    ) = tuple((stacked[layer_index] for stacked in stacks))
    return (
        lax.all_gather(w_qkv, "fsdp", axis=0, tiled=True),
        lax.all_gather(b_qv, "fsdp", axis=0, tiled=True),
        lax.all_gather(w_out, "fsdp", axis=0, tiled=True),
        lax.all_gather(b_out, "fsdp", axis=0, tiled=True),
        lax.all_gather(gain_attn, "fsdp", axis=0, tiled=True),
        lax.all_gather(shift_attn, "fsdp", axis=0, tiled=True),
        lax.all_gather(w_up, "fsdp", axis=0, tiled=True),
        lax.all_gather(b_up, "fsdp", axis=0, tiled=True),
        lax.all_gather(w_down, "fsdp", axis=0, tiled=True),
        lax.all_gather(b_down, "fsdp", axis=0, tiled=True),
        lax.all_gather(gain_ffn, "fsdp", axis=0, tiled=True),
        lax.all_gather(shift_ffn, "fsdp", axis=0, tiled=True),
    )


def attend_forward(queries, keys_all, values_all, key_live):
    total_rows, local_heads = (queries.shape[0], queries.shape[1])
    block_rows = math.gcd(total_rows, 512)
    block_count = total_rows // block_rows
    score_scale = HD ** (-0.5)

    def one_block(query_block):
        scores = (
            jnp.einsum("qhd,khd->hqk", query_block, keys_all, preferred_element_type=jnp.float32)
            * score_scale
        )
        scores = jnp.where(key_live[None, None, :], scores, masked_score)
        top_score = jnp.max(scores, axis=-1, keepdims=True)
        exponent = jnp.exp(scores - top_score)
        row_total = jnp.sum(exponent, axis=-1, keepdims=True)
        probability = (exponent / row_total).astype(jnp.bfloat16)
        context = jnp.einsum(
            "hqk,khd->qhd", probability, values_all, preferred_element_type=jnp.float32
        )
        return (context.astype(jnp.bfloat16), (top_score + jnp.log(row_total))[..., 0])

    blocks = queries.reshape(block_count, block_rows, local_heads, HD)
    context, log_total = lax.map(one_block, blocks)
    return (context.reshape(total_rows, local_heads, HD), log_total)


def attend_backward(queries, keys_all, values_all, grad_context, log_total, key_live):
    total_rows, local_heads = (queries.shape[0], queries.shape[1])
    block_rows = math.gcd(total_rows, 512)
    block_count = total_rows // block_rows
    score_scale = HD ** (-0.5)

    def one_block(running, inputs):
        grad_keys, grad_values = running
        query_block, grad_block, log_block = inputs
        scores = (
            jnp.einsum("qhd,khd->hqk", query_block, keys_all, preferred_element_type=jnp.float32)
            * score_scale
        )
        scores = jnp.where(key_live[None, None, :], scores, masked_score)
        probability = jnp.exp(scores - log_block[:, :, None])
        grad_prob = jnp.einsum(
            "qhd,khd->hqk", grad_block, values_all, preferred_element_type=jnp.float32
        )
        grad_values = grad_values + jnp.einsum(
            "hqk,qhd->khd",
            probability.astype(jnp.bfloat16),
            grad_block,
            preferred_element_type=jnp.float32,
        )
        inner_sum = jnp.sum(grad_prob * probability, axis=-1, keepdims=True)
        grad_scores = (probability * (grad_prob - inner_sum)).astype(jnp.bfloat16)
        grad_query = (
            jnp.einsum("hqk,khd->qhd", grad_scores, keys_all, preferred_element_type=jnp.float32)
            * score_scale
        )
        grad_keys = (
            grad_keys
            + jnp.einsum(
                "hqk,qhd->khd", grad_scores, query_block, preferred_element_type=jnp.float32
            )
            * score_scale
        )
        return ((grad_keys, grad_values), grad_query)

    zero_keys = jnp.zeros((total_rows, local_heads, HD), jnp.float32)
    shaped = (
        queries.reshape(block_count, block_rows, local_heads, HD),
        grad_context.reshape(block_count, block_rows, local_heads, HD),
        log_total,
    )
    (grad_keys, grad_values), grad_queries = lax.scan(one_block, (zero_keys, zero_keys), shaped)
    return (grad_queries.reshape(total_rows, local_heads, HD), grad_keys, grad_values)


def layer_forward(hidden, weights, key_live):
    (
        w_qkv,
        b_qv,
        w_out,
        b_out,
        gain_attn,
        shift_attn,
        w_up,
        b_up,
        w_down,
        b_down,
        gain_ffn,
        shift_ffn,
    ) = weights
    local_rows = hidden.shape[0]
    groups = lax.axis_size("seq")
    local_heads = HEADS // groups
    bias_qv = b_qv.astype(jnp.float32)
    bias_full = jnp.concatenate([bias_qv[:D], jnp.zeros((D,), jnp.float32), bias_qv[D:]])
    hidden_low = hidden.astype(jnp.bfloat16)
    projected = (jnp.dot(hidden_low, w_qkv, preferred_element_type=jnp.float32) + bias_full).astype(
        jnp.bfloat16
    )
    by_head = lax.all_to_all(
        projected.reshape(local_rows, 3, groups, local_heads, HD),
        "seq",
        split_axis=2,
        concat_axis=0,
        tiled=True,
    )
    context, log_total = attend_forward(
        by_head[:, 0, 0], by_head[:, 1, 0], by_head[:, 2, 0], key_live
    )
    ctx_rows = lax.all_to_all(
        context.reshape(local_rows * groups, 1, local_heads, HD),
        "seq",
        split_axis=0,
        concat_axis=1,
        tiled=True,
    ).reshape(local_rows, D)
    attended = jnp.dot(ctx_rows, w_out, preferred_element_type=jnp.float32) + b_out.astype(
        jnp.float32
    )
    residual_one = hidden + attended
    normed = norm_rows(residual_one, gain_attn.astype(jnp.float32), shift_attn.astype(jnp.float32))
    pre_gelu = jnp.dot(
        normed.astype(jnp.bfloat16), w_up, preferred_element_type=jnp.float32
    ) + b_up.astype(jnp.float32)
    active = gelu_exact(pre_gelu).astype(jnp.bfloat16)
    branch_out = jnp.dot(active, w_down, preferred_element_type=jnp.float32) + b_down.astype(
        jnp.float32
    )
    residual_two = normed + branch_out
    output = norm_rows(residual_two, gain_ffn.astype(jnp.float32), shift_ffn.astype(jnp.float32))
    stored = (
        hidden,
        by_head,
        log_total,
        ctx_rows,
        residual_one,
        normed,
        pre_gelu,
        active,
        residual_two,
    )
    return (output, stored)


def layer_backward(grad_output, weights, stored, key_live):
    (
        w_qkv,
        b_qv,
        w_out,
        b_out,
        gain_attn,
        shift_attn,
        w_up,
        b_up,
        w_down,
        b_down,
        gain_ffn,
        shift_ffn,
    ) = weights
    hidden, by_head, log_total, ctx_rows, residual_one, normed, pre_gelu, active, residual_two = (
        stored
    )
    local_rows = hidden.shape[0]
    groups = lax.axis_size("seq")
    local_heads = HEADS // groups
    ffn_pull = jax.vjp(
        norm_rows, residual_two, gain_ffn.astype(jnp.float32), shift_ffn.astype(jnp.float32)
    )[1]
    grad_two, grad_gain_ffn, grad_shift_ffn = ffn_pull(grad_output)
    grad_branch = grad_two.astype(jnp.bfloat16)
    grad_b_down = jnp.sum(grad_branch.astype(jnp.float32), axis=0)
    grad_w_down = jnp.einsum("rf,rd->fd", active, grad_branch, preferred_element_type=jnp.float32)
    grad_active = jnp.einsum("rd,fd->rf", grad_branch, w_down, preferred_element_type=jnp.float32)
    gelu_pull = jax.vjp(gelu_exact, pre_gelu)[1]
    grad_pre = gelu_pull(grad_active)[0].astype(jnp.bfloat16)
    grad_b_up = jnp.sum(grad_pre.astype(jnp.float32), axis=0)
    normed_low = normed.astype(jnp.bfloat16)
    grad_w_up = jnp.einsum("rd,rf->df", normed_low, grad_pre, preferred_element_type=jnp.float32)
    grad_normed = (
        jnp.einsum("rf,df->rd", grad_pre, w_up, preferred_element_type=jnp.float32) + grad_two
    )
    attn_pull = jax.vjp(
        norm_rows, residual_one, gain_attn.astype(jnp.float32), shift_attn.astype(jnp.float32)
    )[1]
    grad_one, grad_gain_attn, grad_shift_attn = attn_pull(grad_normed)
    grad_attended = grad_one.astype(jnp.bfloat16)
    grad_b_out = jnp.sum(grad_attended.astype(jnp.float32), axis=0)
    grad_w_out = jnp.einsum(
        "rk,rd->kd", ctx_rows, grad_attended, preferred_element_type=jnp.float32
    )
    grad_ctx = jnp.einsum(
        "rd,kd->rk", grad_attended, w_out, preferred_element_type=jnp.float32
    ).astype(jnp.bfloat16)
    grad_heads = lax.all_to_all(
        grad_ctx.reshape(local_rows, groups, local_heads, HD),
        "seq",
        split_axis=1,
        concat_axis=0,
        tiled=True,
    )
    grad_queries, grad_keys, grad_values = attend_backward(
        by_head[:, 0, 0], by_head[:, 1, 0], by_head[:, 2, 0], grad_heads[:, 0], log_total, key_live
    )
    grad_stack = jnp.stack([grad_queries, grad_keys, grad_values], axis=1).astype(jnp.bfloat16)[
        :, :, None
    ]
    grad_projected = lax.all_to_all(
        grad_stack, "seq", split_axis=0, concat_axis=2, tiled=True
    ).reshape(local_rows, 3 * D)
    grad_sums = jnp.sum(grad_projected.astype(jnp.float32), axis=0)
    grad_b_qv = jnp.concatenate([grad_sums[:D], grad_sums[2 * D :]])
    hidden_low = hidden.astype(jnp.bfloat16)
    grad_w_qkv = jnp.einsum(
        "rd,re->de", hidden_low, grad_projected, preferred_element_type=jnp.float32
    )
    grad_hidden = (
        jnp.einsum("re,de->rd", grad_projected, w_qkv, preferred_element_type=jnp.float32)
        + grad_one
    )
    weight_grads = (
        grad_w_qkv,
        grad_b_qv,
        grad_w_out,
        grad_b_out,
        grad_gain_attn,
        grad_shift_attn,
        grad_w_up,
        grad_b_up,
        grad_w_down,
        grad_b_down,
        grad_gain_ffn,
        grad_shift_ffn,
    )
    return (grad_hidden, weight_grads)


def fsdp_layer_sum(weight_grads):
    (
        grad_w_qkv,
        grad_b_qv,
        grad_w_out,
        grad_b_out,
        grad_gain_attn,
        grad_shift_attn,
        grad_w_up,
        grad_b_up,
        grad_w_down,
        grad_b_down,
        grad_gain_ffn,
        grad_shift_ffn,
    ) = weight_grads
    return (
        lax.psum_scatter(grad_w_qkv.astype(jnp.bfloat16), "fsdp", scatter_dimension=0, tiled=True),
        lax.psum_scatter(grad_b_qv.astype(jnp.bfloat16), "fsdp", scatter_dimension=0, tiled=True),
        lax.psum_scatter(grad_w_out.astype(jnp.bfloat16), "fsdp", scatter_dimension=0, tiled=True),
        lax.psum_scatter(grad_b_out.astype(jnp.bfloat16), "fsdp", scatter_dimension=0, tiled=True),
        lax.psum_scatter(grad_gain_attn.astype(jnp.bfloat16), "fsdp", scatter_dimension=0, tiled=True),
        lax.psum_scatter(grad_shift_attn.astype(jnp.bfloat16), "fsdp", scatter_dimension=0, tiled=True),
        lax.psum_scatter(grad_w_up.astype(jnp.bfloat16), "fsdp", scatter_dimension=0, tiled=True),
        lax.psum_scatter(grad_b_up.astype(jnp.bfloat16), "fsdp", scatter_dimension=0, tiled=True),
        lax.psum_scatter(grad_w_down.astype(jnp.bfloat16), "fsdp", scatter_dimension=0, tiled=True),
        lax.psum_scatter(grad_b_down.astype(jnp.bfloat16), "fsdp", scatter_dimension=0, tiled=True),
        lax.psum_scatter(grad_gain_ffn.astype(jnp.bfloat16), "fsdp", scatter_dimension=0, tiled=True),
        lax.psum_scatter(grad_shift_ffn.astype(jnp.bfloat16), "fsdp", scatter_dimension=0, tiled=True),
    )


def seq_total_sum(shard_grads, grad_memory):
    (
        grad_w_qkv,
        grad_b_qv,
        grad_w_out,
        grad_b_out,
        grad_gain_attn,
        grad_shift_attn,
        grad_w_up,
        grad_b_up,
        grad_w_down,
        grad_b_down,
        grad_gain_ffn,
        grad_shift_ffn,
    ) = shard_grads
    pieces = (
        lax.psum_scatter(
            grad_w_qkv.astype(jnp.bfloat16), "seq", scatter_dimension=2, tiled=True
        ).astype(jnp.float32),
        lax.psum_scatter(
            grad_w_out.astype(jnp.bfloat16), "seq", scatter_dimension=2, tiled=True
        ).astype(jnp.float32),
        lax.psum_scatter(
            grad_w_up.astype(jnp.bfloat16), "seq", scatter_dimension=2, tiled=True
        ).astype(jnp.float32),
        lax.psum_scatter(
            grad_w_down.astype(jnp.bfloat16), "seq", scatter_dimension=2, tiled=True
        ).astype(jnp.float32),
    )
    matrices = (
        lax.all_gather(pieces[0].astype(jnp.bfloat16), "seq", axis=2, tiled=True).astype(
            jnp.float32
        ),
        lax.all_gather(pieces[1].astype(jnp.bfloat16), "seq", axis=2, tiled=True).astype(
            jnp.float32
        ),
        lax.all_gather(pieces[2].astype(jnp.bfloat16), "seq", axis=2, tiled=True).astype(
            jnp.float32
        ),
        lax.all_gather(pieces[3].astype(jnp.bfloat16), "seq", axis=2, tiled=True).astype(
            jnp.float32
        ),
    )
    smalls = (
        lax.psum(grad_b_qv.astype(jnp.bfloat16), "seq").astype(jnp.float32),
        lax.psum(grad_b_out.astype(jnp.bfloat16), "seq").astype(jnp.float32),
        lax.psum(grad_gain_attn.astype(jnp.bfloat16), "seq").astype(jnp.float32),
        lax.psum(grad_shift_attn.astype(jnp.bfloat16), "seq").astype(jnp.float32),
        lax.psum(grad_b_up.astype(jnp.bfloat16), "seq").astype(jnp.float32),
        lax.psum(grad_b_down.astype(jnp.bfloat16), "seq").astype(jnp.float32),
        lax.psum(grad_gain_ffn.astype(jnp.bfloat16), "seq").astype(jnp.float32),
        lax.psum(grad_shift_ffn.astype(jnp.bfloat16), "seq").astype(jnp.float32),
        lax.psum(grad_memory.astype(jnp.bfloat16), "seq").astype(jnp.float32),
    )
    weights_sum = (
        matrices[0],
        smalls[0],
        matrices[1],
        smalls[1],
        smalls[2],
        smalls[3],
        matrices[2],
        smalls[4],
        matrices[3],
        smalls[5],
        smalls[6],
        smalls[7],
    )
    return (weights_sum, smalls[8])


def plain_body(
    tokens,
    memory,
    lengths,
    w_qkv,
    b_qv,
    w_out,
    b_out,
    gain_attn,
    shift_attn,
    w_up,
    b_up,
    w_down,
    b_down,
    gain_ffn,
    shift_ffn,
    cotangent,
):
    local_rows = tokens.shape[0]
    groups = lax.axis_size("seq")
    seq_place = lax.axis_index("seq")
    length = lengths[0]
    positions = seq_place * local_rows + jnp.arange(local_rows, dtype=jnp.int32)
    key_live = jnp.arange(local_rows * groups, dtype=jnp.int32) < length + 2 * MEM
    row_live = (positions < length + 2 * MEM)[:, None]
    token_live = ((positions >= MEM) & (positions < length + MEM))[:, None]
    memory_slots = jnp.arange(2 * MEM, dtype=jnp.int32)
    targets = jnp.where(memory_slots < MEM, memory_slots, length + memory_slots)
    select = positions[:, None] == targets[None, :]
    hidden = jnp.where(token_live, tokens.astype(jnp.float32), 0.0) + jnp.dot(
        select.astype(jnp.bfloat16), memory[0], preferred_element_type=jnp.float32
    )
    stacks = (
        w_qkv,
        b_qv,
        w_out,
        b_out,
        gain_attn,
        shift_attn,
        w_up,
        b_up,
        w_down,
        b_down,
        gain_ffn,
        shift_ffn,
    )
    kept = []
    for layer_index in range(LAYERS):
        weights = gather_layer(stacks, layer_index)
        hidden, stored = layer_forward(hidden, weights, key_live)
        kept.append((weights, stored))
    result = jnp.where(row_live, hidden, 0.0)
    grad_hidden = jnp.where(row_live, cotangent, 0.0)
    collected = []
    for layer_index in reversed(range(LAYERS)):
        weights, stored = kept[layer_index]
        grad_hidden, weight_grads = layer_backward(grad_hidden, weights, stored, key_live)
        collected.insert(0, fsdp_layer_sum(weight_grads))
    stacked_grads = tuple((jnp.stack(member) for member in zip(*collected)))
    grad_tokens = jnp.where(token_live, grad_hidden, 0.0)
    grad_memory = jnp.dot(
        select.astype(jnp.float32).T, grad_hidden, precision=lax.Precision.HIGHEST
    )[None]
    summed, memory_sum = seq_total_sum(stacked_grads, grad_memory)
    return (result, grad_tokens, memory_sum) + tuple(summed)


def kernel_backward(grad_output, weights, vecs, stored, key_live):
    wq, wo, wu, wd = weights
    xb, heads, lse, ctx, r1, pre, act, r2 = stored
    g = ctx.shape[0]
    rows = xb.shape[0]
    gain_ffn, gain_attn, shift_attn = vecs[GAIN_F], vecs[GAIN_A], vecs[SHIFT_A]

    def norm_backward(grad, residual, gain):
        standard, scale = standardize(residual)
        inner = grad * gain
        back = scale * (inner - jnp.mean(inner, -1, keepdims=True) - standard * jnp.mean(inner * standard, -1, keepdims=True))
        return back, jnp.sum(grad * standard, 0), jnp.sum(grad, 0), standard

    grad_two, grad_gain_ffn, grad_shift_ffn, _ = norm_backward(grad_output, r2, gain_ffn)
    branch = grad_two.astype(jnp.bfloat16)
    grad_b_down = jnp.sum(branch.astype(jnp.float32), 0)
    grad_w_down = t_dot(act, branch)
    grad_active = dot_t(branch, wd)
    slope = 0.5 * (lax.erf(pre * 0.5**0.5) + 1.0) + pre * jnp.exp(-0.5 * pre * pre) * (0.5 / math.pi) ** 0.5
    grad_pre = (grad_active * slope).astype(jnp.bfloat16)
    grad_b_up = jnp.sum(grad_pre.astype(jnp.float32), 0)
    standard = standardize(r1)[0]
    normed_low = (standard * gain_attn + shift_attn).astype(jnp.bfloat16)
    grad_w_up = t_dot(normed_low, grad_pre)
    grad_normed = dot_t(grad_pre, wu) + grad_two
    grad_one, grad_gain_attn, grad_shift_attn, _ = norm_backward(grad_normed, r1, gain_attn)
    attended = grad_one.astype(jnp.bfloat16)
    grad_b_out = jnp.sum(attended.astype(jnp.float32), 0)
    ctx_rows = jnp.concatenate([ctx[..., :128], ctx[..., 192:]], -1).transpose(1, 0, 2).reshape(rows, D)
    grad_w_out = t_dot(ctx_rows, attended)
    grad_ctx = dot_t(attended, wo).astype(jnp.bfloat16).reshape(rows, g, 3, HD)
    grad_heads = lax.all_to_all(grad_ctx, "seq", split_axis=1, concat_axis=0, tiled=True)[:, 0]
    q = jnp.concatenate([heads[:, 0:128], heads[:, 384:448]], -1).reshape(-1, 3, HD)
    k = jnp.concatenate([heads[:, 128:256], heads[:, 512:576]], -1).reshape(-1, 3, HD)
    v = jnp.concatenate([heads[:, 256:384], heads[:, 448:512]], -1).reshape(-1, 3, HD)
    log_total = jnp.moveaxis(lse[:, :3].reshape(2, -1, 3), 2, 1)
    gq, gk, gv = attend_backward(q, k, v, grad_heads, log_total, key_live)
    stack = jnp.stack([gq, gk, gv], 1).astype(jnp.bfloat16)[:, :, None]
    projected = lax.all_to_all(stack, "seq", split_axis=0, concat_axis=2, tiled=True).reshape(rows, 3 * D)
    sums = jnp.sum(projected.astype(jnp.float32), 0)
    grad_b_qv = jnp.concatenate([sums[:D], sums[2 * D :]])
    grad_w_qkv = t_dot(xb, projected)
    w_full = ungroup_columns(wq.reshape(D, g, GROUP))
    grad_hidden = dot_t(projected, w_full) + grad_one
    return grad_hidden, (grad_w_qkv, grad_b_qv, grad_w_out, grad_b_out, grad_gain_attn, grad_shift_attn, grad_w_up, grad_b_up,
                         grad_w_down, grad_b_down, grad_gain_ffn, grad_shift_ffn)


def kernel_body(
    tokens, memory, lengths, w_qkv, b_qv, w_out, b_out, gain_attn, shift_attn, w_up, b_up, w_down, b_down, gain_ffn, shift_ffn, cotangent,
):
    local_rows = tokens.shape[0]
    n, g = lax.axis_size("fsdp"), lax.axis_size("seq")
    positions = lax.axis_index("seq") * local_rows + jnp.arange(local_rows, dtype=jnp.int32)
    length = lengths[0]
    key_live = jnp.arange(local_rows * g, dtype=jnp.int32) < length + 2 * MEM
    row_live = (positions < length + 2 * MEM)[:, None]
    token_live = ((positions >= MEM) & (positions < length + MEM))[:, None]
    memory_slots = jnp.arange(2 * MEM, dtype=jnp.int32)
    targets = jnp.where(memory_slots < MEM, memory_slots, length + memory_slots)
    select = positions[:, None] == targets[None, :]
    x0 = jnp.where(token_live, tokens.astype(jnp.float32), 0.0) + dot(select.astype(jnp.bfloat16), memory[0])
    mask = jnp.where(key_live, 0.0, masked_score)[None].astype(jnp.float32)
    bqkv, vecs = gather_vectors(n, g, b_qv, b_out, gain_attn, shift_attn, b_up, b_down, gain_ffn, shift_ffn)
    sq = group_columns(w_qkv, g).reshape(LAYERS, w_qkv.shape[1], g * GROUP)
    y, fq, fo, fu, fd, *stored = run_forward(n, g, x0, mask, bqkv, vecs, sq, w_out, w_up, w_down)
    result = jnp.where(row_live, y, 0.0)
    grad_hidden = jnp.where(row_live, cotangent, 0.0)
    collected = []
    for layer in reversed(range(LAYERS)):
        grad_hidden, grads = kernel_backward(
            grad_hidden, (fq[layer], fo[layer], fu[layer], fd[layer]), vecs[layer, :, 0], [item[layer] for item in stored], key_live)
        collected.insert(0, fsdp_layer_sum(grads))
    stacked = tuple(jnp.stack(member) for member in zip(*collected))
    grad_tokens = jnp.where(token_live, grad_hidden, 0.0)
    grad_memory = jnp.dot(select.astype(jnp.float32).T, grad_hidden, precision=lax.Precision.HIGHEST)[None]
    summed, memory_sum = seq_total_sum(stacked, grad_memory)
    return (result, grad_tokens, memory_sum) + tuple(summed)


def pick_body(mesh):
    n, g = mesh.shape["fsdp"], mesh.shape["seq"]
    fits = n % 2 == 0 and (D // n) % 32 == 0 and HEADS == 3 * g
    return kernel_body if fits else plain_body


def solution(mesh):
    in_specs = (
        P(("fsdp", "seq"), None),
        P("fsdp", None, None),
        P("fsdp"),
        P(None, "fsdp", None),
        P(None, "fsdp"),
        P(None, "fsdp", None),
        P(None, "fsdp"),
        P(None, "fsdp"),
        P(None, "fsdp"),
        P(None, "fsdp", None),
        P(None, "fsdp"),
        P(None, "fsdp", None),
        P(None, "fsdp"),
        P(None, "fsdp"),
        P(None, "fsdp"),
        P(("fsdp", "seq"), None),
    )
    out_specs = (
        P(("fsdp", "seq"), None),
        P(("fsdp", "seq"), None),
        P("fsdp", None, None),
        P(None, "fsdp", None),
        P(None, "fsdp"),
        P(None, "fsdp", None),
        P(None, "fsdp"),
        P(None, "fsdp"),
        P(None, "fsdp"),
        P(None, "fsdp", None),
        P(None, "fsdp"),
        P(None, "fsdp", None),
        P(None, "fsdp"),
        P(None, "fsdp"),
        P(None, "fsdp"),
    )
    return jax.shard_map(pick_body(mesh), mesh=mesh, in_specs=in_specs, out_specs=out_specs, check_vma=False)
```

```python
import functools
import math

import jax
import jax.numpy as jnp
from jax import lax
from jax.experimental import pallas as pl
from jax.experimental.pallas import tpu as pltpu
from jax.sharding import PartitionSpec as P

D = 768
HEADS = 12
HD = 64
FF = 3072
MEM = 10
LAYERS = 2
GROUP = 640
CTX = 256
MEM_ROWS = 32
SMALL = 16
MESH = pl.DeviceIdType.MESH

norm_eps = 1e-12
masked_score = -1e30

B_OUT, GAIN_A, SHIFT_A, B_UP, B_DOWN, GAIN_F, SHIFT_F, VECS = 0, 1, 2, 3, 7, 8, 9, 10
WIDE = (B_OUT, GAIN_A, SHIFT_A, B_DOWN, GAIN_F, SHIFT_F)


def dot(a, b):
    return jnp.dot(a, b, preferred_element_type=jnp.float32)


def dot_t(a, b):
    return lax.dot_general(a, b, (((1,), (1,)), ((), ())), preferred_element_type=jnp.float32)


def t_dot(a, b):
    return lax.dot_general(a, b, (((0,), (0,)), ((), ())), preferred_element_type=jnp.float32)


def standardize(values):
    row_mean = jnp.mean(values, axis=-1, keepdims=True)
    centred = values - row_mean
    variance = jnp.mean(centred * centred, axis=-1, keepdims=True)
    scale = lax.rsqrt(variance + norm_eps)
    return centred * scale, scale


class Place:
    def __init__(self, n, g):
        self.n, self.g = n, g
        self.f, self.s = f, s = lax.axis_index("fsdp"), lax.axis_index("seq")
        self.core = lax.rem(f, 2)
        chip = f // 2
        self.partner = f + 1 - 2 * self.core
        self.fx = f + 2 - 4 * lax.rem(chip, 2)
        self.fy = lax.rem(f + n // 2, n)
        self.fd = lax.rem(self.fx + n // 2, n)
        self.me = 2 * lax.rem(s, 2) + self.core
        away_f, away_s = f - self.core + lax.rem(s, 2), 2 * self.core + s // 2
        self.away = self.at(away_f, away_s)
        self.back = self.at(f - self.core + s // 2, 2 * lax.rem(s, 2) + self.core)
        self.away_home = self.back
        self.stays = jnp.logical_and(away_f == f, away_s == s)

    def at(self, f, s):
        return {"fsdp": f, "seq": s}

    def on_plane(self, f):
        return self.at(f, self.s)

    def member(self, m):
        return self.at(self.f - self.core + lax.rem(m, 2), self.s - lax.rem(self.s, 2) + m // 2)

    def barrier(self):
        barrier = pltpu.get_barrier_semaphore()
        count = self.n * self.g
        here = self.f * self.g + self.s
        for j in range(1, count):
            other = lax.rem(here + j, count)
            pl.semaphore_signal(barrier, 1, device_id=self.at(other // self.g, lax.rem(other, self.g)), device_id_type=MESH)
        pl.semaphore_wait(barrier, count - 1)


def remote(src, dst, send_sem, recv_sem, device):
    return pltpu.make_async_remote_copy(
        src_ref=src, dst_ref=dst, send_sem=send_sem, recv_sem=recv_sem, device_id=device, device_id_type=MESH)


def aligned(start, size, unit):
    return pl.ds(pl.multiple_of(start, unit), size)


def selection(place, rows, length):
    slot = lax.broadcasted_iota(jnp.int32, (MEM_ROWS, rows), 0)
    position = place.s * rows + lax.broadcasted_iota(jnp.int32, (MEM_ROWS, rows), 1)
    target = jnp.where(slot < MEM, slot, length + slot)
    return jnp.where(jnp.logical_and(position == target, slot < 2 * MEM), 1.0, 0.0)


def forward_kernel(n, g, *refs):
    (
        len_ref, tok_ref, mem_ref, bqv_ref, bout_ref, ga_ref, sa_ref, bup_ref, bdown_ref, gf_ref, sf_ref, cot_ref, sq_ref, so_ref, su_ref, sd_ref,
        y_ref, cot_out, mask_in, vec, fq_ref, fo_ref, fu_ref, fd_ref, xb_out, heads_out, lse_out, ctx_out, r1_out, slope_out, act_out, r2_out,
        wq, wo, wu, wd, x_s, xb, heads, lse, ctx, r1, slope, act, r2, acc_s, nb_s, qkv_send, ctx_send,
        pack, packs, cat, bqkv, bup, mem_s, x_out, x_in, mask_s, cot_s,
        w_send, w_recv, c_send, c_recv, own_sem, q_send_sem, q_recv_sem, k_send_sem, k_recv_sem, save_sem,
        p_send, p_recv, r_send, r_recv, r_local,
    ) = refs
    place = Place(n, g)
    f, s, me = place.f, place.s, place.me
    rows = tok_ref.shape[0]
    span = rows * g
    bf, f32 = jnp.bfloat16, jnp.float32
    place.barrier()

    lands = (wq, wo, wu, wd)
    shards = (sq_ref, so_ref, su_ref, sd_ref)
    fulls = (fq_ref, fo_ref, fu_ref, fd_ref)

    def spot(m, owner, part=None):
        layer, kind = divmod(m, 4)
        depth = shards[kind].shape[1]
        if part is None:
            return lands[kind].at[layer, aligned(owner * depth, depth, 32)]
        return lands[kind].at[layer, aligned(owner * depth + part * (depth // 2), depth // 2, 16)]

    def direct(m, way):
        layer, kind = divmod(m, 4)
        return remote(shards[kind].at[layer], spot(m, f), w_send.at[m, way], w_recv.at[m, way], place.on_plane((place.fx, place.fy)[way]))

    def relay(m, way):
        owner, target = ((place.fy, place.fx), (place.fx, place.fy))[way]
        return remote(spot(m, owner, way), spot(m, owner, way), w_send.at[m, 2 + way], w_recv.at[m, 2 + way], place.on_plane(target))

    def to_core(m, k):
        source = (spot(m, f), spot(m, place.fx), spot(m, place.fy), spot(m, place.fd, 0), spot(m, place.fd, 1))[k]
        return remote(source, source, c_send.at[m, k], c_recv.at[m, k], place.on_plane(place.partner))

    def own_copy(m):
        layer, kind = divmod(m, 4)
        return pltpu.make_async_copy(shards[kind].at[layer], spot(m, f), own_sem.at[m])

    def save_full(m):
        layer, kind = divmod(m, 4)
        return pltpu.make_async_copy(lands[kind].at[layer], fulls[kind].at[layer], own_sem.at[m])

    def launch(m):
        if m < 4 * LAYERS:
            for way in range(2):
                direct(m, way).start()

    def arrived(m):
        for way in range(2):
            direct(m, way).wait_recv()
        for way in range(2):
            relay(m, way).start()
        for k in (1, 2):
            to_core(m, k).start()

    def complete(m):
        for way in range(2):
            relay(m, way).wait_recv()
            to_core(m, 3 + way).start()

    def need(m):
        for k in range(5):
            to_core(m, k).wait_recv()
        save_full(m).start()

    saves = []

    def save(src, dst):
        copy = pltpu.make_async_copy(src, dst, save_sem.at[len(saves)])
        copy.start()
        saves.append(copy)

    length = len_ref[0]
    position = s * rows + lax.broadcasted_iota(jnp.int32, (rows, 1), 0)
    mem_s[...] = jnp.zeros_like(mem_s)
    mem_s[0 : 2 * MEM, :] = mem_ref[0]
    chosen = t_dot(selection(place, rows, length).astype(bf), mem_s[...])
    is_token = jnp.logical_and(position >= MEM, position < length + MEM)
    x_out[...] = (jnp.where(is_token, tok_ref[...].astype(f32), 0.0) + chosen).astype(bf)
    mask_s[...] = jnp.where(lax.broadcasted_iota(jnp.int32, (8, span), 1) < length + 2 * MEM, 0.0, masked_score)

    def move(k, device):
        source, target = ((x_out, x_in), (mask_s, mask_in), (cot_s, cot_out))[k]
        return remote(source, target, r_send.at[k], r_recv.at[k], device)

    @pl.when(jnp.logical_not(place.stays))
    def _():
        for k in range(2):
            move(k, place.away).start()

    launch(0)
    launch(1)

    pack[...] = jnp.zeros_like(pack)
    for v, ref in enumerate((bout_ref, ga_ref, sa_ref, bdown_ref, gf_ref, sf_ref)):
        pack[2 * v : 2 * v + 2, 0 : D // n] = ref[...].astype(f32)
    for t in range(2):
        width = min(128, 2 * D // n - 128 * t)
        pack[16 + 2 * t : 18 + 2 * t, 0:width] = bqv_ref[:, 128 * t : 128 * t + width].astype(f32)
    for t in range(3):
        pack[20 + 2 * t : 22 + 2 * t, :] = bup_ref[:, 128 * t : 128 * t + 128].astype(f32)
    packs[f] = pack[...]

    def p_copy(j):
        return remote(pack, packs.at[f], p_send.at[j - 1], p_recv.at[j - 1], place.on_plane(lax.rem(f + j, n)))

    for j in range(1, n):
        p_copy(j).start()
    for m in range(4 * LAYERS):
        own_copy(m).start()

    cot_s[...] = jnp.where(position < length + 2 * MEM, cot_ref[...], 0.0).astype(bf)

    @pl.when(jnp.logical_not(place.stays))
    def _():
        move(2, place.away).start()

    @pl.when(place.stays)
    def _():
        x_in[...] = x_out[...]
        mask_in[...] = mask_s[...]
        pltpu.make_async_copy(cot_s, cot_out, r_local).start()

    for m in range(4 * LAYERS):
        own_copy(m).wait()
        to_core(m, 0).start()
    arrived(0)
    launch(2)
    launch(3)

    for j in range(1, n):
        owner = lax.rem(f - j + n, n)
        remote(pack, packs.at[owner], p_send.at[j - 1], p_recv.at[j - 1], place.on_plane(owner)).wait_recv()
    for j in range(n):
        cat[:, 128 * j : 128 * j + 128] = packs[j, 0:16, :].astype(bf)
        for layer in range(LAYERS):
            for t in range(3):
                at = (j % 2) * 384 + 128 * t
                row = layer * (FF // D) + j // 2
                bup[row : row + 1, at : at + 128] = packs[j, 20 + 2 * t + layer : 21 + 2 * t + layer, :]
    low_row = lax.broadcasted_iota(jnp.int32, (1, 128), 1) < 64
    for layer in range(LAYERS):
        for grp in range(g):
            row = slice(layer * g + grp, layer * g + grp + 1)
            bqkv[row, :] = jnp.zeros((1, GROUP), f32)
            bqkv[row, 0:128] = packs[grp, 16 + layer : 17 + layer, :]
            bqkv[row, 256:384] = packs[g + grp, 16 + layer : 17 + layer, :]
            turned = pltpu.roll(packs[g + grp, 16:24, :], 64, 1)[2 + layer : 3 + layer]
            bqkv[row, 384:512] = jnp.where(low_row, packs[grp, 18 + layer : 19 + layer, :], turned)
    from_lane = lax.broadcasted_iota(jnp.int32, (128, D), 0)
    to_lane = lax.broadcasted_iota(jnp.int32, (128, D), 1)
    wide = jnp.zeros((16, D), f32)
    for j in range(n):
        spread = jnp.logical_and(to_lane == from_lane + (D // n) * j, from_lane < D // n)
        wide = wide + dot(cat[:, 128 * j : 128 * j + 128], jnp.where(spread, 1.0, 0.0).astype(bf))
    vec[...] = wide

    def vector(kind, layer):
        row = 2 * WIDE.index(kind) + layer
        return vec[row : row + 1, :]

    @pl.when(jnp.logical_not(place.stays))
    def _():
        for k in range(2):
            move(k, place.back).wait_recv()

    lane = lax.broadcasted_iota(jnp.int32, (rows, 128), 1)
    x_s[...] = x_in[...].astype(f32)

    for layer in range(LAYERS):
        m0 = 4 * layer
        xb[layer] = x_s[...].astype(bf)
        save(xb.at[layer], xb_out.at[layer])
        complete(m0)
        need(m0)

        def q_copy(i, layer=layer):
            return remote(
                qkv_send.at[i - 1], heads.at[layer, aligned(me * rows, rows, rows)],
                q_send_sem.at[layer, i - 1], q_recv_sem.at[layer, i - 1], place.member(lax.rem(me + i, g)))

        def q_arrival(i, layer=layer):
            origin = lax.rem(me - i + g, g)
            return remote(
                qkv_send.at[i - 1], heads.at[layer, aligned(origin * rows, rows, rows)],
                q_send_sem.at[layer, i - 1], q_recv_sem.at[layer, i - 1], place.member(origin))

        if layer:
            for i in range(1, g):
                q_copy(i, layer - 1).wait_send()

        for i in list(range(1, g)) + [0]:
            group = lax.rem(me + i, g)
            columns = aligned(group * GROUP, GROUP, 128)
            projected = (dot(xb[layer], wq[layer, :, columns]) + bqkv[pl.ds(layer * g + group, 1), :]).astype(bf)
            if i:
                qkv_send[i - 1] = projected
                q_copy(i).start()
            else:
                heads[layer, aligned(me * rows, rows, rows), :] = projected
        arrived(m0 + 1)
        if layer == 0:
            arrived(m0 + 2)
            launch(m0 + 4)
            complete(m0 + 1)
        else:
            complete(m0 + 1)
            arrived(m0 + 2)
        for i in range(1, g):
            q_arrival(i).wait_recv()
        save(heads.at[layer], heads_out.at[layer])

        def c_copy(i, b):
            return remote(ctx_send.at[layer, i], ctx.at[layer, me], k_send_sem.at[layer, i], k_recv_sem.at[layer, i], place.member(b))

        def attend(i, carry):
            b = lax.rem(me + i, g)
            block = aligned(b * rows, rows, rows)
            q_a = heads[layer, block, 0:128] * bf(HD**-0.5)
            q_d = heads[layer, block, 384:512] * bf(HD**-0.5)
            zero = jnp.zeros_like(q_a)
            outs, logs = [], []
            for h in range(3):
                if h == 2:
                    scores = dot_t(q_d, heads[layer, :, 512:640])
                else:
                    part = jnp.where(lane < 64, q_a, zero) if h == 0 else jnp.where(lane < 64, zero, q_a)
                    scores = dot_t(part, heads[layer, :, 128:256])
                scores = scores + mask_in[0:1, :]
                top = jnp.max(scores, axis=-1, keepdims=True)
                exponent = jnp.exp(scores - top)
                total = jnp.sum(exponent, axis=-1, keepdims=True)
                values = heads[layer, :, 384:512] if h == 2 else heads[layer, :, 256:384]
                outs.append(dot(exponent.astype(bf), values) * (1.0 / total))
                logs.append(top + jnp.log(total))
            table = jnp.where(lane == 0, logs[0], jnp.where(lane == 1, logs[1], logs[2]))
            lse[layer, :, block] = table.T[0:8]
            first = jnp.where(lane < 64, outs[0], outs[1]).astype(bf)
            second = jnp.where(lane < 64, 0.0, outs[2]).astype(bf)

            @pl.when(i < g)
            def _():
                ctx_send[layer, i, :, 0:128] = first
                ctx_send[layer, i, :, 128:256] = second
                c_copy(i, b).start()

            @pl.when(i == g)
            def _():
                ctx[layer, me, :, 0:128] = first
                ctx[layer, me, :, 128:256] = second

            return carry

        lax.fori_loop(1, g + 1, attend, 0)
        save(lse.at[layer], lse_out.at[layer])
        if layer == 0:
            arrived(m0 + 3)
            launch(m0 + 5)
            launch(m0 + 6)
        else:
            arrived(m0 + 3)
        need(m0 + 1)
        for i in range(1, g):
            origin = lax.rem(me - i + g, g)
            remote(ctx_send.at[layer, i], ctx.at[layer, origin], k_send_sem.at[layer, i], k_recv_sem.at[layer, i], place.member(origin)).wait_recv()
        save(ctx.at[layer], ctx_out.at[layer])

        total = x_s[...] + vector(B_OUT, layer)
        for grp in range(g):
            base = grp * 3 * HD
            total = total + dot(ctx[layer, grp, :, 0:128], wo[layer, base : base + 128, :])
            total = total + dot(ctx[layer, grp, :, 128:256], wo[layer, base + 64 : base + 192, :])
        r1[layer] = total
        save(r1.at[layer], r1_out.at[layer])
        normed = standardize(total)[0] * vector(GAIN_A, layer) + vector(SHIFT_A, layer)
        nb_s[...] = normed.astype(bf)
        acc_s[...] = normed + vector(B_DOWN, layer)
        complete(m0 + 2)
        complete(m0 + 3)
        if layer == 0:
            arrived(m0 + 4)
            launch(m0 + 7)
        need(m0 + 2)
        need(m0 + 3)

        def ffn(c, carry):
            columns = aligned(c * D, D, 128)
            up = dot(nb_s[...], wu[layer, :, columns]) + bup[pl.ds(layer * (FF // D) + c, 1), :]
            cdf = 0.5 * lax.erf(up * (0.5**0.5)) + 0.5
            slope[layer, :, columns] = (cdf + up * jnp.exp(-0.5 * up * up) * (0.5 / math.pi) ** 0.5).astype(bf)
            active = (up * cdf).astype(bf)
            act[layer, :, columns] = active
            acc_s[...] += dot(active, wd[layer, columns, :])
            return carry

        lax.fori_loop(0, FF // D, ffn, 0)
        save(slope.at[layer], slope_out.at[layer])
        save(act.at[layer], act_out.at[layer])
        r2[layer] = acc_s[...]
        save(r2.at[layer], r2_out.at[layer])
        x_s[...] = standardize(acc_s[...])[0] * vector(GAIN_F, layer) + vector(SHIFT_F, layer)
    y_ref[...] = x_s[...]

    for m in range(4 * LAYERS):
        for way in range(2):
            direct(m, way).wait_send()
            relay(m, way).wait_send()
        for k in range(5):
            to_core(m, k).wait_send()
        save_full(m).wait()
    for j in range(1, n):
        p_copy(j).wait_send()
    for i in range(1, g):
        q_copy(i, LAYERS - 1).wait_send()
    for layer in range(LAYERS):
        for i in range(1, g):
            remote(ctx_send.at[layer, i], ctx.at[layer, me], k_send_sem.at[layer, i], k_recv_sem.at[layer, i], place.member(lax.rem(me + i, g))).wait_send()
    for copy in saves:
        copy.wait()

    @pl.when(jnp.logical_not(place.stays))
    def _():
        for k in range(3):
            move(k, place.away).wait_send()
        move(2, place.back).wait_recv()

    @pl.when(place.stays)
    def _():
        pltpu.make_async_copy(cot_s, cot_out, r_local).wait()


def run_forward(n, g, lengths, tokens, memory, vectors, cotangent, sq, so, su, sd):
    rows, span = tokens.shape[0], tokens.shape[0] * g
    any_spec = pl.BlockSpec(memory_space=pl.ANY)
    vmem = pl.BlockSpec(memory_space=pltpu.VMEM)
    bf, f32 = jnp.bfloat16, jnp.float32
    shapes = [
        ((rows, D), f32, vmem),
        ((rows, D), bf, any_spec),
        ((8, span), f32, vmem),
        ((16, D), f32, vmem),
        ((LAYERS, D, g * GROUP), bf, any_spec),
        ((LAYERS, D, D), bf, any_spec),
        ((LAYERS, D, FF), bf, any_spec),
        ((LAYERS, FF, D), bf, any_spec),
        ((LAYERS, rows, D), bf, any_spec),
        ((LAYERS, span, GROUP), bf, any_spec),
        ((LAYERS, 8, span), f32, any_spec),
        ((LAYERS, g, rows, CTX), bf, any_spec),
        ((LAYERS, rows, D), f32, any_spec),
        ((LAYERS, rows, FF), bf, any_spec),
        ((LAYERS, rows, FF), bf, any_spec),
        ((LAYERS, rows, D), f32, any_spec),
    ]
    dma = pltpu.SemaphoreType.DMA
    return pl.pallas_call(
        functools.partial(forward_kernel, n, g),
        name="forward",
        out_shape=[jax.ShapeDtypeStruct(a, b) for a, b, _ in shapes],
        in_specs=[pl.BlockSpec(memory_space=pltpu.SMEM)] + [vmem] * 11 + [any_spec] * 4,
        out_specs=[c for _, _, c in shapes],
        scratch_shapes=[
            pltpu.VMEM((LAYERS, D, g * GROUP), bf),
            pltpu.VMEM((LAYERS, D, D), bf),
            pltpu.VMEM((LAYERS, D, FF), bf),
            pltpu.VMEM((LAYERS, FF, D), bf),
            pltpu.VMEM((rows, D), f32),
            pltpu.VMEM((LAYERS, rows, D), bf),
            pltpu.VMEM((LAYERS, span, GROUP), bf),
            pltpu.VMEM((LAYERS, 8, span), f32),
            pltpu.VMEM((LAYERS, g, rows, CTX), bf),
            pltpu.VMEM((LAYERS, rows, D), f32),
            pltpu.VMEM((LAYERS, rows, FF), bf),
            pltpu.VMEM((LAYERS, rows, FF), bf),
            pltpu.VMEM((LAYERS, rows, D), f32),
            pltpu.VMEM((rows, D), f32),
            pltpu.VMEM((rows, D), bf),
            pltpu.VMEM((g - 1, rows, GROUP), bf),
            pltpu.VMEM((LAYERS, g, rows, CTX), bf),
            pltpu.VMEM((32, 128), f32),
            pltpu.VMEM((n, 32, 128), f32),
            pltpu.VMEM((16, n * 128), bf),
            pltpu.VMEM((LAYERS * g, GROUP), f32),
            pltpu.VMEM((LAYERS * (FF // D), D), f32),
            pltpu.VMEM((MEM_ROWS, D), bf),
            pltpu.VMEM((rows, D), bf),
            pltpu.VMEM((rows, D), bf),
            pltpu.VMEM((8, span), f32),
            pltpu.VMEM((rows, D), bf),
            dma((4 * LAYERS, 4)),
            dma((4 * LAYERS, 4)),
            dma((4 * LAYERS, 5)),
            dma((4 * LAYERS, 5)),
            dma((4 * LAYERS,)),
            dma((LAYERS, g - 1)),
            dma((LAYERS, g - 1)),
            dma((LAYERS, g)),
            dma((LAYERS, g)),
            dma((8 * LAYERS,)),
            dma((n - 1,)),
            dma((n - 1,)),
            dma((3,)),
            dma((3,)),
            dma(()),
        ],
        compiler_params=pltpu.CompilerParams(
            collective_id=0, has_side_effects=True, vmem_limit_bytes=62 * 1024 * 1024
        ),
    )(lengths, tokens, memory, *vectors, cotangent, sq, so, su, sd)


def group_columns(w, g):
    lead = w.shape[:-1]
    q, k, v = (w[..., i * D : (i + 1) * D].reshape(lead + (g, 3 * HD)) for i in range(3))
    return jnp.concatenate(
        [q[..., :128], k[..., :128], v[..., :128], q[..., 128:], v[..., 128:], k[..., 128:], jnp.zeros_like(k[..., 128:])], axis=-1)


def ungroup_columns(w):
    lead = w.shape[:-2]
    q = jnp.concatenate([w[..., 0:128], w[..., 384:448]], axis=-1).reshape(lead + (D,))
    k = jnp.concatenate([w[..., 128:256], w[..., 512:576]], axis=-1).reshape(lead + (D,))
    v = jnp.concatenate([w[..., 256:384], w[..., 448:512]], axis=-1).reshape(lead + (D,))
    return jnp.concatenate([q, k, v], axis=-1)


def norm_rows(values, gain_vec, shift_vec):
    row_mean = jnp.mean(values, axis=-1, keepdims=True)
    centred = values - row_mean
    variance = jnp.mean(centred * centred, axis=-1, keepdims=True)
    return centred * lax.rsqrt(variance + norm_eps) * gain_vec + shift_vec


def gelu_exact(values):
    return jax.nn.gelu(values, approximate=False)


def gather_layer(stacks, layer_index):
    (
        w_qkv,
        b_qv,
        w_out,
        b_out,
        gain_attn,
        shift_attn,
        w_up,
        b_up,
        w_down,
        b_down,
        gain_ffn,
        shift_ffn,
    ) = tuple((stacked[layer_index] for stacked in stacks))
    return (
        lax.all_gather(w_qkv, "fsdp", axis=0, tiled=True),
        lax.all_gather(b_qv, "fsdp", axis=0, tiled=True),
        lax.all_gather(w_out, "fsdp", axis=0, tiled=True),
        lax.all_gather(b_out, "fsdp", axis=0, tiled=True),
        lax.all_gather(gain_attn, "fsdp", axis=0, tiled=True),
        lax.all_gather(shift_attn, "fsdp", axis=0, tiled=True),
        lax.all_gather(w_up, "fsdp", axis=0, tiled=True),
        lax.all_gather(b_up, "fsdp", axis=0, tiled=True),
        lax.all_gather(w_down, "fsdp", axis=0, tiled=True),
        lax.all_gather(b_down, "fsdp", axis=0, tiled=True),
        lax.all_gather(gain_ffn, "fsdp", axis=0, tiled=True),
        lax.all_gather(shift_ffn, "fsdp", axis=0, tiled=True),
    )


def attend_forward(queries, keys_all, values_all, key_live):
    total_rows, local_heads = (queries.shape[0], queries.shape[1])
    block_rows = math.gcd(total_rows, 512)
    block_count = total_rows // block_rows
    score_scale = HD ** (-0.5)

    def one_block(query_block):
        scores = (
            jnp.einsum("qhd,khd->hqk", query_block, keys_all, preferred_element_type=jnp.float32)
            * score_scale
        )
        scores = jnp.where(key_live[None, None, :], scores, masked_score)
        top_score = jnp.max(scores, axis=-1, keepdims=True)
        exponent = jnp.exp(scores - top_score)
        row_total = jnp.sum(exponent, axis=-1, keepdims=True)
        probability = (exponent / row_total).astype(jnp.bfloat16)
        context = jnp.einsum(
            "hqk,khd->qhd", probability, values_all, preferred_element_type=jnp.float32
        )
        return (context.astype(jnp.bfloat16), (top_score + jnp.log(row_total))[..., 0])

    blocks = queries.reshape(block_count, block_rows, local_heads, HD)
    context, log_total = lax.map(one_block, blocks)
    return (context.reshape(total_rows, local_heads, HD), log_total)


def attend_backward(queries, keys_all, values_all, grad_context, log_total, key_live):
    total_rows, local_heads = (queries.shape[0], queries.shape[1])
    block_rows = math.gcd(total_rows, 512)
    block_count = total_rows // block_rows
    score_scale = HD ** (-0.5)

    def one_block(running, inputs):
        grad_keys, grad_values = running
        query_block, grad_block, log_block = inputs
        scores = (
            jnp.einsum("qhd,khd->hqk", query_block, keys_all, preferred_element_type=jnp.float32)
            * score_scale
        )
        scores = jnp.where(key_live[None, None, :], scores, masked_score)
        probability = jnp.exp(scores - log_block[:, :, None])
        grad_prob = jnp.einsum(
            "qhd,khd->hqk", grad_block, values_all, preferred_element_type=jnp.float32
        )
        grad_values = grad_values + jnp.einsum(
            "hqk,qhd->khd",
            probability.astype(jnp.bfloat16),
            grad_block,
            preferred_element_type=jnp.float32,
        )
        inner_sum = jnp.sum(grad_prob * probability, axis=-1, keepdims=True)
        grad_scores = (probability * (grad_prob - inner_sum)).astype(jnp.bfloat16)
        grad_query = (
            jnp.einsum("hqk,khd->qhd", grad_scores, keys_all, preferred_element_type=jnp.float32)
            * score_scale
        )
        grad_keys = (
            grad_keys
            + jnp.einsum(
                "hqk,qhd->khd", grad_scores, query_block, preferred_element_type=jnp.float32
            )
            * score_scale
        )
        return ((grad_keys, grad_values), grad_query)

    zero_keys = jnp.zeros((total_rows, local_heads, HD), jnp.float32)
    shaped = (
        queries.reshape(block_count, block_rows, local_heads, HD),
        grad_context.reshape(block_count, block_rows, local_heads, HD),
        log_total,
    )
    (grad_keys, grad_values), grad_queries = lax.scan(one_block, (zero_keys, zero_keys), shaped)
    return (grad_queries.reshape(total_rows, local_heads, HD), grad_keys, grad_values)


def layer_forward(hidden, weights, key_live):
    (
        w_qkv,
        b_qv,
        w_out,
        b_out,
        gain_attn,
        shift_attn,
        w_up,
        b_up,
        w_down,
        b_down,
        gain_ffn,
        shift_ffn,
    ) = weights
    local_rows = hidden.shape[0]
    groups = lax.axis_size("seq")
    local_heads = HEADS // groups
    bias_qv = b_qv.astype(jnp.float32)
    bias_full = jnp.concatenate([bias_qv[:D], jnp.zeros((D,), jnp.float32), bias_qv[D:]])
    hidden_low = hidden.astype(jnp.bfloat16)
    projected = (jnp.dot(hidden_low, w_qkv, preferred_element_type=jnp.float32) + bias_full).astype(
        jnp.bfloat16
    )
    by_head = lax.all_to_all(
        projected.reshape(local_rows, 3, groups, local_heads, HD),
        "seq",
        split_axis=2,
        concat_axis=0,
        tiled=True,
    )
    context, log_total = attend_forward(
        by_head[:, 0, 0], by_head[:, 1, 0], by_head[:, 2, 0], key_live
    )
    ctx_rows = lax.all_to_all(
        context.reshape(local_rows * groups, 1, local_heads, HD),
        "seq",
        split_axis=0,
        concat_axis=1,
        tiled=True,
    ).reshape(local_rows, D)
    attended = jnp.dot(ctx_rows, w_out, preferred_element_type=jnp.float32) + b_out.astype(
        jnp.float32
    )
    residual_one = hidden + attended
    normed = norm_rows(residual_one, gain_attn.astype(jnp.float32), shift_attn.astype(jnp.float32))
    pre_gelu = jnp.dot(
        normed.astype(jnp.bfloat16), w_up, preferred_element_type=jnp.float32
    ) + b_up.astype(jnp.float32)
    active = gelu_exact(pre_gelu).astype(jnp.bfloat16)
    branch_out = jnp.dot(active, w_down, preferred_element_type=jnp.float32) + b_down.astype(
        jnp.float32
    )
    residual_two = normed + branch_out
    output = norm_rows(residual_two, gain_ffn.astype(jnp.float32), shift_ffn.astype(jnp.float32))
    stored = (
        hidden,
        by_head,
        log_total,
        ctx_rows,
        residual_one,
        normed,
        pre_gelu,
        active,
        residual_two,
    )
    return (output, stored)


def layer_backward(grad_output, weights, stored, key_live):
    (
        w_qkv,
        b_qv,
        w_out,
        b_out,
        gain_attn,
        shift_attn,
        w_up,
        b_up,
        w_down,
        b_down,
        gain_ffn,
        shift_ffn,
    ) = weights
    hidden, by_head, log_total, ctx_rows, residual_one, normed, pre_gelu, active, residual_two = (
        stored
    )
    local_rows = hidden.shape[0]
    groups = lax.axis_size("seq")
    local_heads = HEADS // groups
    ffn_pull = jax.vjp(
        norm_rows, residual_two, gain_ffn.astype(jnp.float32), shift_ffn.astype(jnp.float32)
    )[1]
    grad_two, grad_gain_ffn, grad_shift_ffn = ffn_pull(grad_output)
    grad_branch = grad_two.astype(jnp.bfloat16)
    grad_b_down = jnp.sum(grad_branch.astype(jnp.float32), axis=0)
    grad_w_down = jnp.einsum("rf,rd->fd", active, grad_branch, preferred_element_type=jnp.float32)
    grad_active = jnp.einsum("rd,fd->rf", grad_branch, w_down, preferred_element_type=jnp.float32)
    gelu_pull = jax.vjp(gelu_exact, pre_gelu)[1]
    grad_pre = gelu_pull(grad_active)[0].astype(jnp.bfloat16)
    grad_b_up = jnp.sum(grad_pre.astype(jnp.float32), axis=0)
    normed_low = normed.astype(jnp.bfloat16)
    grad_w_up = jnp.einsum("rd,rf->df", normed_low, grad_pre, preferred_element_type=jnp.float32)
    grad_normed = (
        jnp.einsum("rf,df->rd", grad_pre, w_up, preferred_element_type=jnp.float32) + grad_two
    )
    attn_pull = jax.vjp(
        norm_rows, residual_one, gain_attn.astype(jnp.float32), shift_attn.astype(jnp.float32)
    )[1]
    grad_one, grad_gain_attn, grad_shift_attn = attn_pull(grad_normed)
    grad_attended = grad_one.astype(jnp.bfloat16)
    grad_b_out = jnp.sum(grad_attended.astype(jnp.float32), axis=0)
    grad_w_out = jnp.einsum(
        "rk,rd->kd", ctx_rows, grad_attended, preferred_element_type=jnp.float32
    )
    grad_ctx = jnp.einsum(
        "rd,kd->rk", grad_attended, w_out, preferred_element_type=jnp.float32
    ).astype(jnp.bfloat16)
    grad_heads = lax.all_to_all(
        grad_ctx.reshape(local_rows, groups, local_heads, HD),
        "seq",
        split_axis=1,
        concat_axis=0,
        tiled=True,
    )
    grad_queries, grad_keys, grad_values = attend_backward(
        by_head[:, 0, 0], by_head[:, 1, 0], by_head[:, 2, 0], grad_heads[:, 0], log_total, key_live
    )
    grad_stack = jnp.stack([grad_queries, grad_keys, grad_values], axis=1).astype(jnp.bfloat16)[
        :, :, None
    ]
    grad_projected = lax.all_to_all(
        grad_stack, "seq", split_axis=0, concat_axis=2, tiled=True
    ).reshape(local_rows, 3 * D)
    grad_sums = jnp.sum(grad_projected.astype(jnp.float32), axis=0)
    grad_b_qv = jnp.concatenate([grad_sums[:D], grad_sums[2 * D :]])
    hidden_low = hidden.astype(jnp.bfloat16)
    grad_w_qkv = jnp.einsum(
        "rd,re->de", hidden_low, grad_projected, preferred_element_type=jnp.float32
    )
    grad_hidden = (
        jnp.einsum("re,de->rd", grad_projected, w_qkv, preferred_element_type=jnp.float32)
        + grad_one
    )
    weight_grads = (
        grad_w_qkv,
        grad_b_qv,
        grad_w_out,
        grad_b_out,
        grad_gain_attn,
        grad_shift_attn,
        grad_w_up,
        grad_b_up,
        grad_w_down,
        grad_b_down,
        grad_gain_ffn,
        grad_shift_ffn,
    )
    return (grad_hidden, weight_grads)


def fsdp_layer_sum(weight_grads):
    (
        grad_w_qkv,
        grad_b_qv,
        grad_w_out,
        grad_b_out,
        grad_gain_attn,
        grad_shift_attn,
        grad_w_up,
        grad_b_up,
        grad_w_down,
        grad_b_down,
        grad_gain_ffn,
        grad_shift_ffn,
    ) = weight_grads
    return (
        lax.psum_scatter(grad_w_qkv.astype(jnp.bfloat16), "fsdp", scatter_dimension=0, tiled=True),
        lax.psum_scatter(grad_b_qv.astype(jnp.bfloat16), "fsdp", scatter_dimension=0, tiled=True),
        lax.psum_scatter(grad_w_out.astype(jnp.bfloat16), "fsdp", scatter_dimension=0, tiled=True),
        lax.psum_scatter(grad_b_out.astype(jnp.bfloat16), "fsdp", scatter_dimension=0, tiled=True),
        lax.psum_scatter(grad_gain_attn.astype(jnp.bfloat16), "fsdp", scatter_dimension=0, tiled=True),
        lax.psum_scatter(grad_shift_attn.astype(jnp.bfloat16), "fsdp", scatter_dimension=0, tiled=True),
        lax.psum_scatter(grad_w_up.astype(jnp.bfloat16), "fsdp", scatter_dimension=0, tiled=True),
        lax.psum_scatter(grad_b_up.astype(jnp.bfloat16), "fsdp", scatter_dimension=0, tiled=True),
        lax.psum_scatter(grad_w_down.astype(jnp.bfloat16), "fsdp", scatter_dimension=0, tiled=True),
        lax.psum_scatter(grad_b_down.astype(jnp.bfloat16), "fsdp", scatter_dimension=0, tiled=True),
        lax.psum_scatter(grad_gain_ffn.astype(jnp.bfloat16), "fsdp", scatter_dimension=0, tiled=True),
        lax.psum_scatter(grad_shift_ffn.astype(jnp.bfloat16), "fsdp", scatter_dimension=0, tiled=True),
    )


def seq_total_sum(shard_grads, grad_memory):
    (
        grad_w_qkv,
        grad_b_qv,
        grad_w_out,
        grad_b_out,
        grad_gain_attn,
        grad_shift_attn,
        grad_w_up,
        grad_b_up,
        grad_w_down,
        grad_b_down,
        grad_gain_ffn,
        grad_shift_ffn,
    ) = shard_grads
    pieces = (
        lax.psum_scatter(
            grad_w_qkv.astype(jnp.bfloat16), "seq", scatter_dimension=2, tiled=True
        ).astype(jnp.float32),
        lax.psum_scatter(
            grad_w_out.astype(jnp.bfloat16), "seq", scatter_dimension=2, tiled=True
        ).astype(jnp.float32),
        lax.psum_scatter(
            grad_w_up.astype(jnp.bfloat16), "seq", scatter_dimension=2, tiled=True
        ).astype(jnp.float32),
        lax.psum_scatter(
            grad_w_down.astype(jnp.bfloat16), "seq", scatter_dimension=2, tiled=True
        ).astype(jnp.float32),
    )
    matrices = (
        lax.all_gather(pieces[0].astype(jnp.bfloat16), "seq", axis=2, tiled=True).astype(
            jnp.float32
        ),
        lax.all_gather(pieces[1].astype(jnp.bfloat16), "seq", axis=2, tiled=True).astype(
            jnp.float32
        ),
        lax.all_gather(pieces[2].astype(jnp.bfloat16), "seq", axis=2, tiled=True).astype(
            jnp.float32
        ),
        lax.all_gather(pieces[3].astype(jnp.bfloat16), "seq", axis=2, tiled=True).astype(
            jnp.float32
        ),
    )
    smalls = (
        lax.psum(grad_b_qv.astype(jnp.bfloat16), "seq").astype(jnp.float32),
        lax.psum(grad_b_out.astype(jnp.bfloat16), "seq").astype(jnp.float32),
        lax.psum(grad_gain_attn.astype(jnp.bfloat16), "seq").astype(jnp.float32),
        lax.psum(grad_shift_attn.astype(jnp.bfloat16), "seq").astype(jnp.float32),
        lax.psum(grad_b_up.astype(jnp.bfloat16), "seq").astype(jnp.float32),
        lax.psum(grad_b_down.astype(jnp.bfloat16), "seq").astype(jnp.float32),
        lax.psum(grad_gain_ffn.astype(jnp.bfloat16), "seq").astype(jnp.float32),
        lax.psum(grad_shift_ffn.astype(jnp.bfloat16), "seq").astype(jnp.float32),
        lax.psum(grad_memory.astype(jnp.bfloat16), "seq").astype(jnp.float32),
    )
    weights_sum = (
        matrices[0],
        smalls[0],
        matrices[1],
        smalls[1],
        smalls[2],
        smalls[3],
        matrices[2],
        smalls[4],
        matrices[3],
        smalls[5],
        smalls[6],
        smalls[7],
    )
    return (weights_sum, smalls[8])


def plain_body(
    tokens,
    memory,
    lengths,
    w_qkv,
    b_qv,
    w_out,
    b_out,
    gain_attn,
    shift_attn,
    w_up,
    b_up,
    w_down,
    b_down,
    gain_ffn,
    shift_ffn,
    cotangent,
):
    local_rows = tokens.shape[0]
    groups = lax.axis_size("seq")
    seq_place = lax.axis_index("seq")
    length = lengths[0]
    positions = seq_place * local_rows + jnp.arange(local_rows, dtype=jnp.int32)
    key_live = jnp.arange(local_rows * groups, dtype=jnp.int32) < length + 2 * MEM
    row_live = (positions < length + 2 * MEM)[:, None]
    token_live = ((positions >= MEM) & (positions < length + MEM))[:, None]
    memory_slots = jnp.arange(2 * MEM, dtype=jnp.int32)
    targets = jnp.where(memory_slots < MEM, memory_slots, length + memory_slots)
    select = positions[:, None] == targets[None, :]
    hidden = jnp.where(token_live, tokens.astype(jnp.float32), 0.0) + jnp.dot(
        select.astype(jnp.bfloat16), memory[0], preferred_element_type=jnp.float32
    )
    stacks = (
        w_qkv,
        b_qv,
        w_out,
        b_out,
        gain_attn,
        shift_attn,
        w_up,
        b_up,
        w_down,
        b_down,
        gain_ffn,
        shift_ffn,
    )
    kept = []
    for layer_index in range(LAYERS):
        weights = gather_layer(stacks, layer_index)
        hidden, stored = layer_forward(hidden, weights, key_live)
        kept.append((weights, stored))
    result = jnp.where(row_live, hidden, 0.0)
    grad_hidden = jnp.where(row_live, cotangent, 0.0)
    collected = []
    for layer_index in reversed(range(LAYERS)):
        weights, stored = kept[layer_index]
        grad_hidden, weight_grads = layer_backward(grad_hidden, weights, stored, key_live)
        collected.insert(0, fsdp_layer_sum(weight_grads))
    stacked_grads = tuple((jnp.stack(member) for member in zip(*collected)))
    grad_tokens = jnp.where(token_live, grad_hidden, 0.0)
    grad_memory = jnp.dot(
        select.astype(jnp.float32).T, grad_hidden, precision=lax.Precision.HIGHEST
    )[None]
    summed, memory_sum = seq_total_sum(stacked_grads, grad_memory)
    return (result, grad_tokens, memory_sum) + tuple(summed)


def backward_kernel(n, g, *refs):
    (
        len_ref, mask_ref, vec, cot_ref, y_ref, fq_ref, fo_ref, fu_ref, fd_ref, xb_ref, heads_ref, lse_ref, ctx_ref, r1_ref, slope_ref, act_ref, r2_ref,
        result_ref, tokens_ref, memory_ref, bqv_out, bout_out, ga_out, sa_out, bup_out, bdown_out, gf_out, sf_out, oq_ref, oo_ref, ou_ref, od_ref,
        wq, wo, wu, wd, slope, act, xb, hd, lse, ctx, r1, r2,
        p_q, p_o, p_u, p_d, pair_q, pair_o, pair_u, pair_d, half_q, half_o, half_u, half_d, plane_q, plane_o, plane_u, plane_d,
        sum_q, sum_o, sum_u, sum_d, whole_q, whole_o, whole_u, whole_d, part_q, part_o, part_u, part_d,
        gx, gn, norm_t, low, live, home, gc_send, gctx, key_t, acc_k, acc_v, acc_d, acc_e, dq_s, g_send, g_in,
        small_a, small_b, small_c, land_a, land_b, land_c,
        load_sem, stream_sem, pair_send, pair_recv, half_send, half_recv, plane_send, plane_recv, z_send, z_recv, out_send, out_recv, out_own,
        c_send, c_recv, g_send_sem, g_recv_sem, sa_send, sa_recv, sb_send, sb_recv, sc_send, sc_recv, home_send, home_recv, store_sem,
        pair_credit, half_credit, plane_credit, z_credit,
    ) = refs
    place = Place(n, g)
    f, s, me, core = place.f, place.s, place.me, place.core
    rows = gx.shape[0]
    span = rows * g
    half = n // 2
    partner = place.on_plane(place.partner)
    bf, f32 = jnp.bfloat16, jnp.float32
    parts = (p_q, p_o, p_u, p_d)
    pairs = (pair_q, pair_o, pair_u, pair_d)
    halves = (half_q, half_o, half_u, half_d)
    planes = (plane_q, plane_o, plane_u, plane_d)
    sums = (sum_q, sum_o, sum_u, sum_d)
    wholes = (whole_q, whole_o, whole_u, whole_d)
    inners = (part_q, part_o, part_u, part_d)
    outs = (oq_ref, oo_ref, ou_ref, od_ref)
    Q, O, U, DN = 0, 1, 2, 3
    inner = jnp.logical_and(s > 0, s < g - 1)
    outer = jnp.logical_not(inner)
    side = s // 2
    inner_chip = place.at(f, 1 + side)
    other_inner = place.at(f, 3 - s)
    end_chip = place.at(f, 3 * side)

    def member(i):
        return place.member(lax.rem(me + i, g))

    def depth(m):
        return pairs[m].shape[1]

    def part_rows(m, owner):
        return parts[m].at[aligned(owner * depth(m), depth(m), 32)]

    def part_half(m, owner, which):
        return parts[m].at[aligned(owner * depth(m) + which * (depth(m) // 2), depth(m) // 2, 16)]

    def half_rows(ref, m, which):
        return ref.at[aligned(which * (depth(m) // 2), depth(m) // 2, 16)]

    names = {}

    def load(name, src, dst):
        index = {"xb": 0, "hd": 1, "lse": 2, "ctx": 3, "r1": 4, "r2": 5, "wq": 6, "wo": 7, "cot": 8, "y": 9}[name]
        copy = pltpu.make_async_copy(src, dst, load_sem.at[index])
        copy.start()
        names[name] = copy

    def loaded(name):
        names.pop(name).wait()

    def stream(layer, c, slot):
        columns = pl.ds(pl.multiple_of(c * D, 128), D)
        return [
            pltpu.make_async_copy(fd_ref.at[layer, columns, :], wd.at[slot], stream_sem.at[0, slot]),
            pltpu.make_async_copy(fu_ref.at[layer, :, columns], wu.at[slot], stream_sem.at[1, slot]),
            pltpu.make_async_copy(slope_ref.at[layer, :, columns], slope.at[slot], stream_sem.at[2, slot]),
            pltpu.make_async_copy(act_ref.at[layer, :, columns], act.at[slot], stream_sem.at[3, slot]),
        ]

    last = LAYERS - 1
    for copy in stream(last, 0, 0):
        copy.start()
    load("cot", cot_ref, low.at[0])
    load("y", y_ref, gn)
    load("r2", r2_ref.at[last], r2)
    load("r1", r1_ref.at[last], r1)
    load("wo", fo_ref.at[last], wo)
    load("ctx", ctx_ref.at[last], ctx)
    load("hd", heads_ref.at[last], hd)
    load("lse", lse_ref.at[last], lse)
    load("xb", xb_ref.at[last], xb)
    load("wq", fq_ref.at[last], wq)

    place.barrier()

    def pair_copy(layer, m, c):
        return remote(part_rows(m, 2 * c + 1 - core), pairs[m].at[c], pair_send.at[layer, m, c], pair_recv.at[layer, m, c], partner)

    def half_copy(layer, m, way):
        device = place.on_plane((place.fx, place.fy)[way])
        return remote(part_half(m, place.fd, way), halves[m].at[way], half_send.at[layer, m, way], half_recv.at[layer, m, way], device)

    def plane_copy(layer, m, way):
        owner = (place.fx, place.fy)[way]
        return remote(part_rows(m, owner), planes[m].at[way], plane_send.at[layer, m, way], plane_recv.at[layer, m, way], place.on_plane(owner))

    def end_copy(layer, m):
        return remote(sums[m].at[layer], wholes[m], z_send.at[layer, m, 0], z_recv.at[layer, m, 0], inner_chip)

    def inner_copy(layer, m):
        return remote(half_rows(sums[m].at[layer], m, 1 - side), inners[m], z_send.at[layer, m, 1], z_recv.at[layer, m, 1], other_inner)

    def out_across(layer, m):
        return remote(half_rows(sums[m].at[layer], m, side), half_rows(outs[m].at[layer], m, side), out_send.at[layer, m, 0], out_recv.at[layer, m, 0], other_inner)

    def out_end(layer, m):
        return remote(half_rows(sums[m].at[layer], m, side), half_rows(outs[m].at[layer], m, side), out_send.at[layer, m, 1], out_recv.at[layer, m, 1], end_chip)

    def out_pass(layer, m):
        other = half_rows(outs[m].at[layer], m, 1 - side)
        return remote(other, other, out_send.at[layer, m, 2], out_recv.at[layer, m, 2], end_chip)

    def out_local(layer, m):
        return pltpu.make_async_copy(half_rows(sums[m].at[layer], m, side), half_rows(outs[m].at[layer], m, side), out_own.at[layer, m])

    def pair_ready(layer, m):
        if layer != last:
            pl.semaphore_wait(pair_credit.at[m], 1)

    def each(count, step, body):
        def go(k, carry):
            body(k * step)
            return carry

        lax.fori_loop(0, count // step, go, 0)

    def add(target, start, source, count, m):
        step = 48 if count % 32 else 32

        def body(at):
            mine, theirs = aligned(start + at, step, 16), aligned(at, step, 16)
            target[mine, :] = (target[mine, :].astype(f32) + source[theirs, :].astype(f32)).astype(bf)

        each(count, step, body)

    def sum_pair(layer, m):
        for c in range(half):
            pair_copy(layer, m, c).wait_recv()
        for c in range(half):
            pair_copy(layer, m, c).wait_send()
        for owner in (place.fd, place.fx, place.fy, f):
            add(parts[m], owner * depth(m), pairs[m].at[owner // 2], depth(m), m)
            if owner is place.fd:
                for way in range(2):
                    if layer != last:
                        pl.semaphore_wait(half_credit.at[m, way], 1)
                    half_copy(layer, m, way).start()
        if layer:
            pl.semaphore_signal(pair_credit.at[m], 1, device_id=partner, device_id_type=MESH)

    def sum_half(layer, m):
        for way in range(2):
            half_copy(layer, m, way).wait_recv()
            owner = (place.fy, place.fx)[way]
            add(parts[m], owner * depth(m) + way * (depth(m) // 2), halves[m].at[way], depth(m) // 2, m)
            if layer != last:
                pl.semaphore_wait(plane_credit.at[m, 1 - way], 1)
            plane_copy(layer, m, 1 - way).start()
        for way in range(2):
            if layer:
                pl.semaphore_signal(
                    half_credit.at[m, way], 1, device_id=place.on_plane((place.fx, place.fy)[way]), device_id_type=MESH)
            half_copy(layer, m, way).wait_send()

    def sum_plane(layer, m):
        for way in range(2):
            plane_copy(layer, m, way).wait_recv()

        def body(at):
            mine, theirs = aligned(f * depth(m) + at, 32, 32), aligned(at, 32, 32)
            total = parts[m][mine, :].astype(f32) + planes[m][0, theirs, :].astype(f32) + planes[m][1, theirs, :].astype(f32)
            sums[m][layer, theirs, :] = total.astype(bf)

        each(depth(m), 32, body)
        for way in range(2):
            if layer:
                pl.semaphore_signal(
                    plane_credit.at[m, way], 1, device_id=place.on_plane((place.fx, place.fy)[way]), device_id_type=MESH)
            plane_copy(layer, m, way).wait_send()

        @pl.when(outer)
        def _():
            if layer != last:
                pl.semaphore_wait(z_credit.at[m, 0], 1)
            end_copy(layer, m).start()

    def sum_end(layer, m):
        @pl.when(inner)
        def _():
            end_copy(layer, m).wait_recv()
            add(sums[m].at[layer], (1 - side) * (depth(m) // 2), half_rows(wholes[m], m, 1 - side), depth(m) // 2, m)
            if layer != last:
                pl.semaphore_wait(z_credit.at[m, 1], 1)
            inner_copy(layer, m).start()
            add(sums[m].at[layer], side * (depth(m) // 2), half_rows(wholes[m], m, side), depth(m) // 2, m)
            if layer:
                pl.semaphore_signal(z_credit.at[m, 0], 1, device_id=end_chip, device_id_type=MESH)

    def sum_line(layer, m):
        @pl.when(inner)
        def _():
            inner_copy(layer, m).wait_recv()
            add(sums[m].at[layer], side * (depth(m) // 2), inners[m], depth(m) // 2, m)
            out_across(layer, m).start()
            out_end(layer, m).start()
            out_local(layer, m).start()
            if layer:
                pl.semaphore_signal(z_credit.at[m, 1], 1, device_id=other_inner, device_id_type=MESH)

    def pass_on(layer, m):
        @pl.when(inner)
        def _():
            out_across(layer, m).wait_recv()
            out_pass(layer, m).start()

    lane = lax.broadcasted_iota(jnp.int32, (rows, 128), 1)
    low_lane = lane < 64

    def vector(kind, layer):
        row = 2 * WIDE.index(kind) + layer
        return vec[row : row + 1, :]

    def norm_back(grad, residual, layer, gain_row, shift_row):
        standard, scale = standardize(residual)
        small_a[layer * SMALL + gain_row : layer * SMALL + gain_row + 1, :] = jnp.sum(grad * standard, axis=0, keepdims=True)
        small_a[layer * SMALL + shift_row : layer * SMALL + shift_row + 1, :] = jnp.sum(grad, axis=0, keepdims=True)
        inner = grad * vector(gain_row, layer)
        back = scale * (inner - jnp.mean(inner, -1, keepdims=True) - standard * jnp.mean(inner * standard, -1, keepdims=True))
        return back, standard

    def row_sum(layer, row, values):
        small_a[layer * SMALL + row : layer * SMALL + row + 1, : values.shape[1]] = jnp.sum(values.astype(f32), axis=0, keepdims=True)

    def go_home(slot, device):
        return remote(low.at[slot], home.at[slot], home_send.at[slot], home_recv.at[slot], device)

    def send_home(slot):
        @pl.when(jnp.logical_not(place.stays))
        def _():
            go_home(slot, place.away_home).start()

        @pl.when(place.stays)
        def _():
            home[slot] = low[slot]

    def sent_home(slot):
        @pl.when(jnp.logical_not(place.stays))
        def _():
            go_home(slot, place.away_home).wait_send()

    def came_home(slot):
        @pl.when(jnp.logical_not(place.stays))
        def _():
            go_home(slot, place.away_home).wait_recv()

    small_a[...] = jnp.zeros_like(small_a)
    live[...] = jnp.where(jnp.broadcast_to(mask_ref[0:1, :], (128, span)) < 0.0, 0.0, 1.0).T.astype(bf)
    loaded("y")
    low[1] = gn[...].astype(bf)
    send_home(1)
    loaded("cot")
    gx[...] = low[0].astype(f32)

    for layer in reversed(range(LAYERS)):
        loaded("r2")
        grad_two, _ = norm_back(gx[...], r2[...], layer, GAIN_F, SHIFT_F)
        gn[...] = grad_two
        low[0] = grad_two.astype(bf)
        row_sum(layer, B_DOWN, low[0])
        loaded("r1")
        normed = standardize(r1[...])[0] * vector(GAIN_A, layer) + vector(SHIFT_A, layer)
        norm_t[...] = normed.astype(bf).T
        if layer != last:
            sum_plane(last, DN)
            sum_pair(last, Q)
            sum_plane(last, U)
        pair_ready(layer, DN)

        def ffn(c, carry):
            slot = lax.rem(c, 2)

            @pl.when(c + 1 < FF // D)
            def _():
                for copy in stream(layer, c + 1, 1 - slot):
                    copy.start()

            for copy in stream(layer, c, slot):
                copy.wait()
            branch = low[0]
            grad_pre = (dot_t(branch, wd[slot]) * slope[slot].astype(f32)).astype(bf)
            small_a[pl.ds(layer * SMALL + B_UP + c, 1), :] = jnp.sum(grad_pre.astype(f32), axis=0, keepdims=True)
            columns = pl.ds(pl.multiple_of(c * D, 128), D)
            p_d[columns, :] = t_dot(act[slot], branch).astype(bf)
            pair_copy(layer, DN, c).start()
            p_u[:, columns] = dot(norm_t[...], grad_pre).astype(bf)
            gn[...] += dot_t(grad_pre, wu[slot])
            return carry

        lax.fori_loop(0, FF // D, ffn, 0)
        if layer:
            for copy in stream(layer - 1, 0, 0):
                copy.start()
            load("r2", r2_ref.at[layer - 1], r2)
        pair_ready(layer, U)
        for c in range(half):
            pair_copy(layer, U, c).start()

        grad_one, _ = norm_back(gn[...], r1[...], layer, GAIN_A, SHIFT_A)
        gx[...] = grad_one
        if layer == last:
            sent_home(1)
        low[1] = grad_one.astype(bf)
        row_sum(layer, B_OUT, low[1])
        if layer:
            load("r1", r1_ref.at[layer - 1], r1)
        loaded("wo")

        def c_copy(i):
            return remote(gc_send.at[i - 1], gctx.at[layer, me], c_send.at[layer, i], c_recv.at[layer, i], member(i))

        if layer != last:
            for i in range(1, g):
                remote(gc_send.at[i - 1], gctx.at[last, me], c_send.at[last, i], c_recv.at[last, i], member(i)).wait_send()

        def out_back(k, carry):
            b = lax.rem(me + k, g)
            base = b * (3 * HD)
            first = dot_t(low[1], wo[pl.ds(pl.multiple_of(base, 64), 128), :]).astype(bf)
            second = dot_t(low[1], wo[pl.ds(pl.multiple_of(base + 64, 64), 128), :]).astype(bf)
            second = jnp.where(low_lane, jnp.zeros_like(second), second)

            @pl.when(k < g)
            def _():
                gc_send[k - 1, :, 0:128] = first
                gc_send[k - 1, :, 128:256] = second
                c_copy(k).start()

            @pl.when(k == g)
            def _():
                gctx[layer, me, :, 0:128] = first
                gctx[layer, me, :, 128:256] = second

            return carry

        lax.fori_loop(1, g + 1, out_back, 0)
        if layer != last:
            sum_half(last, Q)
            sum_plane(last, O)
        loaded("ctx")
        for grp in range(g):
            base = grp * 3 * HD
            p_o[base : base + 128, :] = t_dot(ctx[grp, :, 0:128], low[1]).astype(bf)
            p_o[base + 128 : base + 192, :] = t_dot(ctx[grp, :, 128:256], low[1])[64:].astype(bf)
        if layer:
            load("wo", fo_ref.at[layer - 1], wo)
            load("ctx", ctx_ref.at[layer - 1], ctx)
        pair_ready(layer, O)
        for c in range(half):
            pair_copy(layer, O, c).start()
        sum_pair(layer, DN)
        sum_pair(layer, U)
        sum_pair(layer, O)
        if layer != last:
            sum_end(last, DN)
            sum_end(last, U)
        sum_half(layer, DN)

        loaded("hd")
        loaded("lse")
        for tile in range(1, 5):
            columns = slice(tile * 128, tile * 128 + 128)
            if tile == 3:
                full = hd[:, columns]
                wide_low = lax.broadcasted_iota(jnp.int32, full.shape, 1) < 64
                hd[:, columns] = jnp.where(wide_low, full, full * live[...])
            else:
                hd[:, columns] = hd[:, columns] * live[...]
        key_t[0:128, :] = hd[:, 128:256].T
        key_t[128:256, :] = hd[:, 512:640].T
        for acc in (acc_k, acc_v, acc_d, acc_e):
            acc[...] = jnp.zeros_like(acc)
        for i in range(1, g):
            c_copy(i).wait_recv()

        def attend(k, carry):
            b = lax.rem(me + k, g)
            block = pl.ds(pl.multiple_of(b * rows, rows), rows)
            q_a = hd[block, 0:128] * bf(HD**-0.5)
            q_d = hd[block, 384:512] * bf(HD**-0.5)
            g_a = gctx[layer, b, :, 0:128]
            g_d = gctx[layer, b, :, 128:256]
            zero = jnp.zeros_like(q_a)
            queries = (jnp.where(low_lane, q_a, zero), jnp.where(low_lane, zero, q_a), jnp.where(low_lane, q_d, zero))
            grads = (jnp.where(low_lane, g_a, zero), jnp.where(low_lane, zero, g_a), g_d)
            turned = []
            for h in range(3):
                keys = slice(512, 640) if h == 2 else slice(128, 256)
                values = slice(384, 512) if h == 2 else slice(256, 384)
                scores = dot_t(hd[:, keys], queries[h])
                prob = jnp.exp(jnp.minimum(scores - lse[h : h + 1, block], 0.0))
                grad_prob = dot_t(hd[:, values], grads[h])
                inner = jnp.sum(grad_prob * prob, axis=0, keepdims=True)
                grad_scores = (prob * (grad_prob - inner)).astype(bf)
                acc_value, acc_key = (acc_d, acc_e) if h == 2 else (acc_v, acc_k)
                acc_value[...] += dot(prob.astype(bf), grads[h])
                acc_key[...] += dot(grad_scores, queries[h])
                turned.append(dot(key_t[h * 64 : h * 64 + 64, :], grad_scores))
            dq_s[block, :] = (jnp.concatenate(turned[:2], axis=0).T * HD**-0.5).astype(bf)
            acc_d[block, :] += jnp.concatenate([turned[2], jnp.zeros_like(turned[2])], axis=0).T * HD**-0.5
            return carry

        lax.fori_loop(1, g + 1, attend, 0)

        def g_copy(i):
            return remote(g_send.at[i - 1], g_in.at[layer, me], g_send_sem.at[layer, i - 1], g_recv_sem.at[layer, i - 1], member(i))

        if layer != last:
            for i in range(1, g):
                remote(g_send.at[i - 1], g_in.at[last, me], g_send_sem.at[last, i - 1], g_recv_sem.at[last, i - 1], member(i)).wait_send()
        for i in list(range(1, g)) + [0]:
            b = lax.rem(me + i, g)
            block = pl.ds(pl.multiple_of(b * rows, rows), rows)
            target = g_send.at[i - 1] if i else g_in.at[layer, me]
            alive = live[block, :].astype(f32)
            target[:, 0:128] = dq_s[block, :]
            target[:, 128:256] = (acc_k[block, :] * alive).astype(bf)
            target[:, 256:384] = (acc_v[block, :] * alive).astype(bf)
            third = acc_d[block, :]
            target[:, 384:512] = jnp.where(low_lane, third, third * alive).astype(bf)
            target[:, 512:640] = (acc_e[block, :] * alive).astype(bf)
            if i:
                g_copy(i).start()
        if layer:
            load("hd", heads_ref.at[layer - 1], hd)
            load("lse", lse_ref.at[layer - 1], lse)
        sum_half(layer, U)
        sum_half(layer, O)
        if layer != last:
            sum_plane(last, Q)
            sum_line(last, DN)
            sum_line(last, U)
            sum_end(last, O)

        loaded("xb")
        loaded("wq")
        norm_t[...] = xb[...].T
        for i in range(g):
            grp = lax.rem(me - i + g, g)
            if i:
                g_copy(i).wait_recv()
            columns = pl.ds(pl.multiple_of(grp * GROUP, 128), GROUP)
            got = g_in[layer, grp]
            gx[...] += dot_t(got, wq[:, columns])
            p_q[:, columns] = dot(norm_t[...], got).astype(bf)
            small_a[pl.ds(layer * SMALL + VECS + grp, 1), 0:GROUP] = jnp.sum(got.astype(f32), axis=0, keepdims=True)
        pair_ready(layer, Q)
        for c in range(half):
            pair_copy(layer, Q, c).start()
        if layer:
            load("xb", xb_ref.at[layer - 1], xb)
            load("wq", fq_ref.at[layer - 1], wq)

    low[0] = gx[...].astype(bf)
    send_home(0)
    a_copy = remote(small_a, land_a, sa_send, sa_recv, partner)
    a_copy.start()
    sum_pair(0, Q)
    sum_plane(0, DN)
    sum_plane(0, U)
    sum_end(last, Q)
    sum_line(last, O)
    pass_on(last, DN)
    pass_on(last, U)
    sum_half(0, Q)
    a_copy.wait()
    small_b[...] = small_a[...] + land_a[...]
    b_copies = [
        remote(small_b, land_b.at[j], sb_send.at[j], sb_recv.at[j], place.on_plane(owner))
        for j, owner in enumerate((place.fx, place.fy, place.fd))
    ]
    for copy in b_copies:
        copy.start()
    sum_plane(0, O)
    sum_end(0, DN)
    came_home(0)
    position = s * rows + lax.broadcasted_iota(jnp.int32, (rows, 1), 0)
    length = len_ref[0]
    small_c[small_a.shape[0] :, :] = dot(selection(place, rows, length).astype(bf), home[0])
    for copy in b_copies:
        copy.wait()
    small_c[: small_a.shape[0], :] = small_b[...] + land_b[0] + land_b[1] + land_b[2]
    c_copies = [
        remote(small_c, land_c.at[i - 1], sc_send.at[i - 1], sc_recv.at[i - 1], place.at(f, lax.rem(s + i, g))) for i in range(1, g)
    ]
    for copy in c_copies:
        copy.start()
    sum_end(0, U)
    sum_line(last, Q)
    pass_on(last, O)
    gn[...] = jnp.where(jnp.logical_and(position >= MEM, position < length + MEM), home[0].astype(f32), 0.0)
    tokens_copy = pltpu.make_async_copy(gn, tokens_ref, store_sem.at[0])
    tokens_copy.start()
    came_home(1)
    gx[...] = jnp.where(position < length + 2 * MEM, home[1].astype(f32), 0.0)
    result_copy = pltpu.make_async_copy(gx, result_ref, store_sem.at[1])
    result_copy.start()
    sum_line(0, DN)
    sum_plane(0, Q)
    sum_end(0, O)
    sum_line(0, U)
    pass_on(last, Q)
    pass_on(0, DN)
    for copy in c_copies:
        copy.wait()
    total = small_c[...]
    for i in range(1, g):
        total = total + land_c[i - 1]
    small_c[...] = total
    memory_ref[0] = total[small_a.shape[0] : small_a.shape[0] + 2 * MEM]
    width = D // n
    from_lane = lax.broadcasted_iota(jnp.int32, (D, 128), 0)
    to_lane = lax.broadcasted_iota(jnp.int32, (D, 128), 1)
    pick = jnp.where(jnp.logical_and(from_lane == to_lane + f * width, to_lane < width), 1.0, 0.0)
    mine = jnp.dot(total[: small_a.shape[0]], pick, precision=lax.Precision.HIGHEST, preferred_element_type=f32)
    for layer in range(LAYERS):
        base = layer * SMALL
        for ref, kind in ((bout_out, B_OUT), (ga_out, GAIN_A), (sa_out, SHIFT_A), (bdown_out, B_DOWN), (gf_out, GAIN_F), (sf_out, SHIFT_F)):
            ref[layer : layer + 1, :] = mine[base + kind : base + kind + 1, 0:width]
        bup_out[layer : layer + 1, :] = small_c[pl.ds(base + B_UP + f // 2, 1), aligned(core * 384, 384, 128)]
        group_row = small_c[pl.ds(base + VECS + lax.rem(f, g), 1), :]
        turned = pltpu.roll(jnp.broadcast_to(group_row[:, 384:512], (8, 128)), 64, 1)[0:1]
        queries = f < g
        bqv_out[layer : layer + 1, 0:128] = jnp.where(queries, group_row[:, 0:128], group_row[:, 256:384])
        bqv_out[layer : layer + 1, 128:192] = jnp.where(queries, group_row[:, 384:512], turned)[:, 0:64]
    sum_end(0, Q)
    sum_line(0, O)
    pass_on(0, U)
    pass_on(0, O)
    sum_line(0, Q)
    pass_on(0, Q)

    for i in range(1, g):
        remote(gc_send.at[i - 1], gctx.at[0, me], c_send.at[0, i], c_recv.at[0, i], member(i)).wait_send()
        remote(g_send.at[i - 1], g_in.at[0, me], g_send_sem.at[0, i - 1], g_recv_sem.at[0, i - 1], member(i)).wait_send()
    sent_home(0)

    @pl.when(inner)
    def _():
        for layer in range(LAYERS):
            for m in range(4):
                inner_copy(layer, m).wait_send()
                out_across(layer, m).wait_send()
                out_end(layer, m).wait_send()
                out_pass(layer, m).wait_send()
                out_local(layer, m).wait()

    @pl.when(outer)
    def _():
        for layer in range(LAYERS):
            for m in range(4):
                end_copy(layer, m).wait_send()
                out_end(layer, m).wait_recv()
                out_pass(layer, m).wait_recv()

    tokens_copy.wait()
    result_copy.wait()


def run_backward(n, g, lengths, mask, vec, cot, y, fq, fo, fu, fd, stored):
    rows, span = y.shape[0], y.shape[0] * g
    any_spec = pl.BlockSpec(memory_space=pl.ANY)
    vmem = pl.BlockSpec(memory_space=pltpu.VMEM)
    bf, f32 = jnp.bfloat16, jnp.float32
    half = n // 2
    wide = g * GROUP
    dims = ((D, wide), (D, D), (D, FF), (FF, D))
    small = SMALL * LAYERS
    width = D // n
    shapes = [((rows, D), f32, any_spec), ((rows, D), f32, any_spec), ((1, 2 * MEM, D), f32, vmem), ((LAYERS, 2 * width), f32, vmem)]
    shapes += [((LAYERS, width), f32, vmem)] * 3 + [((LAYERS, FF // n), f32, vmem)] + [((LAYERS, width), f32, vmem)] * 3
    shapes += [((LAYERS, a // n, b), bf, any_spec) for a, b in dims]
    dma, regular = pltpu.SemaphoreType.DMA, pltpu.SemaphoreType.REGULAR
    scratch = [
        pltpu.VMEM((D, wide), bf), pltpu.VMEM((D, D), bf), pltpu.VMEM((2, D, D), bf), pltpu.VMEM((2, D, D), bf),
        pltpu.VMEM((2, rows, D), bf), pltpu.VMEM((2, rows, D), bf), pltpu.VMEM((rows, D), bf), pltpu.VMEM((span, GROUP), bf),
        pltpu.VMEM((8, span), f32), pltpu.VMEM((g, rows, CTX), bf), pltpu.VMEM((rows, D), f32), pltpu.VMEM((rows, D), f32),
    ]
    scratch += [pltpu.VMEM(shape, bf) for shape in dims]
    scratch += [pltpu.VMEM((half, a // n, b), bf) for a, b in dims]
    scratch += [pltpu.VMEM((2, a // n // 2, b), bf) for a, b in dims]
    scratch += [pltpu.VMEM((2, a // n, b), bf) for a, b in dims]
    scratch += [pltpu.VMEM((LAYERS, a // n, b), bf) for a, b in dims]
    scratch += [pltpu.VMEM((a // n, b), bf) for a, b in dims]
    scratch += [pltpu.VMEM((a // n // 2, b), bf) for a, b in dims]
    scratch += [
        pltpu.VMEM((rows, D), f32), pltpu.VMEM((rows, D), f32), pltpu.VMEM((D, rows), bf), pltpu.VMEM((2, rows, D), bf),
        pltpu.VMEM((span, 128), bf), pltpu.VMEM((2, rows, D), bf),
        pltpu.VMEM((g - 1, rows, CTX), bf), pltpu.VMEM((LAYERS, g, rows, CTX), bf), pltpu.VMEM((256, span), bf),
        pltpu.VMEM((span, 128), f32), pltpu.VMEM((span, 128), f32), pltpu.VMEM((span, 128), f32), pltpu.VMEM((span, 128), f32),
        pltpu.VMEM((span, 128), bf), pltpu.VMEM((g - 1, rows, GROUP), bf), pltpu.VMEM((LAYERS, g, rows, GROUP), bf),
        pltpu.VMEM((small, D), f32), pltpu.VMEM((small, D), f32), pltpu.VMEM((small + MEM_ROWS, D), f32),
        pltpu.VMEM((small, D), f32), pltpu.VMEM((3, small, D), f32), pltpu.VMEM((g - 1, small + MEM_ROWS, D), f32),
        dma((10,)), dma((4, 2)), dma((LAYERS, 4, half)), dma((LAYERS, 4, half)), dma((LAYERS, 4, 2)), dma((LAYERS, 4, 2)),
        dma((LAYERS, 4, 2)), dma((LAYERS, 4, 2)), dma((LAYERS, 4, 2)), dma((LAYERS, 4, 2)), dma((LAYERS, 4, 3)), dma((LAYERS, 4, 3)), dma((LAYERS, 4)),
        dma((LAYERS, g)), dma((LAYERS, g)), dma((LAYERS, g - 1)), dma((LAYERS, g - 1)), dma(()), dma(()),
        dma((3,)), dma((3,)), dma((g - 1,)), dma((g - 1,)), dma((2,)), dma((2,)), dma((2,)),
        regular((4,)), regular((4, 2)), regular((4, 2)), regular((4, 2)),
    ]
    return pl.pallas_call(
        functools.partial(backward_kernel, n, g),
        name="backward",
        out_shape=[jax.ShapeDtypeStruct(a, b) for a, b, _ in shapes],
        in_specs=[pl.BlockSpec(memory_space=pltpu.SMEM)] + [vmem] * 2 + [any_spec] * 14,
        out_specs=[c for _, _, c in shapes],
        scratch_shapes=scratch,
        compiler_params=pltpu.CompilerParams(
            collective_id=1, has_side_effects=True, vmem_limit_bytes=64 * 1024 * 1024 - 65536
        ),
    )(lengths, mask, vec, cot, y, fq, fo, fu, fd, *stored)


def kernel_body(
    tokens, memory, lengths, w_qkv, b_qv, w_out, b_out, gain_attn, shift_attn, w_up, b_up, w_down, b_down, gain_ffn, shift_ffn, cotangent,
):
    n, g = lax.axis_size("fsdp"), lax.axis_size("seq")
    sq = group_columns(w_qkv, g).reshape(LAYERS, w_qkv.shape[1], g * GROUP)
    vectors = (b_qv, b_out, gain_attn, shift_attn, b_up, b_down, gain_ffn, shift_ffn)
    y, cot, mask, vec, fq, fo, fu, fd, *stored = run_forward(n, g, lengths, tokens, memory, vectors, cotangent, sq, w_out, w_up, w_down)
    result, grad_tokens, grad_memory, bqv, bout, ga, sa, bup, bdown, gf, sf, oq, oo, ou, od = run_backward(
        n, g, lengths, mask, vec, cot, y, fq, fo, fu, fd, stored)
    f32 = jnp.float32
    oq = ungroup_columns(oq.reshape(LAYERS, D // n, g, GROUP)).astype(f32)
    return (result, grad_tokens, grad_memory, oq, bqv, oo.astype(f32), bout, ga, sa, ou.astype(f32), bup, od.astype(f32), bdown, gf, sf)


def pick_body(mesh):
    return kernel_body if mesh.shape["fsdp"] == 8 and mesh.shape["seq"] == 4 else plain_body


def solution(mesh):
    in_specs = (
        P(("fsdp", "seq"), None),
        P("fsdp", None, None),
        P("fsdp"),
        P(None, "fsdp", None),
        P(None, "fsdp"),
        P(None, "fsdp", None),
        P(None, "fsdp"),
        P(None, "fsdp"),
        P(None, "fsdp"),
        P(None, "fsdp", None),
        P(None, "fsdp"),
        P(None, "fsdp", None),
        P(None, "fsdp"),
        P(None, "fsdp"),
        P(None, "fsdp"),
        P(("fsdp", "seq"), None),
    )
    out_specs = (
        P(("fsdp", "seq"), None),
        P(("fsdp", "seq"), None),
        P("fsdp", None, None),
        P(None, "fsdp", None),
        P(None, "fsdp"),
        P(None, "fsdp", None),
        P(None, "fsdp"),
        P(None, "fsdp"),
        P(None, "fsdp"),
        P(None, "fsdp", None),
        P(None, "fsdp"),
        P(None, "fsdp", None),
        P(None, "fsdp"),
        P(None, "fsdp"),
        P(None, "fsdp"),
    )
    return jax.shard_map(pick_body(mesh), mesh=mesh, in_specs=in_specs, out_specs=out_specs, check_vma=False)
```

```python
import functools
import math

import jax
import jax.numpy as jnp
from jax import lax
from jax.experimental import pallas as pl
from jax.experimental.pallas import tpu as pltpu
from jax.sharding import PartitionSpec as P

D = 768
HEADS = 12
HD = 64
FF = 3072
MEM = 10
LAYERS = 2
GROUP = 640
CTX = 256
MEM_ROWS = 32
SMALL = 16
MESH = pl.DeviceIdType.MESH

norm_eps = 1e-12
masked_score = -1e30

B_OUT, GAIN_A, SHIFT_A, B_UP, B_DOWN, GAIN_F, SHIFT_F, VECS = 0, 1, 2, 3, 7, 8, 9, 10
WIDE = (B_OUT, GAIN_A, SHIFT_A, B_DOWN, GAIN_F, SHIFT_F)


def dot(a, b):
    return jnp.dot(a, b, preferred_element_type=jnp.float32)


def dot_t(a, b):
    return lax.dot_general(a, b, (((1,), (1,)), ((), ())), preferred_element_type=jnp.float32)


def t_dot(a, b):
    return lax.dot_general(a, b, (((0,), (0,)), ((), ())), preferred_element_type=jnp.float32)


def standardize(values):
    row_mean = jnp.mean(values, axis=-1, keepdims=True)
    centred = values - row_mean
    variance = jnp.mean(centred * centred, axis=-1, keepdims=True)
    scale = lax.rsqrt(variance + norm_eps)
    return centred * scale, scale


SHARED = ()


class Place:
    def __init__(self, n, g):
        self.n, self.g = n, g
        self.f, self.s = f, s = lax.axis_index("fsdp"), lax.axis_index("seq")
        self.core = lax.rem(f, 2)
        chip = f // 2
        self.partner = f + 1 - 2 * self.core
        self.fx = f + 2 - 4 * lax.rem(chip, 2)
        self.fy = lax.rem(f + n // 2, n)
        self.fd = lax.rem(self.fx + n // 2, n)
        self.me = 2 * lax.rem(s, 2) + self.core
        away_f, away_s = f - self.core + lax.rem(s, 2), 2 * self.core + s // 2
        self.away = self.at(away_f, away_s)
        self.back = self.at(f - self.core + s // 2, 2 * lax.rem(s, 2) + self.core)
        self.away_home = self.back
        self.stays = jnp.logical_and(away_f == f, away_s == s)

    def at(self, f, s):
        return {"fsdp": f, "seq": s}

    def on_plane(self, f):
        return self.at(f, self.s)

    def member(self, m):
        return self.at(self.f - self.core + lax.rem(m, 2), self.s - lax.rem(self.s, 2) + m // 2)

    def barrier(self):
        barrier = pltpu.get_barrier_semaphore()
        count = self.n * self.g
        here = self.f * self.g + self.s
        for j in range(1, count):
            other = lax.rem(here + j, count)
            pl.semaphore_signal(barrier, 1, device_id=self.at(other // self.g, lax.rem(other, self.g)), device_id_type=MESH)
        pl.semaphore_wait(barrier, count - 1)


def remote(src, dst, send_sem, recv_sem, device):
    return pltpu.make_async_remote_copy(
        src_ref=src, dst_ref=dst, send_sem=send_sem, recv_sem=recv_sem, device_id=device, device_id_type=MESH)


def aligned(start, size, unit):
    return pl.ds(pl.multiple_of(start, unit), size)


def swap_halves(values):
    return pltpu.roll(values, 64, 1)


def group_tiles(take, give, low):
    for pair in range(HEADS // 6):
        (q0, q1, q2), (k0, k1, k2), (v0, v1, v2) = ([take(kind, 3 * pair + t) for t in range(3)] for kind in range(3))
        first, second = 2 * pair, 2 * pair + 1
        for tile, (a, b, c) in enumerate(((q0, q1, q2), (k0, k1, k2), (v0, v1, v2))):
            give(first, tile, a)
            give(second, tile, jnp.where(low, swap_halves(b), swap_halves(c)))
        give(first, 3, jnp.where(low, q1, swap_halves(v1)))
        give(second, 3, jnp.where(low, swap_halves(q2), v2))
        give(first, 4, jnp.where(low, k1, 0.0))
        give(second, 4, jnp.where(low, swap_halves(k2), 0.0))


def ungroup_tiles(take, give, low):
    for pair in range(HEADS // 6):
        first, second = 2 * pair, 2 * pair + 1
        d0, d1, e0, e1 = take(first, 3), take(second, 3), take(first, 4), take(second, 4)
        lows = (d0, e0, swap_halves(d0))
        highs = (swap_halves(d1), swap_halves(e1), d1)
        for kind in range(3):
            turned = swap_halves(take(second, kind))
            give(kind, 3 * pair, take(first, kind))
            give(kind, 3 * pair + 1, jnp.where(low, lows[kind], turned))
            give(kind, 3 * pair + 2, jnp.where(low, turned, highs[kind]))


def selection(place, rows, length):
    slot = lax.broadcasted_iota(jnp.int32, (MEM_ROWS, rows), 0)
    position = place.s * rows + lax.broadcasted_iota(jnp.int32, (MEM_ROWS, rows), 1)
    target = jnp.where(slot < MEM, slot, length + slot)
    return jnp.where(jnp.logical_and(position == target, slot < 2 * MEM), 1.0, 0.0)


def forward_kernel(n, g, *refs):
    (
        len_ref, tok_ref, mem_ref, bqv_ref, bout_ref, ga_ref, sa_ref, bup_ref, bdown_ref, gf_ref, sf_ref, cot_ref, raw_ref, so_ref, su_ref, sd_ref,
        y_ref, cot_out, mask_in, vec, fq_ref, fo_ref, fu_ref, fd_ref, xb_out, heads_out, lse_out, ctx_out, r1_out, slope_out, act_out, r2_out,
        wq, wo, wu, wd, x_s, xb, heads, lse, ctx, r1, slope, act, r2, acc_s, nb_s, ctx_send,
        pack, packs, cat, bqkv, bup, mem_s, sq, x_out, x_in, mask_s, cot_s,
        w_send, w_recv, c_send, c_recv, own_sem, x_send, x_recv, qw_send, qw_recv, k_send_sem, k_recv_sem, save_sem,
        p_send, p_recv, r_send, r_recv, r_local,
    ) = refs
    place = Place(n, g)
    f, s, me = place.f, place.s, place.me
    rows = tok_ref.shape[0]
    span = rows * g
    bf, f32 = jnp.bfloat16, jnp.float32
    lands = (wq, wo, wu, wd)
    shards = (sq, so_ref, su_ref, sd_ref)
    fulls = (fq_ref, fo_ref, fu_ref, fd_ref)
    shard = D // n
    odd = lax.rem(s, 2)

    def spot(m, owner, part=None):
        layer, kind = divmod(m, 4)
        depth = shards[kind].shape[1]
        if part is None:
            return lands[kind].at[layer, aligned(owner * depth, depth, 32)]
        size = depth // 4 if m in SHARED else depth // 2
        return lands[kind].at[layer, aligned(owner * depth + part * size, size, 8)]

    def direct(m, way):
        layer, kind = divmod(m, 4)
        return remote(shards[kind].at[layer], spot(m, f), w_send.at[m, way], w_recv.at[m, way], place.on_plane((place.fx, place.fy)[way]))

    def relay(m, way):
        owner, target = ((place.fy, place.fx), (place.fx, place.fy))[way]
        quarter = spot(m, owner, 2 * way + odd if m in SHARED else way)
        return remote(quarter, quarter, w_send.at[m, 2 + way], w_recv.at[m, 2 + way], place.on_plane(target))

    def share(m, way):
        quarter = spot(m, place.fd, 2 * way + odd)
        return remote(quarter, quarter, w_send.at[m, 4 + way], w_recv.at[m, 4 + way], place.at(f, s + 1 - 2 * odd))

    def to_core(m, k):
        if k < 3:
            source = (spot(m, f), spot(m, place.fx), spot(m, place.fy))[k]
        else:
            source = spot(m, place.fd, (odd, 2 + odd, 1 - odd, 3 - odd)[k - 3] if m in SHARED else k - 3)
        return remote(source, source, c_send.at[m, k], c_recv.at[m, k], place.on_plane(place.partner))

    def own_copy(m):
        layer, kind = divmod(m, 4)
        return pltpu.make_async_copy(shards[kind].at[layer], spot(m, f), own_sem.at[m])

    def save_full(m):
        layer, kind = divmod(m, 4)
        return pltpu.make_async_copy(lands[kind].at[layer], fulls[kind].at[layer], own_sem.at[m])

    def launch(m):
        if m < 4 * LAYERS:
            for way in range(2):
                direct(m, way).start()

    def arrived(m):
        for way in range(2):
            direct(m, way).wait_recv()
        for way in range(2):
            relay(m, way).start()
        for k in (1, 2):
            to_core(m, k).start()

    def complete(m):
        for way in range(2):
            relay(m, way).wait_recv()
            if m in SHARED:
                share(m, way).start()
            to_core(m, 3 + way).start()

    def need(m):
        if m in SHARED:
            for way in range(2):
                share(m, way).wait_recv()
                to_core(m, 5 + way).start()
        for k in range(7 if m in SHARED else 5):
            to_core(m, k).wait_recv()
        save_full(m).start()

    def head_columns(core):
        return aligned((2 * odd + core) * GROUP, GROUP, 128)

    def q_rows(layer, owner):
        return wq.at[layer, aligned(owner * shard, shard, 32)]

    def q_direct(layer, way, other):
        core = 1 - place.core if other else place.core
        device = place.on_plane((place.fx, place.fy)[way] - place.core + core)
        return remote(sq.at[layer, :, head_columns(core)], q_rows(layer, f), qw_send.at[layer, way, other], qw_recv.at[layer, way, other], device)

    def q_relay(layer, way):
        owner, target = ((place.fy, place.fx), (place.fx, place.fy))[way]
        block = q_rows(layer, owner - place.core + way)
        return remote(block, block, qw_send.at[layer, 2, way], qw_recv.at[layer, 2, way], place.on_plane(target))

    def q_core(layer):
        return remote(
            sq.at[layer, :, head_columns(1 - place.core)], q_rows(layer, f), qw_send.at[layer, 3, 0], qw_recv.at[layer, 3, 0], place.on_plane(place.partner))

    def q_own(layer):
        return pltpu.make_async_copy(sq.at[layer, :, head_columns(place.core)], q_rows(layer, f), own_sem.at[4 * layer])

    def q_launch(layer):
        for way in range(2):
            for other in range(2):
                q_direct(layer, way, other).start()
        q_core(layer).start()
        q_own(layer).start()

    def q_arrived(layer):
        for way in range(2):
            for other in range(2):
                q_direct(layer, way, other).wait_recv()
        for way in range(2):
            q_relay(layer, way).start()

    def q_need(layer):
        for way in range(2):
            q_relay(layer, way).wait_recv()
        q_core(layer).wait_recv()
        q_own(layer).wait()
        save_full(4 * layer).start()

    saves = []

    def save(src, dst):
        copy = pltpu.make_async_copy(src, dst, save_sem.at[len(saves)])
        copy.start()
        saves.append(copy)

    length = len_ref[0]
    position = s * rows + lax.broadcasted_iota(jnp.int32, (rows, 1), 0)
    mem_s[...] = jnp.zeros_like(mem_s)
    mem_s[0 : 2 * MEM, :] = mem_ref[0]
    chosen = t_dot(selection(place, rows, length).astype(bf), mem_s[...])
    is_token = jnp.logical_and(position >= MEM, position < length + MEM)
    x_out[...] = (jnp.where(is_token, tok_ref[...].astype(f32), 0.0) + chosen).astype(bf)
    mask_s[...] = jnp.where(lax.broadcasted_iota(jnp.int32, (8, span), 1) < length + 2 * MEM, 0.0, masked_score)

    def move(k, device):
        source, target = ((x_out, x_in), (mask_s, mask_in), (cot_s, cot_out))[k]
        return remote(source, target, r_send.at[k], r_recv.at[k], device)

    place.barrier()

    @pl.when(jnp.logical_not(place.stays))
    def _():
        for k in range(2):
            move(k, place.away).start()

    low_lane = lax.broadcasted_iota(jnp.int32, (D // n, 128), 1) < 64

    def regroup(layer):
        def take(kind, tile):
            at = kind * D + tile * 128
            return raw_ref[layer, :, at : at + 128].astype(f32)

        def give(group, tile, values):
            at = group * GROUP + tile * 128
            sq[layer, :, at : at + 128] = values.astype(bf)

        group_tiles(take, give, low_lane)

    regroup(0)
    q_launch(0)
    launch(1)
    regroup(1)

    pack[...] = jnp.zeros_like(pack)
    for v, ref in enumerate((bout_ref, ga_ref, sa_ref, bdown_ref, gf_ref, sf_ref)):
        pack[2 * v : 2 * v + 2, 0 : D // n] = ref[...].astype(f32)
    for t in range(2):
        width = min(128, 2 * D // n - 128 * t)
        pack[16 + 2 * t : 18 + 2 * t, 0:width] = bqv_ref[:, 128 * t : 128 * t + width].astype(f32)
    for t in range(3):
        pack[20 + 2 * t : 22 + 2 * t, :] = bup_ref[:, 128 * t : 128 * t + 128].astype(f32)
    packs[f] = pack[...]

    def p_copy(j):
        return remote(pack, packs.at[f], p_send.at[j - 1], p_recv.at[j - 1], place.on_plane(lax.rem(f + j, n)))

    for j in range(1, n):
        p_copy(j).start()
    plain = [m for m in range(4 * LAYERS) if m % 4]
    for m in plain:
        own_copy(m).start()

    cot_s[...] = jnp.where(position < length + 2 * MEM, cot_ref[...], 0.0).astype(bf)

    @pl.when(jnp.logical_not(place.stays))
    def _():
        move(2, place.away).start()

    @pl.when(place.stays)
    def _():
        x_in[...] = x_out[...]
        mask_in[...] = mask_s[...]
        pltpu.make_async_copy(cot_s, cot_out, r_local).start()

    for m in plain:
        own_copy(m).wait()
        to_core(m, 0).start()
    q_arrived(0)
    launch(2)
    launch(3)

    for j in range(1, n):
        owner = lax.rem(f - j + n, n)
        remote(pack, packs.at[owner], p_send.at[j - 1], p_recv.at[j - 1], place.on_plane(owner)).wait_recv()
    for j in range(n):
        cat[:, 128 * j : 128 * j + 128] = packs[j, 0:16, :].astype(bf)
        for layer in range(LAYERS):
            for t in range(3):
                at = (j % 2) * 384 + 128 * t
                row = layer * (FF // D) + j // 2
                bup[row : row + 1, at : at + 128] = packs[j, 20 + 2 * t + layer : 21 + 2 * t + layer, :]
    low_row = lax.broadcasted_iota(jnp.int32, (1, 128), 1) < 64
    for layer in range(LAYERS):
        for grp in range(g):
            row = slice(layer * g + grp, layer * g + grp + 1)
            bqkv[row, :] = jnp.zeros((1, GROUP), f32)
            bqkv[row, 0:128] = packs[grp, 16 + layer : 17 + layer, :]
            bqkv[row, 256:384] = packs[g + grp, 16 + layer : 17 + layer, :]
            turned = pltpu.roll(packs[g + grp, 16:24, :], 64, 1)[2 + layer : 3 + layer]
            bqkv[row, 384:512] = jnp.where(low_row, packs[grp, 18 + layer : 19 + layer, :], turned)
    from_lane = lax.broadcasted_iota(jnp.int32, (128, D), 0)
    to_lane = lax.broadcasted_iota(jnp.int32, (128, D), 1)
    wide = jnp.zeros((16, D), f32)
    for j in range(n):
        spread = jnp.logical_and(to_lane == from_lane + (D // n) * j, from_lane < D // n)
        wide = wide + dot(cat[:, 128 * j : 128 * j + 128], jnp.where(spread, 1.0, 0.0).astype(bf))
    vec[...] = wide

    def vector(kind, layer):
        row = 2 * WIDE.index(kind) + layer
        return vec[row : row + 1, :]

    @pl.when(jnp.logical_not(place.stays))
    def _():
        for k in range(2):
            move(k, place.back).wait_recv()

    lane = lax.broadcasted_iota(jnp.int32, (rows, 128), 1)
    x_s[...] = x_in[...].astype(f32)

    x_copies = []
    for layer in range(LAYERS):
        m0 = 4 * layer
        def x_rows(quarter):
            return xb.at[layer, aligned(quarter * rows, rows, rows)]

        across, aside = lax.rem(me + 2, g), me + 1 - 2 * place.core
        partner = place.on_plane(place.partner)
        to_across = remote(x_rows(me), x_rows(me), x_send.at[layer, 0], x_recv.at[layer, 0], place.member(across))
        to_aside = remote(x_rows(me), x_rows(me), x_send.at[layer, 1], x_recv.at[layer, 1], partner)
        pass_aside = remote(x_rows(across), x_rows(across), x_send.at[layer, 2], x_recv.at[layer, 2], partner)
        xb[layer, aligned(me * rows, rows, rows), :] = x_s[...].astype(bf)
        to_across.start()
        to_aside.start()
        x_copies.extend([to_across, to_aside, pass_aside])
        q_need(layer)

        def project(quarter):
            block = aligned(quarter * rows, rows, rows)
            heads[layer, block, :] = (dot(xb[layer, block, :], wq[layer]) + bqkv[pl.ds(layer * g + me, 1), :]).astype(bf)

        project(me)
        to_aside.wait_recv()
        project(aside)
        to_across.wait_recv()
        pass_aside.start()
        project(across)
        pass_aside.wait_recv()
        project(lax.rem(aside + 2, g))
        save(xb.at[layer], xb_out.at[layer])
        arrived(m0 + 1)
        if layer == 0:
            arrived(m0 + 2)
            q_launch(1)
            complete(m0 + 1)
        else:
            complete(m0 + 1)
            arrived(m0 + 2)
        save(heads.at[layer], heads_out.at[layer])

        def c_copy(i, b):
            return remote(ctx_send.at[layer, i], ctx.at[layer, me], k_send_sem.at[layer, i], k_recv_sem.at[layer, i], place.member(b))

        def attend(i, carry):
            b = lax.rem(me + i, g)
            block = aligned(b * rows, rows, rows)
            q_a = heads[layer, block, 0:128] * bf(HD**-0.5)
            q_d = heads[layer, block, 384:512] * bf(HD**-0.5)
            zero = jnp.zeros_like(q_a)
            outs, logs = [], []
            for h in range(3):
                if h == 2:
                    scores = dot_t(q_d, heads[layer, :, 512:640])
                else:
                    part = jnp.where(lane < 64, q_a, zero) if h == 0 else jnp.where(lane < 64, zero, q_a)
                    scores = dot_t(part, heads[layer, :, 128:256])
                scores = scores + mask_in[0:1, :]
                top = jnp.max(scores, axis=-1, keepdims=True)
                exponent = jnp.exp(scores - top)
                total = jnp.sum(exponent, axis=-1, keepdims=True)
                values = heads[layer, :, 384:512] if h == 2 else heads[layer, :, 256:384]
                outs.append(dot(exponent.astype(bf), values) * (1.0 / total))
                logs.append(top + jnp.log(total))
            table = jnp.where(lane == 0, logs[0], jnp.where(lane == 1, logs[1], logs[2]))
            lse[layer, :, block] = table.T[0:8]
            first = jnp.where(lane < 64, outs[0], outs[1]).astype(bf)
            second = jnp.where(lane < 64, 0.0, outs[2]).astype(bf)

            @pl.when(i < g)
            def _():
                ctx_send[layer, i, :, 0:128] = first
                ctx_send[layer, i, :, 128:256] = second
                c_copy(i, b).start()

            @pl.when(i == g)
            def _():
                ctx[layer, me, :, 0:128] = first
                ctx[layer, me, :, 128:256] = second

            return carry

        lax.fori_loop(1, g + 1, attend, 0)
        save(lse.at[layer], lse_out.at[layer])
        if layer == 0:
            arrived(m0 + 3)
            launch(m0 + 5)
            launch(m0 + 6)
        else:
            arrived(m0 + 3)
        need(m0 + 1)
        for i in range(1, g):
            origin = lax.rem(me - i + g, g)
            remote(ctx_send.at[layer, i], ctx.at[layer, origin], k_send_sem.at[layer, i], k_recv_sem.at[layer, i], place.member(origin)).wait_recv()
        save(ctx.at[layer], ctx_out.at[layer])

        total = x_s[...] + vector(B_OUT, layer)
        for grp in range(g):
            base = grp * 3 * HD
            total = total + dot(ctx[layer, grp, :, 0:128], wo[layer, base : base + 128, :])
            total = total + dot(ctx[layer, grp, :, 128:256], wo[layer, base + 64 : base + 192, :])
        r1[layer] = total
        save(r1.at[layer], r1_out.at[layer])
        normed = standardize(total)[0] * vector(GAIN_A, layer) + vector(SHIFT_A, layer)
        nb_s[...] = normed.astype(bf)
        acc_s[...] = normed + vector(B_DOWN, layer)
        complete(m0 + 2)
        complete(m0 + 3)
        if layer == 0:
            q_arrived(1)
            launch(m0 + 7)
        need(m0 + 2)
        need(m0 + 3)

        def ffn(c, carry):
            columns = aligned(c * D, D, 128)
            up = dot(nb_s[...], wu[layer, :, columns]) + bup[pl.ds(layer * (FF // D) + c, 1), :]
            cdf = 0.5 * lax.erf(up * (0.5**0.5)) + 0.5
            slope[layer, :, columns] = (cdf + up * jnp.exp(-0.5 * up * up) * (0.5 / math.pi) ** 0.5).astype(bf)
            active = (up * cdf).astype(bf)
            act[layer, :, columns] = active
            acc_s[...] += dot(active, wd[layer, columns, :])
            return carry

        lax.fori_loop(0, FF // D, ffn, 0)
        save(slope.at[layer], slope_out.at[layer])
        save(act.at[layer], act_out.at[layer])
        r2[layer] = acc_s[...]
        save(r2.at[layer], r2_out.at[layer])
        x_s[...] = standardize(acc_s[...])[0] * vector(GAIN_F, layer) + vector(SHIFT_F, layer)
    y_ref[...] = x_s[...]

    for m in plain:
        for way in range(2):
            direct(m, way).wait_send()
            relay(m, way).wait_send()
            if m in SHARED:
                share(m, way).wait_send()
        for k in range(7 if m in SHARED else 5):
            to_core(m, k).wait_send()
        save_full(m).wait()
    for layer in range(LAYERS):
        for way in range(2):
            for other in range(2):
                q_direct(layer, way, other).wait_send()
            q_relay(layer, way).wait_send()
        q_core(layer).wait_send()
        save_full(4 * layer).wait()
    for copy in x_copies:
        copy.wait_send()
    for j in range(1, n):
        p_copy(j).wait_send()
    for layer in range(LAYERS):
        for i in range(1, g):
            remote(ctx_send.at[layer, i], ctx.at[layer, me], k_send_sem.at[layer, i], k_recv_sem.at[layer, i], place.member(lax.rem(me + i, g))).wait_send()
    for copy in saves:
        copy.wait()

    @pl.when(jnp.logical_not(place.stays))
    def _():
        for k in range(3):
            move(k, place.away).wait_send()
        move(2, place.back).wait_recv()

    @pl.when(place.stays)
    def _():
        pltpu.make_async_copy(cot_s, cot_out, r_local).wait()


def run_forward(n, g, lengths, tokens, memory, vectors, cotangent, sq, so, su, sd):
    rows, span = tokens.shape[0], tokens.shape[0] * g
    any_spec = pl.BlockSpec(memory_space=pl.ANY)
    vmem = pl.BlockSpec(memory_space=pltpu.VMEM)
    bf, f32 = jnp.bfloat16, jnp.float32
    shapes = [
        ((rows, D), f32, vmem),
        ((rows, D), bf, any_spec),
        ((8, span), f32, vmem),
        ((16, D), f32, vmem),
        ((LAYERS, D, GROUP), bf, any_spec),
        ((LAYERS, D, D), bf, any_spec),
        ((LAYERS, D, FF), bf, any_spec),
        ((LAYERS, FF, D), bf, any_spec),
        ((LAYERS, span, D), bf, any_spec),
        ((LAYERS, span, GROUP), bf, any_spec),
        ((LAYERS, 8, span), f32, any_spec),
        ((LAYERS, g, rows, CTX), bf, any_spec),
        ((LAYERS, rows, D), f32, any_spec),
        ((LAYERS, rows, FF), bf, any_spec),
        ((LAYERS, rows, FF), bf, any_spec),
        ((LAYERS, rows, D), f32, any_spec),
    ]
    dma = pltpu.SemaphoreType.DMA
    return pl.pallas_call(
        functools.partial(forward_kernel, n, g),
        name="forward",
        out_shape=[jax.ShapeDtypeStruct(a, b) for a, b, _ in shapes],
        in_specs=[pl.BlockSpec(memory_space=pltpu.SMEM)] + [vmem] * 12 + [any_spec] * 3,
        out_specs=[c for _, _, c in shapes],
        scratch_shapes=[
            pltpu.VMEM((LAYERS, D, GROUP), bf),
            pltpu.VMEM((LAYERS, D, D), bf),
            pltpu.VMEM((LAYERS, D, FF), bf),
            pltpu.VMEM((LAYERS, FF, D), bf),
            pltpu.VMEM((rows, D), f32),
            pltpu.VMEM((LAYERS, span, D), bf),
            pltpu.VMEM((LAYERS, span, GROUP), bf),
            pltpu.VMEM((LAYERS, 8, span), f32),
            pltpu.VMEM((LAYERS, g, rows, CTX), bf),
            pltpu.VMEM((LAYERS, rows, D), f32),
            pltpu.VMEM((LAYERS, rows, FF), bf),
            pltpu.VMEM((LAYERS, rows, FF), bf),
            pltpu.VMEM((LAYERS, rows, D), f32),
            pltpu.VMEM((rows, D), f32),
            pltpu.VMEM((rows, D), bf),
            pltpu.VMEM((LAYERS, g, rows, CTX), bf),
            pltpu.VMEM((32, 128), f32),
            pltpu.VMEM((n, 32, 128), f32),
            pltpu.VMEM((16, n * 128), bf),
            pltpu.VMEM((LAYERS * g, GROUP), f32),
            pltpu.VMEM((LAYERS * (FF // D), D), f32),
            pltpu.VMEM((MEM_ROWS, D), bf),
            pltpu.VMEM((LAYERS, D // n, g * GROUP), bf),
            pltpu.VMEM((rows, D), bf),
            pltpu.VMEM((rows, D), bf),
            pltpu.VMEM((8, span), f32),
            pltpu.VMEM((rows, D), bf),
            dma((4 * LAYERS, 6)),
            dma((4 * LAYERS, 6)),
            dma((4 * LAYERS, 7)),
            dma((4 * LAYERS, 7)),
            dma((4 * LAYERS,)),
            dma((LAYERS, 3)),
            dma((LAYERS, 3)),
            dma((LAYERS, 4, 2)),
            dma((LAYERS, 4, 2)),
            dma((LAYERS, g)),
            dma((LAYERS, g)),
            dma((8 * LAYERS,)),
            dma((n - 1,)),
            dma((n - 1,)),
            dma((3,)),
            dma((3,)),
            dma(()),
        ],
        compiler_params=pltpu.CompilerParams(
            collective_id=0, has_side_effects=True, vmem_limit_bytes=62 * 1024 * 1024
        ),
    )(lengths, tokens, memory, *vectors, cotangent, sq, so, su, sd)


def norm_rows(values, gain_vec, shift_vec):
    row_mean = jnp.mean(values, axis=-1, keepdims=True)
    centred = values - row_mean
    variance = jnp.mean(centred * centred, axis=-1, keepdims=True)
    return centred * lax.rsqrt(variance + norm_eps) * gain_vec + shift_vec


def gelu_exact(values):
    return jax.nn.gelu(values, approximate=False)


def gather_layer(stacks, layer_index):
    (
        w_qkv,
        b_qv,
        w_out,
        b_out,
        gain_attn,
        shift_attn,
        w_up,
        b_up,
        w_down,
        b_down,
        gain_ffn,
        shift_ffn,
    ) = tuple((stacked[layer_index] for stacked in stacks))
    return (
        lax.all_gather(w_qkv, "fsdp", axis=0, tiled=True),
        lax.all_gather(b_qv, "fsdp", axis=0, tiled=True),
        lax.all_gather(w_out, "fsdp", axis=0, tiled=True),
        lax.all_gather(b_out, "fsdp", axis=0, tiled=True),
        lax.all_gather(gain_attn, "fsdp", axis=0, tiled=True),
        lax.all_gather(shift_attn, "fsdp", axis=0, tiled=True),
        lax.all_gather(w_up, "fsdp", axis=0, tiled=True),
        lax.all_gather(b_up, "fsdp", axis=0, tiled=True),
        lax.all_gather(w_down, "fsdp", axis=0, tiled=True),
        lax.all_gather(b_down, "fsdp", axis=0, tiled=True),
        lax.all_gather(gain_ffn, "fsdp", axis=0, tiled=True),
        lax.all_gather(shift_ffn, "fsdp", axis=0, tiled=True),
    )


def attend_forward(queries, keys_all, values_all, key_live):
    total_rows, local_heads = (queries.shape[0], queries.shape[1])
    block_rows = math.gcd(total_rows, 512)
    block_count = total_rows // block_rows
    score_scale = HD ** (-0.5)

    def one_block(query_block):
        scores = (
            jnp.einsum("qhd,khd->hqk", query_block, keys_all, preferred_element_type=jnp.float32)
            * score_scale
        )
        scores = jnp.where(key_live[None, None, :], scores, masked_score)
        top_score = jnp.max(scores, axis=-1, keepdims=True)
        exponent = jnp.exp(scores - top_score)
        row_total = jnp.sum(exponent, axis=-1, keepdims=True)
        probability = (exponent / row_total).astype(jnp.bfloat16)
        context = jnp.einsum(
            "hqk,khd->qhd", probability, values_all, preferred_element_type=jnp.float32
        )
        return (context.astype(jnp.bfloat16), (top_score + jnp.log(row_total))[..., 0])

    blocks = queries.reshape(block_count, block_rows, local_heads, HD)
    context, log_total = lax.map(one_block, blocks)
    return (context.reshape(total_rows, local_heads, HD), log_total)


def attend_backward(queries, keys_all, values_all, grad_context, log_total, key_live):
    total_rows, local_heads = (queries.shape[0], queries.shape[1])
    block_rows = math.gcd(total_rows, 512)
    block_count = total_rows // block_rows
    score_scale = HD ** (-0.5)

    def one_block(running, inputs):
        grad_keys, grad_values = running
        query_block, grad_block, log_block = inputs
        scores = (
            jnp.einsum("qhd,khd->hqk", query_block, keys_all, preferred_element_type=jnp.float32)
            * score_scale
        )
        scores = jnp.where(key_live[None, None, :], scores, masked_score)
        probability = jnp.exp(scores - log_block[:, :, None])
        grad_prob = jnp.einsum(
            "qhd,khd->hqk", grad_block, values_all, preferred_element_type=jnp.float32
        )
        grad_values = grad_values + jnp.einsum(
            "hqk,qhd->khd",
            probability.astype(jnp.bfloat16),
            grad_block,
            preferred_element_type=jnp.float32,
        )
        inner_sum = jnp.sum(grad_prob * probability, axis=-1, keepdims=True)
        grad_scores = (probability * (grad_prob - inner_sum)).astype(jnp.bfloat16)
        grad_query = (
            jnp.einsum("hqk,khd->qhd", grad_scores, keys_all, preferred_element_type=jnp.float32)
            * score_scale
        )
        grad_keys = (
            grad_keys
            + jnp.einsum(
                "hqk,qhd->khd", grad_scores, query_block, preferred_element_type=jnp.float32
            )
            * score_scale
        )
        return ((grad_keys, grad_values), grad_query)

    zero_keys = jnp.zeros((total_rows, local_heads, HD), jnp.float32)
    shaped = (
        queries.reshape(block_count, block_rows, local_heads, HD),
        grad_context.reshape(block_count, block_rows, local_heads, HD),
        log_total,
    )
    (grad_keys, grad_values), grad_queries = lax.scan(one_block, (zero_keys, zero_keys), shaped)
    return (grad_queries.reshape(total_rows, local_heads, HD), grad_keys, grad_values)


def layer_forward(hidden, weights, key_live):
    (
        w_qkv,
        b_qv,
        w_out,
        b_out,
        gain_attn,
        shift_attn,
        w_up,
        b_up,
        w_down,
        b_down,
        gain_ffn,
        shift_ffn,
    ) = weights
    local_rows = hidden.shape[0]
    groups = lax.axis_size("seq")
    local_heads = HEADS // groups
    bias_qv = b_qv.astype(jnp.float32)
    bias_full = jnp.concatenate([bias_qv[:D], jnp.zeros((D,), jnp.float32), bias_qv[D:]])
    hidden_low = hidden.astype(jnp.bfloat16)
    projected = (jnp.dot(hidden_low, w_qkv, preferred_element_type=jnp.float32) + bias_full).astype(
        jnp.bfloat16
    )
    by_head = lax.all_to_all(
        projected.reshape(local_rows, 3, groups, local_heads, HD),
        "seq",
        split_axis=2,
        concat_axis=0,
        tiled=True,
    )
    context, log_total = attend_forward(
        by_head[:, 0, 0], by_head[:, 1, 0], by_head[:, 2, 0], key_live
    )
    ctx_rows = lax.all_to_all(
        context.reshape(local_rows * groups, 1, local_heads, HD),
        "seq",
        split_axis=0,
        concat_axis=1,
        tiled=True,
    ).reshape(local_rows, D)
    attended = jnp.dot(ctx_rows, w_out, preferred_element_type=jnp.float32) + b_out.astype(
        jnp.float32
    )
    residual_one = hidden + attended
    normed = norm_rows(residual_one, gain_attn.astype(jnp.float32), shift_attn.astype(jnp.float32))
    pre_gelu = jnp.dot(
        normed.astype(jnp.bfloat16), w_up, preferred_element_type=jnp.float32
    ) + b_up.astype(jnp.float32)
    active = gelu_exact(pre_gelu).astype(jnp.bfloat16)
    branch_out = jnp.dot(active, w_down, preferred_element_type=jnp.float32) + b_down.astype(
        jnp.float32
    )
    residual_two = normed + branch_out
    output = norm_rows(residual_two, gain_ffn.astype(jnp.float32), shift_ffn.astype(jnp.float32))
    stored = (
        hidden,
        by_head,
        log_total,
        ctx_rows,
        residual_one,
        normed,
        pre_gelu,
        active,
        residual_two,
    )
    return (output, stored)


def layer_backward(grad_output, weights, stored, key_live):
    (
        w_qkv,
        b_qv,
        w_out,
        b_out,
        gain_attn,
        shift_attn,
        w_up,
        b_up,
        w_down,
        b_down,
        gain_ffn,
        shift_ffn,
    ) = weights
    hidden, by_head, log_total, ctx_rows, residual_one, normed, pre_gelu, active, residual_two = (
        stored
    )
    local_rows = hidden.shape[0]
    groups = lax.axis_size("seq")
    local_heads = HEADS // groups
    ffn_pull = jax.vjp(
        norm_rows, residual_two, gain_ffn.astype(jnp.float32), shift_ffn.astype(jnp.float32)
    )[1]
    grad_two, grad_gain_ffn, grad_shift_ffn = ffn_pull(grad_output)
    grad_branch = grad_two.astype(jnp.bfloat16)
    grad_b_down = jnp.sum(grad_branch.astype(jnp.float32), axis=0)
    grad_w_down = jnp.einsum("rf,rd->fd", active, grad_branch, preferred_element_type=jnp.float32)
    grad_active = jnp.einsum("rd,fd->rf", grad_branch, w_down, preferred_element_type=jnp.float32)
    gelu_pull = jax.vjp(gelu_exact, pre_gelu)[1]
    grad_pre = gelu_pull(grad_active)[0].astype(jnp.bfloat16)
    grad_b_up = jnp.sum(grad_pre.astype(jnp.float32), axis=0)
    normed_low = normed.astype(jnp.bfloat16)
    grad_w_up = jnp.einsum("rd,rf->df", normed_low, grad_pre, preferred_element_type=jnp.float32)
    grad_normed = (
        jnp.einsum("rf,df->rd", grad_pre, w_up, preferred_element_type=jnp.float32) + grad_two
    )
    attn_pull = jax.vjp(
        norm_rows, residual_one, gain_attn.astype(jnp.float32), shift_attn.astype(jnp.float32)
    )[1]
    grad_one, grad_gain_attn, grad_shift_attn = attn_pull(grad_normed)
    grad_attended = grad_one.astype(jnp.bfloat16)
    grad_b_out = jnp.sum(grad_attended.astype(jnp.float32), axis=0)
    grad_w_out = jnp.einsum(
        "rk,rd->kd", ctx_rows, grad_attended, preferred_element_type=jnp.float32
    )
    grad_ctx = jnp.einsum(
        "rd,kd->rk", grad_attended, w_out, preferred_element_type=jnp.float32
    ).astype(jnp.bfloat16)
    grad_heads = lax.all_to_all(
        grad_ctx.reshape(local_rows, groups, local_heads, HD),
        "seq",
        split_axis=1,
        concat_axis=0,
        tiled=True,
    )
    grad_queries, grad_keys, grad_values = attend_backward(
        by_head[:, 0, 0], by_head[:, 1, 0], by_head[:, 2, 0], grad_heads[:, 0], log_total, key_live
    )
    grad_stack = jnp.stack([grad_queries, grad_keys, grad_values], axis=1).astype(jnp.bfloat16)[
        :, :, None
    ]
    grad_projected = lax.all_to_all(
        grad_stack, "seq", split_axis=0, concat_axis=2, tiled=True
    ).reshape(local_rows, 3 * D)
    grad_sums = jnp.sum(grad_projected.astype(jnp.float32), axis=0)
    grad_b_qv = jnp.concatenate([grad_sums[:D], grad_sums[2 * D :]])
    hidden_low = hidden.astype(jnp.bfloat16)
    grad_w_qkv = jnp.einsum(
        "rd,re->de", hidden_low, grad_projected, preferred_element_type=jnp.float32
    )
    grad_hidden = (
        jnp.einsum("re,de->rd", grad_projected, w_qkv, preferred_element_type=jnp.float32)
        + grad_one
    )
    weight_grads = (
        grad_w_qkv,
        grad_b_qv,
        grad_w_out,
        grad_b_out,
        grad_gain_attn,
        grad_shift_attn,
        grad_w_up,
        grad_b_up,
        grad_w_down,
        grad_b_down,
        grad_gain_ffn,
        grad_shift_ffn,
    )
    return (grad_hidden, weight_grads)


def fsdp_layer_sum(weight_grads):
    (
        grad_w_qkv,
        grad_b_qv,
        grad_w_out,
        grad_b_out,
        grad_gain_attn,
        grad_shift_attn,
        grad_w_up,
        grad_b_up,
        grad_w_down,
        grad_b_down,
        grad_gain_ffn,
        grad_shift_ffn,
    ) = weight_grads
    return (
        lax.psum_scatter(grad_w_qkv.astype(jnp.bfloat16), "fsdp", scatter_dimension=0, tiled=True),
        lax.psum_scatter(grad_b_qv.astype(jnp.bfloat16), "fsdp", scatter_dimension=0, tiled=True),
        lax.psum_scatter(grad_w_out.astype(jnp.bfloat16), "fsdp", scatter_dimension=0, tiled=True),
        lax.psum_scatter(grad_b_out.astype(jnp.bfloat16), "fsdp", scatter_dimension=0, tiled=True),
        lax.psum_scatter(grad_gain_attn.astype(jnp.bfloat16), "fsdp", scatter_dimension=0, tiled=True),
        lax.psum_scatter(grad_shift_attn.astype(jnp.bfloat16), "fsdp", scatter_dimension=0, tiled=True),
        lax.psum_scatter(grad_w_up.astype(jnp.bfloat16), "fsdp", scatter_dimension=0, tiled=True),
        lax.psum_scatter(grad_b_up.astype(jnp.bfloat16), "fsdp", scatter_dimension=0, tiled=True),
        lax.psum_scatter(grad_w_down.astype(jnp.bfloat16), "fsdp", scatter_dimension=0, tiled=True),
        lax.psum_scatter(grad_b_down.astype(jnp.bfloat16), "fsdp", scatter_dimension=0, tiled=True),
        lax.psum_scatter(grad_gain_ffn.astype(jnp.bfloat16), "fsdp", scatter_dimension=0, tiled=True),
        lax.psum_scatter(grad_shift_ffn.astype(jnp.bfloat16), "fsdp", scatter_dimension=0, tiled=True),
    )


def seq_total_sum(shard_grads, grad_memory):
    (
        grad_w_qkv,
        grad_b_qv,
        grad_w_out,
        grad_b_out,
        grad_gain_attn,
        grad_shift_attn,
        grad_w_up,
        grad_b_up,
        grad_w_down,
        grad_b_down,
        grad_gain_ffn,
        grad_shift_ffn,
    ) = shard_grads
    pieces = (
        lax.psum_scatter(
            grad_w_qkv.astype(jnp.bfloat16), "seq", scatter_dimension=2, tiled=True
        ).astype(jnp.float32),
        lax.psum_scatter(
            grad_w_out.astype(jnp.bfloat16), "seq", scatter_dimension=2, tiled=True
        ).astype(jnp.float32),
        lax.psum_scatter(
            grad_w_up.astype(jnp.bfloat16), "seq", scatter_dimension=2, tiled=True
        ).astype(jnp.float32),
        lax.psum_scatter(
            grad_w_down.astype(jnp.bfloat16), "seq", scatter_dimension=2, tiled=True
        ).astype(jnp.float32),
    )
    matrices = (
        lax.all_gather(pieces[0].astype(jnp.bfloat16), "seq", axis=2, tiled=True).astype(
            jnp.float32
        ),
        lax.all_gather(pieces[1].astype(jnp.bfloat16), "seq", axis=2, tiled=True).astype(
            jnp.float32
        ),
        lax.all_gather(pieces[2].astype(jnp.bfloat16), "seq", axis=2, tiled=True).astype(
            jnp.float32
        ),
        lax.all_gather(pieces[3].astype(jnp.bfloat16), "seq", axis=2, tiled=True).astype(
            jnp.float32
        ),
    )
    smalls = (
        lax.psum(grad_b_qv.astype(jnp.bfloat16), "seq").astype(jnp.float32),
        lax.psum(grad_b_out.astype(jnp.bfloat16), "seq").astype(jnp.float32),
        lax.psum(grad_gain_attn.astype(jnp.bfloat16), "seq").astype(jnp.float32),
        lax.psum(grad_shift_attn.astype(jnp.bfloat16), "seq").astype(jnp.float32),
        lax.psum(grad_b_up.astype(jnp.bfloat16), "seq").astype(jnp.float32),
        lax.psum(grad_b_down.astype(jnp.bfloat16), "seq").astype(jnp.float32),
        lax.psum(grad_gain_ffn.astype(jnp.bfloat16), "seq").astype(jnp.float32),
        lax.psum(grad_shift_ffn.astype(jnp.bfloat16), "seq").astype(jnp.float32),
        lax.psum(grad_memory.astype(jnp.bfloat16), "seq").astype(jnp.float32),
    )
    weights_sum = (
        matrices[0],
        smalls[0],
        matrices[1],
        smalls[1],
        smalls[2],
        smalls[3],
        matrices[2],
        smalls[4],
        matrices[3],
        smalls[5],
        smalls[6],
        smalls[7],
    )
    return (weights_sum, smalls[8])


def plain_body(
    tokens,
    memory,
    lengths,
    w_qkv,
    b_qv,
    w_out,
    b_out,
    gain_attn,
    shift_attn,
    w_up,
    b_up,
    w_down,
    b_down,
    gain_ffn,
    shift_ffn,
    cotangent,
):
    local_rows = tokens.shape[0]
    groups = lax.axis_size("seq")
    seq_place = lax.axis_index("seq")
    length = lengths[0]
    positions = seq_place * local_rows + jnp.arange(local_rows, dtype=jnp.int32)
    key_live = jnp.arange(local_rows * groups, dtype=jnp.int32) < length + 2 * MEM
    row_live = (positions < length + 2 * MEM)[:, None]
    token_live = ((positions >= MEM) & (positions < length + MEM))[:, None]
    memory_slots = jnp.arange(2 * MEM, dtype=jnp.int32)
    targets = jnp.where(memory_slots < MEM, memory_slots, length + memory_slots)
    select = positions[:, None] == targets[None, :]
    hidden = jnp.where(token_live, tokens.astype(jnp.float32), 0.0) + jnp.dot(
        select.astype(jnp.bfloat16), memory[0], preferred_element_type=jnp.float32
    )
    stacks = (
        w_qkv,
        b_qv,
        w_out,
        b_out,
        gain_attn,
        shift_attn,
        w_up,
        b_up,
        w_down,
        b_down,
        gain_ffn,
        shift_ffn,
    )
    kept = []
    for layer_index in range(LAYERS):
        weights = gather_layer(stacks, layer_index)
        hidden, stored = layer_forward(hidden, weights, key_live)
        kept.append((weights, stored))
    result = jnp.where(row_live, hidden, 0.0)
    grad_hidden = jnp.where(row_live, cotangent, 0.0)
    collected = []
    for layer_index in reversed(range(LAYERS)):
        weights, stored = kept[layer_index]
        grad_hidden, weight_grads = layer_backward(grad_hidden, weights, stored, key_live)
        collected.insert(0, fsdp_layer_sum(weight_grads))
    stacked_grads = tuple((jnp.stack(member) for member in zip(*collected)))
    grad_tokens = jnp.where(token_live, grad_hidden, 0.0)
    grad_memory = jnp.dot(
        select.astype(jnp.float32).T, grad_hidden, precision=lax.Precision.HIGHEST
    )[None]
    summed, memory_sum = seq_total_sum(stacked_grads, grad_memory)
    return (result, grad_tokens, memory_sum) + tuple(summed)


SMALL_OUT = SMALL * LAYERS


def backward_kernel(n, g, *refs):
    (
        len_ref, mask_ref, vec, cot_ref, y_ref, fq_ref, fo_ref, fu_ref, fd_ref, xb_ref, heads_ref, lse_ref, ctx_ref, r1_ref, slope_ref, act_ref, r2_ref,
        result_ref, tokens_ref, small_ref, oq_ref, oo_ref, ou_ref, od_ref,
        wq, wo, wu, wd, slope, act, xb, hd, lse, ctx, r1, r2,
        p_o, p_u, p_d, pair_o, pair_u, pair_d, half_o, half_u, half_d, plane_o, plane_u, plane_d,
        sum_o, sum_u, sum_d, whole_o, whole_u, whole_d, part_o, part_u, part_d, p_q, half_q, plane_q, sum_q, line_q,
        gx, gn, norm_t, low, live, home, gc_send, gctx, key_t, acc_k, acc_v, acc_d, acc_e, dq_s, grad_p, aside_send, aside_in, across_in,
        small_a, small_b, small_c, land_a, land_b, land_c,
        load_sem, stream_sem, pair_send, pair_recv, half_send, half_recv, plane_send, plane_recv, z_send, z_recv, out_send, out_recv, out_own,
        c_send, c_recv, x_send, x_recv, qh_send, qh_recv, qp_send, qp_recv, ql_send, ql_recv, qo_send, qo_recv, qo_own, sa_send, sa_recv, sb_send, sb_recv, sc_send, sc_recv, home_send, home_recv, store_sem,
        pair_credit, half_credit, plane_credit, z_credit,
    ) = refs
    place = Place(n, g)
    f, s, me, core = place.f, place.s, place.me, place.core
    rows = gx.shape[0]
    span = rows * g
    half = n // 2
    partner = place.on_plane(place.partner)
    bf, f32 = jnp.bfloat16, jnp.float32
    parts = (p_o, p_u, p_d)
    pairs = (pair_o, pair_u, pair_d)
    halves = (half_o, half_u, half_d)
    planes = (plane_o, plane_u, plane_d)
    sums = (sum_o, sum_u, sum_d)
    wholes = (whole_o, whole_u, whole_d)
    inners = (part_o, part_u, part_d)
    outs = (oo_ref, ou_ref, od_ref)
    O, U, DN = 0, 1, 2
    width = D // n
    inner = jnp.logical_and(s > 0, s < g - 1)
    outer = jnp.logical_not(inner)
    side = s // 2
    inner_chip = place.at(f, 1 + side)
    other_inner = place.at(f, 3 - s)
    end_chip = place.at(f, 3 * side)

    def member(i):
        return place.member(lax.rem(me + i, g))

    def depth(m):
        return pairs[m].shape[1]

    def part_rows(m, owner):
        return parts[m].at[aligned(owner * depth(m), depth(m), 32)]

    def part_half(m, owner, which):
        return parts[m].at[aligned(owner * depth(m) + which * (depth(m) // 2), depth(m) // 2, 16)]

    def half_rows(ref, m, which):
        return ref.at[aligned(which * (depth(m) // 2), depth(m) // 2, 16)]

    names = {}

    def load(name, src, dst):
        index = {"xb": 0, "hd": 1, "lse": 2, "ctx": 3, "r1": 4, "r2": 5, "wq": 6, "wo": 7, "cot": 8, "y": 9}[name]
        copy = pltpu.make_async_copy(src, dst, load_sem.at[index])
        copy.start()
        names[name] = copy

    def loaded(name):
        names.pop(name).wait()

    def stream(layer, c, slot):
        columns = pl.ds(pl.multiple_of(c * D, 128), D)
        return [
            pltpu.make_async_copy(fd_ref.at[layer, columns, :], wd.at[slot], stream_sem.at[0, slot]),
            pltpu.make_async_copy(fu_ref.at[layer, :, columns], wu.at[slot], stream_sem.at[1, slot]),
            pltpu.make_async_copy(slope_ref.at[layer, :, columns], slope.at[slot], stream_sem.at[2, slot]),
            pltpu.make_async_copy(act_ref.at[layer, :, columns], act.at[slot], stream_sem.at[3, slot]),
        ]

    last = LAYERS - 1
    for copy in stream(last, 0, 0):
        copy.start()
    load("cot", cot_ref, low.at[0])
    load("y", y_ref, gn)
    load("r2", r2_ref.at[last], r2)
    load("r1", r1_ref.at[last], r1)
    load("wo", fo_ref.at[last], wo)
    load("ctx", ctx_ref.at[last], ctx)
    load("hd", heads_ref.at[last], hd)
    load("lse", lse_ref.at[last], lse)
    load("xb", xb_ref.at[last], xb)
    load("wq", fq_ref.at[last], wq)

    place.barrier()

    def pair_copy(layer, m, c):
        return remote(part_rows(m, 2 * c + 1 - core), pairs[m].at[c], pair_send.at[layer, m, c], pair_recv.at[layer, m, c], partner)

    def half_copy(layer, m, way):
        device = place.on_plane((place.fx, place.fy)[way])
        return remote(part_half(m, place.fd, way), halves[m].at[way], half_send.at[layer, m, way], half_recv.at[layer, m, way], device)

    def plane_copy(layer, m, way):
        owner = (place.fx, place.fy)[way]
        return remote(part_rows(m, owner), planes[m].at[way], plane_send.at[layer, m, way], plane_recv.at[layer, m, way], place.on_plane(owner))

    def end_copy(layer, m):
        return remote(sums[m].at[layer], wholes[m], z_send.at[layer, m, 0], z_recv.at[layer, m, 0], inner_chip)

    def inner_copy(layer, m):
        return remote(half_rows(sums[m].at[layer], m, 1 - side), inners[m], z_send.at[layer, m, 1], z_recv.at[layer, m, 1], other_inner)

    def out_across(layer, m):
        return remote(half_rows(sums[m].at[layer], m, side), half_rows(outs[m].at[layer], m, side), out_send.at[layer, m, 0], out_recv.at[layer, m, 0], other_inner)

    def out_end(layer, m):
        return remote(half_rows(sums[m].at[layer], m, side), half_rows(outs[m].at[layer], m, side), out_send.at[layer, m, 1], out_recv.at[layer, m, 1], end_chip)

    def out_pass(layer, m):
        other = half_rows(outs[m].at[layer], m, 1 - side)
        return remote(other, other, out_send.at[layer, m, 2], out_recv.at[layer, m, 2], end_chip)

    def out_local(layer, m):
        return pltpu.make_async_copy(half_rows(sums[m].at[layer], m, side), half_rows(outs[m].at[layer], m, side), out_own.at[layer, m])

    def pair_ready(layer, m):
        if layer != last:
            pl.semaphore_wait(pair_credit.at[m], 1)

    def each(count, step, body):
        def go(k, carry):
            body(k * step)
            return carry

        lax.fori_loop(0, count // step, go, 0)

    def add(target, start, source, count):
        step = 48 if count % 32 else 32

        def body(at):
            mine, theirs = aligned(start + at, step, 16), aligned(at, step, 16)
            target[mine, :] = (target[mine, :].astype(f32) + source[theirs, :].astype(f32)).astype(bf)

        each(count, step, body)

    def sum_pair(layer, m):
        for c in range(half):
            pair_copy(layer, m, c).wait_recv()
        for c in range(half):
            pair_copy(layer, m, c).wait_send()
        for owner in (place.fd, place.fx, place.fy, f):
            add(parts[m], owner * depth(m), pairs[m].at[owner // 2], depth(m))
            if owner is place.fd:
                for way in range(2):
                    if layer != last:
                        pl.semaphore_wait(half_credit.at[m, way], 1)
                    half_copy(layer, m, way).start()
        if layer:
            pl.semaphore_signal(pair_credit.at[m], 1, device_id=partner, device_id_type=MESH)

    def sum_half(layer, m):
        for way in range(2):
            half_copy(layer, m, way).wait_recv()
            owner = (place.fy, place.fx)[way]
            add(parts[m], owner * depth(m) + way * (depth(m) // 2), halves[m].at[way], depth(m) // 2)
            if layer != last:
                pl.semaphore_wait(plane_credit.at[m, 1 - way], 1)
            plane_copy(layer, m, 1 - way).start()
        for way in range(2):
            if layer:
                pl.semaphore_signal(
                    half_credit.at[m, way], 1, device_id=place.on_plane((place.fx, place.fy)[way]), device_id_type=MESH)
            half_copy(layer, m, way).wait_send()

    def sum_plane(layer, m):
        for way in range(2):
            plane_copy(layer, m, way).wait_recv()

        def body(at):
            mine, theirs = aligned(f * depth(m) + at, 32, 32), aligned(at, 32, 32)
            total = parts[m][mine, :].astype(f32) + planes[m][0, theirs, :].astype(f32) + planes[m][1, theirs, :].astype(f32)
            sums[m][layer, theirs, :] = total.astype(bf)

        each(depth(m), 32, body)
        for way in range(2):
            if layer:
                pl.semaphore_signal(
                    plane_credit.at[m, way], 1, device_id=place.on_plane((place.fx, place.fy)[way]), device_id_type=MESH)
            plane_copy(layer, m, way).wait_send()

        @pl.when(outer)
        def _():
            if layer != last:
                pl.semaphore_wait(z_credit.at[m, 0], 1)
            end_copy(layer, m).start()

    def sum_end(layer, m):
        @pl.when(inner)
        def _():
            end_copy(layer, m).wait_recv()
            add(sums[m].at[layer], (1 - side) * (depth(m) // 2), half_rows(wholes[m], m, 1 - side), depth(m) // 2)
            if layer != last:
                pl.semaphore_wait(z_credit.at[m, 1], 1)
            inner_copy(layer, m).start()
            add(sums[m].at[layer], side * (depth(m) // 2), half_rows(wholes[m], m, side), depth(m) // 2)
            if layer:
                pl.semaphore_signal(z_credit.at[m, 0], 1, device_id=end_chip, device_id_type=MESH)

    def sum_line(layer, m):
        @pl.when(inner)
        def _():
            inner_copy(layer, m).wait_recv()
            add(sums[m].at[layer], side * (depth(m) // 2), inners[m], depth(m) // 2)
            out_across(layer, m).start()
            out_end(layer, m).start()
            out_local(layer, m).start()
            if layer:
                pl.semaphore_signal(z_credit.at[m, 1], 1, device_id=other_inner, device_id_type=MESH)

    def pass_on(layer, m):
        @pl.when(inner)
        def _():
            out_across(layer, m).wait_recv()
            out_pass(layer, m).start()

    neighbours = (place.fx, place.fy)

    def q_rows(owner, start=0, count=2 * width):
        return p_q.at[aligned((owner // 2) * (2 * width) + start, count, 32)]

    def q_half_copy(layer, way):
        return remote(q_rows(place.fd, way * width, width), half_q.at[layer, way], qh_send.at[layer, way], qh_recv.at[layer, way], place.on_plane(neighbours[way]))

    def q_plane_copy(layer, way):
        return remote(q_rows(neighbours[way]), plane_q.at[layer, way], qp_send.at[layer, way], qp_recv.at[layer, way], place.on_plane(neighbours[way]))

    def q_line_copy(layer):
        return remote(sum_q.at[layer, aligned((1 - side) * width, width, 32)], line_q.at[layer], ql_send.at[layer], ql_recv.at[layer], place.at(f, lax.rem(s + 2, g)))

    def q_out(layer, i):
        columns = aligned(me * GROUP, GROUP, 128)
        device = place.at(f - core + side, lax.rem(s + i, g))
        return remote(
            sum_q.at[layer, aligned(side * width, width, 32)], oq_ref.at[layer, :, columns], qo_send.at[layer, i], qo_recv.at[layer, me], device)

    def q_out_local(layer):
        columns = aligned(me * GROUP, GROUP, 128)
        return pltpu.make_async_copy(sum_q.at[layer, aligned(side * width, width, 32)], oq_ref.at[layer, :, columns], qo_own.at[layer])

    def q_start(layer):
        for way in range(2):
            q_half_copy(layer, way).start()

    def q_sum_half(layer):
        for way in range(2):
            q_half_copy(layer, way).wait_recv()
            owner = (place.fy, place.fx)[way]
            add(p_q, (owner // 2) * (2 * width) + way * width, half_q.at[layer, way], width)
            q_plane_copy(layer, 1 - way).start()

    def q_sum_plane(layer):
        for way in range(2):
            q_plane_copy(layer, way).wait_recv()

        def body(at):
            mine, theirs = aligned((f // 2) * (2 * width) + at, 32, 32), aligned(at, 32, 32)
            total = p_q[mine, :].astype(f32) + plane_q[layer, 0, theirs, :].astype(f32) + plane_q[layer, 1, theirs, :].astype(f32)
            sum_q[layer, theirs, :] = total.astype(bf)

        each(2 * width, 32, body)
        q_line_copy(layer).start()
        for way in range(2):
            q_half_copy(layer, way).wait_send()
            q_plane_copy(layer, way).wait_send()

    def q_sum_line(layer):
        q_line_copy(layer).wait_recv()
        add(sum_q.at[layer], side * width, line_q.at[layer], width)
        for i in range(1, g):
            q_out(layer, i).start()

        @pl.when(side == core)
        def _():
            q_out_local(layer).start()

        @pl.when(side != core)
        def _():
            q_out(layer, 0).start()

    def q_finish(layer):
        q_line_copy(layer).wait_send()
        for i in range(1, g):
            q_out(layer, i).wait_send()

        @pl.when(side == core)
        def _():
            q_out_local(layer).wait()

        @pl.when(side != core)
        def _():
            q_out(layer, 0).wait_send()

        for group in range(g):
            columns = aligned(group * GROUP, GROUP, 128)
            arrival = remote(
                sum_q.at[layer, aligned(side * width, width, 32)], oq_ref.at[layer, :, columns], qo_send.at[layer, 0], qo_recv.at[layer, group], partner)

            @pl.when(jnp.logical_not(jnp.logical_and(side == core, me == group)))
            def _(arrival=arrival):
                arrival.wait_recv()

    lane = lax.broadcasted_iota(jnp.int32, (rows, 128), 1)
    low_lane = lane < 64

    def vector(kind, layer):
        row = 2 * WIDE.index(kind) + layer
        return vec[row : row + 1, :]

    def norm_back(grad, residual, layer, gain_row, shift_row):
        standard, scale = standardize(residual)
        small_a[layer * SMALL + gain_row : layer * SMALL + gain_row + 1, :] = jnp.sum(grad * standard, axis=0, keepdims=True)
        small_a[layer * SMALL + shift_row : layer * SMALL + shift_row + 1, :] = jnp.sum(grad, axis=0, keepdims=True)
        inner = grad * vector(gain_row, layer)
        back = scale * (inner - jnp.mean(inner, -1, keepdims=True) - standard * jnp.mean(inner * standard, -1, keepdims=True))
        return back, standard

    def row_sum(layer, row, values):
        small_a[layer * SMALL + row : layer * SMALL + row + 1, : values.shape[1]] = jnp.sum(values.astype(f32), axis=0, keepdims=True)

    def go_home(slot, device):
        return remote(low.at[slot], home.at[slot], home_send.at[slot], home_recv.at[slot], device)

    def send_home(slot):
        @pl.when(jnp.logical_not(place.stays))
        def _():
            go_home(slot, place.away_home).start()

        @pl.when(place.stays)
        def _():
            home[slot] = low[slot]

    def sent_home(slot):
        @pl.when(jnp.logical_not(place.stays))
        def _():
            go_home(slot, place.away_home).wait_send()

    def came_home(slot):
        @pl.when(jnp.logical_not(place.stays))
        def _():
            go_home(slot, place.away_home).wait_recv()

    small_a[...] = jnp.zeros_like(small_a)
    live[...] = jnp.where(jnp.broadcast_to(mask_ref[0:1, :], (128, span)) < 0.0, 0.0, 1.0).T.astype(bf)
    loaded("y")
    low[1] = gn[...].astype(bf)
    send_home(1)
    loaded("cot")
    gx[...] = low[0].astype(f32)

    for layer in reversed(range(LAYERS)):
        loaded("r2")
        grad_two, _ = norm_back(gx[...], r2[...], layer, GAIN_F, SHIFT_F)
        gn[...] = grad_two
        low[0] = grad_two.astype(bf)
        row_sum(layer, B_DOWN, low[0])
        loaded("r1")
        normed = standardize(r1[...])[0] * vector(GAIN_A, layer) + vector(SHIFT_A, layer)
        norm_t[...] = normed.astype(bf).T
        if layer != last:
            sum_plane(last, DN)
            q_sum_half(last)
            sum_plane(last, U)
        pair_ready(layer, DN)

        def ffn(c, carry):
            slot = lax.rem(c, 2)

            @pl.when(c + 1 < FF // D)
            def _():
                for copy in stream(layer, c + 1, 1 - slot):
                    copy.start()

            for copy in stream(layer, c, slot):
                copy.wait()
            branch = low[0]
            grad_pre = (dot_t(branch, wd[slot]) * slope[slot].astype(f32)).astype(bf)
            small_a[pl.ds(layer * SMALL + B_UP + c, 1), :] = jnp.sum(grad_pre.astype(f32), axis=0, keepdims=True)
            columns = pl.ds(pl.multiple_of(c * D, 128), D)
            p_d[columns, :] = t_dot(act[slot], branch).astype(bf)
            pair_copy(layer, DN, c).start()
            p_u[:, columns] = dot(norm_t[...], grad_pre).astype(bf)
            gn[...] += dot_t(grad_pre, wu[slot])
            return carry

        lax.fori_loop(0, FF // D, ffn, 0)
        if layer:
            for copy in stream(layer - 1, 0, 0):
                copy.start()
            load("r2", r2_ref.at[layer - 1], r2)
        pair_ready(layer, U)
        for c in range(half):
            pair_copy(layer, U, c).start()

        grad_one, _ = norm_back(gn[...], r1[...], layer, GAIN_A, SHIFT_A)
        gx[...] = grad_one
        if layer == last:
            sent_home(1)
        low[1] = grad_one.astype(bf)
        row_sum(layer, B_OUT, low[1])
        if layer:
            load("r1", r1_ref.at[layer - 1], r1)
        loaded("wo")

        def c_copy(i):
            return remote(gc_send.at[i - 1], gctx.at[me], c_send.at[layer, i], c_recv.at[layer, i], member(i))

        if layer != last:
            for i in range(1, g):
                remote(gc_send.at[i - 1], gctx.at[me], c_send.at[last, i], c_recv.at[last, i], member(i)).wait_send()

        def out_back(k, carry):
            b = lax.rem(me + k, g)
            base = b * (3 * HD)
            first = dot_t(low[1], wo[pl.ds(pl.multiple_of(base, 64), 128), :]).astype(bf)
            second = dot_t(low[1], wo[pl.ds(pl.multiple_of(base + 64, 64), 128), :]).astype(bf)
            second = jnp.where(low_lane, jnp.zeros_like(second), second)

            @pl.when(k < g)
            def _():
                gc_send[k - 1, :, 0:128] = first
                gc_send[k - 1, :, 128:256] = second
                c_copy(k).start()

            @pl.when(k == g)
            def _():
                gctx[me, :, 0:128] = first
                gctx[me, :, 128:256] = second

            return carry

        lax.fori_loop(1, g + 1, out_back, 0)
        if layer != last:
            q_sum_plane(last)
            sum_plane(last, O)
        loaded("ctx")
        for grp in range(g):
            base = grp * 3 * HD
            p_o[base : base + 128, :] = t_dot(ctx[grp, :, 0:128], low[1]).astype(bf)
            p_o[base + 128 : base + 192, :] = t_dot(ctx[grp, :, 128:256], low[1])[64:].astype(bf)
        if layer:
            load("wo", fo_ref.at[layer - 1], wo)
            load("ctx", ctx_ref.at[layer - 1], ctx)
        pair_ready(layer, O)
        for c in range(half):
            pair_copy(layer, O, c).start()
        sum_pair(layer, DN)
        sum_pair(layer, U)
        sum_pair(layer, O)
        if layer != last:
            sum_end(last, DN)
            sum_end(last, U)
        sum_half(layer, DN)

        loaded("hd")
        loaded("lse")
        for tile in range(1, 5):
            columns = slice(tile * 128, tile * 128 + 128)
            if tile == 3:
                full = hd[:, columns]
                wide_low = lax.broadcasted_iota(jnp.int32, full.shape, 1) < 64
                hd[:, columns] = jnp.where(wide_low, full, full * live[...])
            else:
                hd[:, columns] = hd[:, columns] * live[...]
        key_t[0:128, :] = hd[:, 128:256].T
        key_t[128:256, :] = hd[:, 512:640].T
        for acc in (acc_k, acc_v, acc_d, acc_e):
            acc[...] = jnp.zeros_like(acc)
        for i in range(1, g):
            c_copy(i).wait_recv()

        def attend(k, carry):
            b = lax.rem(me + k, g)
            block = pl.ds(pl.multiple_of(b * rows, rows), rows)
            q_a = hd[block, 0:128] * bf(HD**-0.5)
            q_d = hd[block, 384:512] * bf(HD**-0.5)
            g_a = gctx[b, :, 0:128]
            g_d = gctx[b, :, 128:256]
            zero = jnp.zeros_like(q_a)
            queries = (jnp.where(low_lane, q_a, zero), jnp.where(low_lane, zero, q_a), jnp.where(low_lane, q_d, zero))
            grads = (jnp.where(low_lane, g_a, zero), jnp.where(low_lane, zero, g_a), g_d)
            turned = []
            for h in range(3):
                keys = slice(512, 640) if h == 2 else slice(128, 256)
                values = slice(384, 512) if h == 2 else slice(256, 384)
                scores = dot_t(hd[:, keys], queries[h])
                prob = jnp.exp(jnp.minimum(scores - lse[h : h + 1, block], 0.0))
                grad_prob = dot_t(hd[:, values], grads[h])
                inner = jnp.sum(grad_prob * prob, axis=0, keepdims=True)
                grad_scores = (prob * (grad_prob - inner)).astype(bf)
                acc_value, acc_key = (acc_d, acc_e) if h == 2 else (acc_v, acc_k)
                acc_value[...] += dot(prob.astype(bf), grads[h])
                acc_key[...] += dot(grad_scores, queries[h])
                turned.append(dot(key_t[h * 64 : h * 64 + 64, :], grad_scores))
            dq_s[block, :] = (jnp.concatenate(turned[:2], axis=0).T * HD**-0.5).astype(bf)
            acc_d[block, :] += jnp.concatenate([turned[2], jnp.zeros_like(turned[2])], axis=0).T * HD**-0.5
            return carry

        lax.fori_loop(1, g + 1, attend, 0)

        if layer:
            load("hd", heads_ref.at[layer - 1], hd)
            load("lse", lse_ref.at[layer - 1], lse)
        wide_low = lax.broadcasted_iota(jnp.int32, (span, 128), 1) < 64
        alive = live[...].astype(f32)
        grad_p[:, 0:128] = dq_s[...]
        grad_p[:, 128:256] = (acc_k[...] * alive).astype(bf)
        grad_p[:, 256:384] = (acc_v[...] * alive).astype(bf)
        grad_p[:, 384:512] = jnp.where(wide_low, acc_d[...], acc_d[...] * alive).astype(bf)
        grad_p[:, 512:640] = (acc_e[...] * alive).astype(bf)

        loaded("wq")
        across, aside = lax.rem(me + 2, g), me + 1 - 2 * core

        def back(quarter):
            return dot_t(grad_p[aligned(quarter * rows, rows, rows), :], wq[...])

        def aside_copy(k):
            return remote(aside_send.at[k], aside_in.at[k], x_send.at[layer, k], x_recv.at[layer, k], partner)

        across_copy = remote(low.at[0], across_in, x_send.at[layer, 2], x_recv.at[layer, 2], place.member(across))
        for k, quarter in ((1, lax.rem(aside + 2, g)), (0, aside)):
            aside_send[k] = back(quarter).astype(bf)
            aside_copy(k).start()
        crossing = back(across)
        aside_copy(1).wait_recv()
        low[0] = (crossing + aside_in[1].astype(f32)).astype(bf)
        across_copy.start()
        loaded("xb")
        p_q[...] = t_dot(xb[...], grad_p[...]).astype(bf)
        q_start(layer)
        small_a[pl.ds(layer * SMALL + VECS + me, 1), 0:GROUP] = jnp.sum(grad_p[...].astype(f32), axis=0, keepdims=True)
        gx[...] += back(me)
        aside_copy(0).wait_recv()
        gx[...] += aside_in[0].astype(f32)
        sum_half(layer, U)
        sum_half(layer, O)
        if layer != last:
            sum_line(last, DN)
            sum_line(last, U)
            sum_end(last, O)
        across_copy.wait_recv()
        gx[...] += across_in[...].astype(f32)
        across_copy.wait_send()
        for k in range(2):
            aside_copy(k).wait_send()
        if layer:
            load("xb", xb_ref.at[layer - 1], xb)
            load("wq", fq_ref.at[layer - 1], wq)

    low[0] = gx[...].astype(bf)
    send_home(0)
    a_copy = remote(small_a, land_a, sa_send, sa_recv, partner)
    a_copy.start()
    q_sum_half(0)
    sum_plane(0, DN)
    sum_plane(0, U)
    q_sum_line(last)
    sum_line(last, O)
    pass_on(last, DN)
    pass_on(last, U)
    a_copy.wait()
    small_b[...] = small_a[...] + land_a[...]
    b_copies = [
        remote(small_b, land_b.at[j], sb_send.at[j], sb_recv.at[j], place.on_plane(owner))
        for j, owner in enumerate((place.fx, place.fy, place.fd))
    ]
    for copy in b_copies:
        copy.start()
    q_sum_plane(0)
    sum_plane(0, O)
    sum_end(0, DN)
    came_home(0)
    position = s * rows + lax.broadcasted_iota(jnp.int32, (rows, 1), 0)
    length = len_ref[0]
    small_c[small_a.shape[0] :, :] = dot(selection(place, rows, length).astype(bf), home[0])
    for copy in b_copies:
        copy.wait()
    small_c[: small_a.shape[0], :] = small_b[...] + land_b[0] + land_b[1] + land_b[2]
    c_copies = [
        remote(small_c, land_c.at[i - 1], sc_send.at[i - 1], sc_recv.at[i - 1], place.at(f, lax.rem(s + i, g))) for i in range(1, g)
    ]
    for copy in c_copies:
        copy.start()
    sum_end(0, U)
    pass_on(last, O)
    is_token = jnp.logical_and(position >= MEM, position < length + MEM)
    home[0] = jnp.where(is_token, home[0], jnp.zeros_like(home[0]))
    tokens_copy = pltpu.make_async_copy(home.at[0], tokens_ref, store_sem.at[0])
    tokens_copy.start()
    came_home(1)
    home[1] = jnp.where(position < length + 2 * MEM, home[1], jnp.zeros_like(home[1]))
    result_copy = pltpu.make_async_copy(home.at[1], result_ref, store_sem.at[1])
    result_copy.start()
    sum_end(0, O)
    q_sum_line(0)
    sum_line(0, DN)
    sum_line(0, U)
    pass_on(0, DN)
    for copy in c_copies:
        copy.wait()
    total = small_c[...]
    for i in range(1, g):
        total = total + land_c[i - 1]
    small_c[...] = total
    small_ref[...] = jnp.zeros_like(small_ref)
    small_ref[SMALL_OUT:, :] = total[small_a.shape[0] :]
    width = D // n
    from_lane = lax.broadcasted_iota(jnp.int32, (D, 128), 0)
    to_lane = lax.broadcasted_iota(jnp.int32, (D, 128), 1)
    pick = jnp.where(jnp.logical_and(from_lane == to_lane + f * width, to_lane < width), 1.0, 0.0)
    small_ref[0 : small_a.shape[0], 0:128] = jnp.dot(
        total[: small_a.shape[0]], pick, precision=lax.Precision.HIGHEST, preferred_element_type=f32)
    for layer in range(LAYERS):
        base = layer * SMALL
        small_ref[layer * 8 : layer * 8 + 1, 128:512] = small_c[pl.ds(base + B_UP + f // 2, 1), aligned(core * 384, 384, 128)]
        group_row = small_c[pl.ds(base + VECS + lax.rem(f, g), 1), :]
        turned = swap_halves(jnp.broadcast_to(group_row[:, 384:512], (8, 128)))[0:1]
        queries = f < g
        small_ref[layer * 8 : layer * 8 + 1, 512:640] = jnp.where(queries, group_row[:, 0:128], group_row[:, 256:384])
        small_ref[layer * 8 : layer * 8 + 1, 640:768] = jnp.where(queries, group_row[:, 384:512], turned)
    sum_line(0, O)
    pass_on(0, U)
    pass_on(0, O)

    for i in range(1, g):
        remote(gc_send.at[i - 1], gctx.at[me], c_send.at[0, i], c_recv.at[0, i], member(i)).wait_send()
    sent_home(0)
    for layer in range(LAYERS):
        q_finish(layer)

    @pl.when(inner)
    def _():
        for layer in range(LAYERS):
            for m in range(3):
                inner_copy(layer, m).wait_send()
                out_across(layer, m).wait_send()
                out_end(layer, m).wait_send()
                out_pass(layer, m).wait_send()
                out_local(layer, m).wait()

    @pl.when(outer)
    def _():
        for layer in range(LAYERS):
            for m in range(3):
                end_copy(layer, m).wait_send()
                out_end(layer, m).wait_recv()
                out_pass(layer, m).wait_recv()

    tokens_copy.wait()
    result_copy.wait()


def run_backward(n, g, lengths, mask, vec, cot, y, fq, fo, fu, fd, stored):
    rows, span = y.shape[0], y.shape[0] * g
    any_spec = pl.BlockSpec(memory_space=pl.ANY)
    vmem = pl.BlockSpec(memory_space=pltpu.VMEM)
    bf, f32 = jnp.bfloat16, jnp.float32
    half = n // 2
    wide = g * GROUP
    dims = ((D, D), (D, FF), (FF, D))
    width = D // n
    small = SMALL * LAYERS
    shapes = [((rows, D), bf, any_spec), ((rows, D), bf, any_spec), ((SMALL_OUT + MEM_ROWS, D), f32, vmem)]
    shapes += [((LAYERS, a // n, b), bf, any_spec) for a, b in ((D, wide),) + dims]
    dma, regular = pltpu.SemaphoreType.DMA, pltpu.SemaphoreType.REGULAR
    scratch = [
        pltpu.VMEM((D, GROUP), bf), pltpu.VMEM((D, D), bf), pltpu.VMEM((2, D, D), bf), pltpu.VMEM((2, D, D), bf),
        pltpu.VMEM((2, rows, D), bf), pltpu.VMEM((2, rows, D), bf), pltpu.VMEM((span, D), bf), pltpu.VMEM((span, GROUP), bf),
        pltpu.VMEM((8, span), f32), pltpu.VMEM((g, rows, CTX), bf), pltpu.VMEM((rows, D), f32), pltpu.VMEM((rows, D), f32),
    ]
    scratch += [pltpu.VMEM(shape, bf) for shape in dims]
    scratch += [pltpu.VMEM((half, a // n, b), bf) for a, b in dims]
    scratch += [pltpu.VMEM((2, a // n // 2, b), bf) for a, b in dims]
    scratch += [pltpu.VMEM((2, a // n, b), bf) for a, b in dims]
    scratch += [pltpu.VMEM((LAYERS, a // n, b), bf) for a, b in dims]
    scratch += [pltpu.VMEM((a // n, b), bf) for a, b in dims]
    scratch += [pltpu.VMEM((a // n // 2, b), bf) for a, b in dims]
    scratch += [
        pltpu.VMEM((D, GROUP), bf), pltpu.VMEM((LAYERS, 2, width, GROUP), bf), pltpu.VMEM((LAYERS, 2, 2 * width, GROUP), bf),
        pltpu.VMEM((LAYERS, 2 * width, GROUP), bf), pltpu.VMEM((LAYERS, width, GROUP), bf),
    ]
    scratch += [
        pltpu.VMEM((rows, D), f32), pltpu.VMEM((rows, D), f32), pltpu.VMEM((D, rows), bf), pltpu.VMEM((2, rows, D), bf),
        pltpu.VMEM((span, 128), bf), pltpu.VMEM((2, rows, D), bf),
        pltpu.VMEM((g - 1, rows, CTX), bf), pltpu.VMEM((g, rows, CTX), bf), pltpu.VMEM((256, span), bf),
        pltpu.VMEM((span, 128), f32), pltpu.VMEM((span, 128), f32), pltpu.VMEM((span, 128), f32), pltpu.VMEM((span, 128), f32),
        pltpu.VMEM((span, 128), bf), pltpu.VMEM((span, GROUP), bf), pltpu.VMEM((2, rows, D), bf), pltpu.VMEM((2, rows, D), bf), pltpu.VMEM((rows, D), bf),
        pltpu.VMEM((small, D), f32), pltpu.VMEM((small, D), f32), pltpu.VMEM((small + MEM_ROWS, D), f32),
        pltpu.VMEM((small, D), f32), pltpu.VMEM((3, small, D), f32), pltpu.VMEM((g - 1, small + MEM_ROWS, D), f32),
        dma((10,)), dma((4, 2)), dma((LAYERS, 3, half)), dma((LAYERS, 3, half)), dma((LAYERS, 3, 2)), dma((LAYERS, 3, 2)),
        dma((LAYERS, 3, 2)), dma((LAYERS, 3, 2)), dma((LAYERS, 3, 2)), dma((LAYERS, 3, 2)), dma((LAYERS, 3, 3)), dma((LAYERS, 3, 3)), dma((LAYERS, 3)),
        dma((LAYERS, g)), dma((LAYERS, g)), dma((LAYERS, 3)), dma((LAYERS, 3)), dma((LAYERS, 2)), dma((LAYERS, 2)), dma((LAYERS, 2)), dma((LAYERS, 2)),
        dma((LAYERS,)), dma((LAYERS,)), dma((LAYERS, g)), dma((LAYERS, g)), dma((LAYERS,)), dma(()), dma(()),
        dma((3,)), dma((3,)), dma((g - 1,)), dma((g - 1,)), dma((2,)), dma((2,)), dma((2,)),
        regular((3,)), regular((3, 2)), regular((3, 2)), regular((3, 2)),
    ]
    return pl.pallas_call(
        functools.partial(backward_kernel, n, g),
        name="backward",
        out_shape=[jax.ShapeDtypeStruct(a, b) for a, b, _ in shapes],
        in_specs=[pl.BlockSpec(memory_space=pltpu.SMEM)] + [vmem] * 2 + [any_spec] * 14,
        out_specs=[c for _, _, c in shapes],
        scratch_shapes=scratch,
        compiler_params=pltpu.CompilerParams(
            collective_id=1, has_side_effects=True, vmem_limit_bytes=64 * 1024 * 1024 - 65536
        ),
    )(lengths, mask, vec, cot, y, fq, fo, fu, fd, *stored)


def finish_kernel(n, g, result_ref, tokens_ref, small_ref, oq_ref, oo_ref, ou_ref, od_ref, *outs):
    result, tokens, memory, q, bqv, o, bout, ga, sa, u, bup, d, bdown, gf, sf = outs
    f32 = jnp.float32
    result[...] = result_ref[...].astype(f32)
    tokens[...] = tokens_ref[...].astype(f32)
    o[...] = oo_ref[...].astype(f32)
    u[...] = ou_ref[...].astype(f32)
    d[...] = od_ref[...].astype(f32)
    low = lax.broadcasted_iota(jnp.int32, (q.shape[1], 128), 1) < 64

    def take(group, tile):
        at = group * GROUP + tile * 128
        return oq_ref[0, :, at : at + 128].astype(f32)

    def give(kind, tile, values):
        at = kind * D + tile * 128
        q[0, :, at : at + 128] = values

    ungroup_tiles(take, give, low)
    width = D // n
    memory[0] = small_ref[SMALL_OUT : SMALL_OUT + 2 * MEM, :]
    for layer in range(LAYERS):
        row = slice(layer, layer + 1)
        for ref, kind in ((bout, B_OUT), (ga, GAIN_A), (sa, SHIFT_A), (bdown, B_DOWN), (gf, GAIN_F), (sf, SHIFT_F)):
            at = layer * SMALL + kind
            ref[row, :] = small_ref[at : at + 1, 0:width]
        bup[row, :] = small_ref[layer * 8 : layer * 8 + 1, 128:512]
        bqv[row, :] = small_ref[layer * 8 : layer * 8 + 1, 512 : 512 + 2 * width]


def run_finish(n, g, result, tokens, small, oq, oo, ou, od):
    f32 = jnp.float32
    rows = result.shape[0]
    steps = 2

    def by_rows(width):
        return pl.BlockSpec((rows // (LAYERS * steps), width), lambda layer, k: (layer * steps + k, 0))

    def by_layer(depth, width):
        return pl.BlockSpec((1, depth // steps, width), lambda layer, k: (layer, k, 0))

    def whole(shape):
        return pl.BlockSpec(shape, lambda layer, k: (0,) * len(shape))

    width = D // n
    wide, deep = (LAYERS, width), FF // n
    shapes = [
        ((rows, D), by_rows(D)), ((rows, D), by_rows(D)), ((1, 2 * MEM, D), None), ((LAYERS, width, 3 * D), by_layer(width, 3 * D)),
        ((LAYERS, 2 * width), None), ((LAYERS, width, D), by_layer(width, D)), (wide, None), (wide, None), (wide, None),
        ((LAYERS, width, FF), by_layer(width, FF)), ((LAYERS, deep), None), ((LAYERS, deep, D), by_layer(deep, D)), (wide, None), (wide, None), (wide, None),
    ]
    return pl.pallas_call(
        functools.partial(finish_kernel, n, g),
        name="finish",
        grid=(LAYERS, steps),
        out_shape=[jax.ShapeDtypeStruct(shape, f32) for shape, _ in shapes],
        in_specs=[by_rows(D), by_rows(D), whole(small.shape), by_layer(width, g * GROUP), by_layer(width, D), by_layer(width, FF), by_layer(deep, D)],
        out_specs=[spec or whole(shape) for shape, spec in shapes],
        compiler_params=pltpu.CompilerParams(vmem_limit_bytes=60 * 1024 * 1024),
    )(result, tokens, small, oq, oo, ou, od)


def kernel_body(
    tokens, memory, lengths, w_qkv, b_qv, w_out, b_out, gain_attn, shift_attn, w_up, b_up, w_down, b_down, gain_ffn, shift_ffn, cotangent,
):
    n, g = lax.axis_size("fsdp"), lax.axis_size("seq")
    vectors = (b_qv, b_out, gain_attn, shift_attn, b_up, b_down, gain_ffn, shift_ffn)
    y, cot, mask, vec, fq, fo, fu, fd, *stored = run_forward(n, g, lengths, tokens, memory, vectors, cotangent, w_qkv, w_out, w_up, w_down)
    return tuple(run_finish(n, g, *run_backward(n, g, lengths, mask, vec, cot, y, fq, fo, fu, fd, stored)))


def pick_body(mesh):
    return kernel_body if mesh.shape["fsdp"] == 8 and mesh.shape["seq"] == 4 else plain_body


def solution(mesh):
    in_specs = (
        P(("fsdp", "seq"), None),
        P("fsdp", None, None),
        P("fsdp"),
        P(None, "fsdp", None),
        P(None, "fsdp"),
        P(None, "fsdp", None),
        P(None, "fsdp"),
        P(None, "fsdp"),
        P(None, "fsdp"),
        P(None, "fsdp", None),
        P(None, "fsdp"),
        P(None, "fsdp", None),
        P(None, "fsdp"),
        P(None, "fsdp"),
        P(None, "fsdp"),
        P(("fsdp", "seq"), None),
    )
    out_specs = (
        P(("fsdp", "seq"), None),
        P(("fsdp", "seq"), None),
        P("fsdp", None, None),
        P(None, "fsdp", None),
        P(None, "fsdp"),
        P(None, "fsdp", None),
        P(None, "fsdp"),
        P(None, "fsdp"),
        P(None, "fsdp"),
        P(None, "fsdp", None),
        P(None, "fsdp"),
        P(None, "fsdp", None),
        P(None, "fsdp"),
        P(None, "fsdp"),
        P(None, "fsdp"),
    )
    return jax.shard_map(pick_body(mesh), mesh=mesh, in_specs=in_specs, out_specs=out_specs, check_vma=False)
```

```python
import functools
import math

import jax
import jax.numpy as jnp
from jax import lax
from jax.experimental import pallas as pl
from jax.experimental.pallas import tpu as pltpu
from jax.sharding import PartitionSpec as P

D = 768
HEADS = 12
HD = 64
FF = 3072
MEM = 10
LAYERS = 2
GROUP = 640
CTX = 256
MEM_ROWS = 32
SMALL = 16
MESH = pl.DeviceIdType.MESH

norm_eps = 1e-12
masked_score = -1e30

B_OUT, GAIN_A, SHIFT_A, B_UP, B_DOWN, GAIN_F, SHIFT_F, VECS = 0, 1, 2, 3, 7, 8, 9, 10
WIDE = (B_OUT, GAIN_A, SHIFT_A, B_DOWN, GAIN_F, SHIFT_F)


def dot(a, b):
    return jnp.dot(a, b, preferred_element_type=jnp.float32)


def dot_t(a, b):
    return lax.dot_general(a, b, (((1,), (1,)), ((), ())), preferred_element_type=jnp.float32)


def t_dot(a, b):
    return lax.dot_general(a, b, (((0,), (0,)), ((), ())), preferred_element_type=jnp.float32)


def standardize(values):
    row_mean = jnp.mean(values, axis=-1, keepdims=True)
    centred = values - row_mean
    variance = jnp.mean(centred * centred, axis=-1, keepdims=True)
    scale = lax.rsqrt(variance + norm_eps)
    return centred * scale, scale


SHARED = ()


class Place:
    def __init__(self, n, g):
        self.n, self.g = n, g
        self.f, self.s = f, s = lax.axis_index("fsdp"), lax.axis_index("seq")
        self.core = lax.rem(f, 2)
        chip = f // 2
        self.partner = f + 1 - 2 * self.core
        self.fx = f + 2 - 4 * lax.rem(chip, 2)
        self.fy = lax.rem(f + n // 2, n)
        self.fd = lax.rem(self.fx + n // 2, n)
        self.me = 2 * lax.rem(s, 2) + self.core
        away_f, away_s = f - self.core + lax.rem(s, 2), 2 * self.core + s // 2
        self.away = self.at(away_f, away_s)
        self.back = self.at(f - self.core + s // 2, 2 * lax.rem(s, 2) + self.core)
        self.away_home = self.back
        self.stays = jnp.logical_and(away_f == f, away_s == s)

    def at(self, f, s):
        return {"fsdp": f, "seq": s}

    def on_plane(self, f):
        return self.at(f, self.s)

    def member(self, m):
        return self.at(self.f - self.core + lax.rem(m, 2), self.s - lax.rem(self.s, 2) + m // 2)

    def barrier(self):
        barrier = pltpu.get_barrier_semaphore()
        count = self.n * self.g
        here = self.f * self.g + self.s
        for j in range(1, count):
            other = lax.rem(here + j, count)
            pl.semaphore_signal(barrier, 1, device_id=self.at(other // self.g, lax.rem(other, self.g)), device_id_type=MESH)
        pl.semaphore_wait(barrier, count - 1)


def remote(src, dst, send_sem, recv_sem, device):
    return pltpu.make_async_remote_copy(
        src_ref=src, dst_ref=dst, send_sem=send_sem, recv_sem=recv_sem, device_id=device, device_id_type=MESH)


def aligned(start, size, unit):
    return pl.ds(pl.multiple_of(start, unit), size)


def swap_halves(values):
    return pltpu.roll(values, 64, 1)


def group_tiles(take, give, low):
    for pair in range(HEADS // 6):
        (q0, q1, q2), (k0, k1, k2), (v0, v1, v2) = ([take(kind, 3 * pair + t) for t in range(3)] for kind in range(3))
        first, second = 2 * pair, 2 * pair + 1
        for tile, (a, b, c) in enumerate(((q0, q1, q2), (k0, k1, k2), (v0, v1, v2))):
            give(first, tile, a)
            give(second, tile, jnp.where(low, swap_halves(b), swap_halves(c)))
        give(first, 3, jnp.where(low, q1, swap_halves(v1)))
        give(second, 3, jnp.where(low, swap_halves(q2), v2))
        give(first, 4, jnp.where(low, k1, 0.0))
        give(second, 4, jnp.where(low, swap_halves(k2), 0.0))


def ungroup_tiles(take, give, low):
    for pair in range(HEADS // 6):
        first, second = 2 * pair, 2 * pair + 1
        d0, d1, e0, e1 = take(first, 3), take(second, 3), take(first, 4), take(second, 4)
        lows = (d0, e0, swap_halves(d0))
        highs = (swap_halves(d1), swap_halves(e1), d1)
        for kind in range(3):
            turned = swap_halves(take(second, kind))
            give(kind, 3 * pair, take(first, kind))
            give(kind, 3 * pair + 1, jnp.where(low, lows[kind], turned))
            give(kind, 3 * pair + 2, jnp.where(low, turned, highs[kind]))


def selection(place, rows, length):
    slot = lax.broadcasted_iota(jnp.int32, (MEM_ROWS, rows), 0)
    position = place.s * rows + lax.broadcasted_iota(jnp.int32, (MEM_ROWS, rows), 1)
    target = jnp.where(slot < MEM, slot, length + slot)
    return jnp.where(jnp.logical_and(position == target, slot < 2 * MEM), 1.0, 0.0)


def forward_kernel(n, g, *refs):
    (
        len_ref, tok_ref, mem_ref, bqv_ref, bout_ref, ga_ref, sa_ref, bup_ref, bdown_ref, gf_ref, sf_ref, cot_ref, raw_ref, so_ref, su_ref, sd_ref,
        y_ref, cot_out, mask_in, vec, fq_ref, fo_ref, fu_ref, fd_ref, xb_out, heads_out, lse_out, ctx_out, r1_out, slope_out, act_out, r2_out,
        wq, wo, wu, wd, x_s, xb, heads, lse, ctx, r1, slope, act, r2, acc_s, nb_s, ctx_send,
        pack, packs, cat, bqkv, bup, mem_s, sq, x_out, x_in, mask_s, cot_s,
        w_send, w_recv, c_send, c_recv, own_sem, x_send, x_recv, qw_send, qw_recv, k_send_sem, k_recv_sem, save_sem,
        p_send, p_recv, r_send, r_recv, r_local,
    ) = refs
    place = Place(n, g)
    f, s, me = place.f, place.s, place.me
    rows = tok_ref.shape[0]
    span = rows * g
    bf, f32 = jnp.bfloat16, jnp.float32
    lands = (wq, wo, wu, wd)
    shards = (sq, so_ref, su_ref, sd_ref)
    fulls = (fq_ref, fo_ref, fu_ref, fd_ref)
    shard = D // n
    odd = lax.rem(s, 2)

    def spot(m, owner, part=None):
        layer, kind = divmod(m, 4)
        depth = shards[kind].shape[1]
        if part is None:
            return lands[kind].at[layer, aligned(owner * depth, depth, 32)]
        size = depth // 4 if m in SHARED else depth // 2
        return lands[kind].at[layer, aligned(owner * depth + part * size, size, 8)]

    def direct(m, way):
        layer, kind = divmod(m, 4)
        return remote(shards[kind].at[layer], spot(m, f), w_send.at[m, way], w_recv.at[m, way], place.on_plane((place.fx, place.fy)[way]))

    def relay(m, way):
        owner, target = ((place.fy, place.fx), (place.fx, place.fy))[way]
        quarter = spot(m, owner, 2 * way + odd if m in SHARED else way)
        return remote(quarter, quarter, w_send.at[m, 2 + way], w_recv.at[m, 2 + way], place.on_plane(target))

    def share(m, way):
        quarter = spot(m, place.fd, 2 * way + odd)
        return remote(quarter, quarter, w_send.at[m, 4 + way], w_recv.at[m, 4 + way], place.at(f, s + 1 - 2 * odd))

    def to_core(m, k):
        if k < 3:
            source = (spot(m, f), spot(m, place.fx), spot(m, place.fy))[k]
        else:
            source = spot(m, place.fd, (odd, 2 + odd, 1 - odd, 3 - odd)[k - 3] if m in SHARED else k - 3)
        return remote(source, source, c_send.at[m, k], c_recv.at[m, k], place.on_plane(place.partner))

    def own_copy(m):
        layer, kind = divmod(m, 4)
        return pltpu.make_async_copy(shards[kind].at[layer], spot(m, f), own_sem.at[m])

    def save_full(m):
        layer, kind = divmod(m, 4)
        return pltpu.make_async_copy(lands[kind].at[layer], fulls[kind].at[layer], own_sem.at[m])

    def launch(m):
        if m < 4 * LAYERS:
            for way in range(2):
                direct(m, way).start()

    def arrived(m):
        for way in range(2):
            direct(m, way).wait_recv()
        for way in range(2):
            relay(m, way).start()
        for k in (1, 2):
            to_core(m, k).start()

    def complete(m):
        for way in range(2):
            relay(m, way).wait_recv()
            if m in SHARED:
                share(m, way).start()
            to_core(m, 3 + way).start()

    def need(m):
        if m in SHARED:
            for way in range(2):
                share(m, way).wait_recv()
                to_core(m, 5 + way).start()
        for k in range(7 if m in SHARED else 5):
            to_core(m, k).wait_recv()
        save_full(m).start()

    def head_columns(core):
        return aligned((2 * odd + core) * GROUP, GROUP, 128)

    def q_rows(layer, owner):
        return wq.at[layer, aligned(owner * shard, shard, 32)]

    def q_direct(layer, way, other):
        core = 1 - place.core if other else place.core
        device = place.on_plane((place.fx, place.fy)[way] - place.core + core)
        return remote(sq.at[layer, :, head_columns(core)], q_rows(layer, f), qw_send.at[layer, way, other], qw_recv.at[layer, way, other], device)

    def q_relay(layer, way):
        owner, target = ((place.fy, place.fx), (place.fx, place.fy))[way]
        block = q_rows(layer, owner - place.core + way)
        return remote(block, block, qw_send.at[layer, 2, way], qw_recv.at[layer, 2, way], place.on_plane(target))

    def q_core(layer):
        return remote(
            sq.at[layer, :, head_columns(1 - place.core)], q_rows(layer, f), qw_send.at[layer, 3, 0], qw_recv.at[layer, 3, 0], place.on_plane(place.partner))

    def q_own(layer):
        return pltpu.make_async_copy(sq.at[layer, :, head_columns(place.core)], q_rows(layer, f), own_sem.at[4 * layer])

    def q_launch(layer):
        for way in range(2):
            for other in range(2):
                q_direct(layer, way, other).start()
        q_core(layer).start()
        q_own(layer).start()

    def q_arrived(layer):
        for way in range(2):
            for other in range(2):
                q_direct(layer, way, other).wait_recv()
        for way in range(2):
            q_relay(layer, way).start()

    def q_need(layer):
        for way in range(2):
            q_relay(layer, way).wait_recv()
        q_core(layer).wait_recv()
        q_own(layer).wait()
        save_full(4 * layer).start()

    saves = []

    def save(src, dst):
        copy = pltpu.make_async_copy(src, dst, save_sem.at[len(saves)])
        copy.start()
        saves.append(copy)

    length = len_ref[0]
    position = s * rows + lax.broadcasted_iota(jnp.int32, (rows, 1), 0)
    mem_s[...] = jnp.zeros_like(mem_s)
    mem_s[0 : 2 * MEM, :] = mem_ref[0]
    chosen = t_dot(selection(place, rows, length).astype(bf), mem_s[...])
    is_token = jnp.logical_and(position >= MEM, position < length + MEM)
    x_out[...] = (jnp.where(is_token, tok_ref[...].astype(f32), 0.0) + chosen).astype(bf)
    mask_s[...] = jnp.where(lax.broadcasted_iota(jnp.int32, (8, span), 1) < length + 2 * MEM, 0.0, masked_score)

    def move(k, device):
        source, target = ((x_out, x_in), (mask_s, mask_in), (cot_s, cot_out))[k]
        return remote(source, target, r_send.at[k], r_recv.at[k], device)

    place.barrier()

    @pl.when(jnp.logical_not(place.stays))
    def _():
        for k in range(2):
            move(k, place.away).start()

    low_lane = lax.broadcasted_iota(jnp.int32, (D // n, 128), 1) < 64

    def regroup(layer):
        def take(kind, tile):
            at = kind * D + tile * 128
            return raw_ref[layer, :, at : at + 128].astype(f32)

        def give(group, tile, values):
            at = group * GROUP + tile * 128
            sq[layer, :, at : at + 128] = values.astype(bf)

        group_tiles(take, give, low_lane)

    regroup(0)
    q_launch(0)
    launch(1)
    regroup(1)

    pack[...] = jnp.zeros_like(pack)
    for v, ref in enumerate((bout_ref, ga_ref, sa_ref, bdown_ref, gf_ref, sf_ref)):
        pack[2 * v : 2 * v + 2, 0 : D // n] = ref[...].astype(f32)
    for t in range(2):
        width = min(128, 2 * D // n - 128 * t)
        pack[16 + 2 * t : 18 + 2 * t, 0:width] = bqv_ref[:, 128 * t : 128 * t + width].astype(f32)
    for t in range(3):
        pack[20 + 2 * t : 22 + 2 * t, :] = bup_ref[:, 128 * t : 128 * t + 128].astype(f32)
    packs[f] = pack[...]

    def p_copy(j):
        return remote(pack, packs.at[f], p_send.at[j - 1], p_recv.at[j - 1], place.on_plane(lax.rem(f + j, n)))

    for j in range(1, n):
        p_copy(j).start()
    plain = [m for m in range(4 * LAYERS) if m % 4]
    for m in plain:
        own_copy(m).start()

    cot_s[...] = jnp.where(position < length + 2 * MEM, cot_ref[...], 0.0).astype(bf)

    @pl.when(place.stays)
    def _():
        x_in[...] = x_out[...]
        mask_in[...] = mask_s[...]
        pltpu.make_async_copy(cot_s, cot_out, r_local).start()

    for m in plain:
        own_copy(m).wait()
        to_core(m, 0).start()
    q_arrived(0)
    launch(2)
    launch(3)

    for j in range(1, n):
        owner = lax.rem(f - j + n, n)
        remote(pack, packs.at[owner], p_send.at[j - 1], p_recv.at[j - 1], place.on_plane(owner)).wait_recv()
    for j in range(n):
        cat[:, 128 * j : 128 * j + 128] = packs[j, 0:16, :].astype(bf)
        for layer in range(LAYERS):
            for t in range(3):
                at = (j % 2) * 384 + 128 * t
                row = layer * (FF // D) + j // 2
                bup[row : row + 1, at : at + 128] = packs[j, 20 + 2 * t + layer : 21 + 2 * t + layer, :]
    low_row = lax.broadcasted_iota(jnp.int32, (1, 128), 1) < 64
    for layer in range(LAYERS):
        for grp in range(g):
            row = slice(layer * g + grp, layer * g + grp + 1)
            bqkv[row, :] = jnp.zeros((1, GROUP), f32)
            bqkv[row, 0:128] = packs[grp, 16 + layer : 17 + layer, :]
            bqkv[row, 256:384] = packs[g + grp, 16 + layer : 17 + layer, :]
            turned = pltpu.roll(packs[g + grp, 16:24, :], 64, 1)[2 + layer : 3 + layer]
            bqkv[row, 384:512] = jnp.where(low_row, packs[grp, 18 + layer : 19 + layer, :], turned)
    from_lane = lax.broadcasted_iota(jnp.int32, (128, D), 0)
    to_lane = lax.broadcasted_iota(jnp.int32, (128, D), 1)
    wide = jnp.zeros((16, D), f32)
    for j in range(n):
        spread = jnp.logical_and(to_lane == from_lane + (D // n) * j, from_lane < D // n)
        wide = wide + dot(cat[:, 128 * j : 128 * j + 128], jnp.where(spread, 1.0, 0.0).astype(bf))
    vec[...] = wide

    def vector(kind, layer):
        row = 2 * WIDE.index(kind) + layer
        return vec[row : row + 1, :]

    @pl.when(jnp.logical_not(place.stays))
    def _():
        for k in range(2):
            move(k, place.back).wait_recv()

    lane = lax.broadcasted_iota(jnp.int32, (rows, 128), 1)
    x_s[...] = x_in[...].astype(f32)

    x_copies = []
    for layer in range(LAYERS):
        m0 = 4 * layer
        def x_rows(quarter):
            return xb.at[layer, aligned(quarter * rows, rows, rows)]

        across, aside = lax.rem(me + 2, g), me + 1 - 2 * place.core
        partner = place.on_plane(place.partner)
        to_across = remote(x_rows(me), x_rows(me), x_send.at[layer, 0], x_recv.at[layer, 0], place.member(across))
        to_aside = remote(x_rows(me), x_rows(me), x_send.at[layer, 1], x_recv.at[layer, 1], partner)
        pass_aside = remote(x_rows(across), x_rows(across), x_send.at[layer, 2], x_recv.at[layer, 2], partner)
        xb[layer, aligned(me * rows, rows, rows), :] = x_s[...].astype(bf)
        to_across.start()
        to_aside.start()
        x_copies.extend([to_across, to_aside, pass_aside])
        q_need(layer)

        def project(quarter):
            block = aligned(quarter * rows, rows, rows)
            heads[layer, block, :] = (dot(xb[layer, block, :], wq[layer]) + bqkv[pl.ds(layer * g + me, 1), :]).astype(bf)

        project(me)
        to_aside.wait_recv()
        project(aside)
        to_across.wait_recv()
        pass_aside.start()
        project(across)
        pass_aside.wait_recv()
        project(lax.rem(aside + 2, g))
        save(xb.at[layer], xb_out.at[layer])
        arrived(m0 + 1)
        arrived(m0 + 2)
        if layer == 0:
            q_launch(1)
        save(heads.at[layer], heads_out.at[layer])

        def c_copy(i, b):
            return remote(ctx_send.at[layer, i], ctx.at[layer, me], k_send_sem.at[layer, i], k_recv_sem.at[layer, i], place.member(b))

        def attend(i, carry):
            b = lax.rem(me + i, g)
            block = aligned(b * rows, rows, rows)
            q_a = heads[layer, block, 0:128] * bf(HD**-0.5)
            q_d = heads[layer, block, 384:512] * bf(HD**-0.5)
            zero = jnp.zeros_like(q_a)
            outs, logs = [], []
            for h in range(3):
                if h == 2:
                    scores = dot_t(q_d, heads[layer, :, 512:640])
                else:
                    part = jnp.where(lane < 64, q_a, zero) if h == 0 else jnp.where(lane < 64, zero, q_a)
                    scores = dot_t(part, heads[layer, :, 128:256])
                scores = scores + mask_in[0:1, :]
                top = jnp.max(scores, axis=-1, keepdims=True)
                exponent = jnp.exp(scores - top)
                total = jnp.sum(exponent, axis=-1, keepdims=True)
                values = heads[layer, :, 384:512] if h == 2 else heads[layer, :, 256:384]
                outs.append(dot(exponent.astype(bf), values) * (1.0 / total))
                logs.append(top + jnp.log(total))
            table = jnp.where(lane == 0, logs[0], jnp.where(lane == 1, logs[1], logs[2]))
            lse[layer, :, block] = table.T[0:8]
            first = jnp.where(lane < 64, outs[0], outs[1]).astype(bf)
            second = jnp.where(lane < 64, 0.0, outs[2]).astype(bf)

            @pl.when(i < g)
            def _():
                ctx_send[layer, i, :, 0:128] = first
                ctx_send[layer, i, :, 128:256] = second
                c_copy(i, b).start()

            @pl.when(i == g)
            def _():
                ctx[layer, me, :, 0:128] = first
                ctx[layer, me, :, 128:256] = second

            return carry

        lax.fori_loop(1, g + 1, attend, 0)
        save(lse.at[layer], lse_out.at[layer])
        complete(m0 + 1)
        if layer == 0:
            @pl.when(jnp.logical_not(place.stays))
            def _():
                move(2, place.away).start()

            q_arrived(1)
            arrived(m0 + 3)
            launch(m0 + 5)
            launch(m0 + 6)
        else:
            arrived(m0 + 3)
        need(m0 + 1)
        for i in range(1, g):
            origin = lax.rem(me - i + g, g)
            remote(ctx_send.at[layer, i], ctx.at[layer, origin], k_send_sem.at[layer, i], k_recv_sem.at[layer, i], place.member(origin)).wait_recv()
        save(ctx.at[layer], ctx_out.at[layer])

        total = x_s[...] + vector(B_OUT, layer)
        for grp in range(g):
            base = grp * 3 * HD
            total = total + dot(ctx[layer, grp, :, 0:128], wo[layer, base : base + 128, :])
            total = total + dot(ctx[layer, grp, :, 128:256], wo[layer, base + 64 : base + 192, :])
        r1[layer] = total
        save(r1.at[layer], r1_out.at[layer])
        normed = standardize(total)[0] * vector(GAIN_A, layer) + vector(SHIFT_A, layer)
        nb_s[...] = normed.astype(bf)
        acc_s[...] = normed + vector(B_DOWN, layer)
        complete(m0 + 2)
        complete(m0 + 3)
        if layer == 0:
            launch(m0 + 7)
        need(m0 + 2)
        need(m0 + 3)

        def ffn(c, carry):
            columns = aligned(c * D, D, 128)
            up = dot(nb_s[...], wu[layer, :, columns]) + bup[pl.ds(layer * (FF // D) + c, 1), :]
            cdf = 0.5 * lax.erf(up * (0.5**0.5)) + 0.5
            slope[layer, :, columns] = (cdf + up * jnp.exp(-0.5 * up * up) * (0.5 / math.pi) ** 0.5).astype(bf)
            active = (up * cdf).astype(bf)
            act[layer, :, columns] = active
            acc_s[...] += dot(active, wd[layer, columns, :])
            return carry

        lax.fori_loop(0, FF // D, ffn, 0)
        save(slope.at[layer], slope_out.at[layer])
        save(act.at[layer], act_out.at[layer])
        r2[layer] = acc_s[...]
        save(r2.at[layer], r2_out.at[layer])
        x_s[...] = standardize(acc_s[...])[0] * vector(GAIN_F, layer) + vector(SHIFT_F, layer)
    y_ref[...] = x_s[...]

    for m in plain:
        for way in range(2):
            direct(m, way).wait_send()
            relay(m, way).wait_send()
            if m in SHARED:
                share(m, way).wait_send()
        for k in range(7 if m in SHARED else 5):
            to_core(m, k).wait_send()
        save_full(m).wait()
    for layer in range(LAYERS):
        for way in range(2):
            for other in range(2):
                q_direct(layer, way, other).wait_send()
            q_relay(layer, way).wait_send()
        q_core(layer).wait_send()
        save_full(4 * layer).wait()
    for copy in x_copies:
        copy.wait_send()
    for j in range(1, n):
        p_copy(j).wait_send()
    for layer in range(LAYERS):
        for i in range(1, g):
            remote(ctx_send.at[layer, i], ctx.at[layer, me], k_send_sem.at[layer, i], k_recv_sem.at[layer, i], place.member(lax.rem(me + i, g))).wait_send()
    for copy in saves:
        copy.wait()

    @pl.when(jnp.logical_not(place.stays))
    def _():
        for k in range(3):
            move(k, place.away).wait_send()
        move(2, place.back).wait_recv()

    @pl.when(place.stays)
    def _():
        pltpu.make_async_copy(cot_s, cot_out, r_local).wait()


def run_forward(n, g, lengths, tokens, memory, vectors, cotangent, sq, so, su, sd):
    rows, span = tokens.shape[0], tokens.shape[0] * g
    any_spec = pl.BlockSpec(memory_space=pl.ANY)
    vmem = pl.BlockSpec(memory_space=pltpu.VMEM)
    bf, f32 = jnp.bfloat16, jnp.float32
    shapes = [
        ((rows, D), f32, vmem),
        ((rows, D), bf, any_spec),
        ((8, span), f32, vmem),
        ((16, D), f32, vmem),
        ((LAYERS, D, GROUP), bf, any_spec),
        ((LAYERS, D, D), bf, any_spec),
        ((LAYERS, D, FF), bf, any_spec),
        ((LAYERS, FF, D), bf, any_spec),
        ((LAYERS, span, D), bf, any_spec),
        ((LAYERS, span, GROUP), bf, any_spec),
        ((LAYERS, 8, span), f32, any_spec),
        ((LAYERS, g, rows, CTX), bf, any_spec),
        ((LAYERS, rows, D), f32, any_spec),
        ((LAYERS, rows, FF), bf, any_spec),
        ((LAYERS, rows, FF), bf, any_spec),
        ((LAYERS, rows, D), f32, any_spec),
    ]
    dma = pltpu.SemaphoreType.DMA
    return pl.pallas_call(
        functools.partial(forward_kernel, n, g),
        name="forward",
        out_shape=[jax.ShapeDtypeStruct(a, b) for a, b, _ in shapes],
        in_specs=[pl.BlockSpec(memory_space=pltpu.SMEM)] + [vmem] * 12 + [any_spec] * 3,
        out_specs=[c for _, _, c in shapes],
        scratch_shapes=[
            pltpu.VMEM((LAYERS, D, GROUP), bf),
            pltpu.VMEM((LAYERS, D, D), bf),
            pltpu.VMEM((LAYERS, D, FF), bf),
            pltpu.VMEM((LAYERS, FF, D), bf),
            pltpu.VMEM((rows, D), f32),
            pltpu.VMEM((LAYERS, span, D), bf),
            pltpu.VMEM((LAYERS, span, GROUP), bf),
            pltpu.VMEM((LAYERS, 8, span), f32),
            pltpu.VMEM((LAYERS, g, rows, CTX), bf),
            pltpu.VMEM((LAYERS, rows, D), f32),
            pltpu.VMEM((LAYERS, rows, FF), bf),
            pltpu.VMEM((LAYERS, rows, FF), bf),
            pltpu.VMEM((LAYERS, rows, D), f32),
            pltpu.VMEM((rows, D), f32),
            pltpu.VMEM((rows, D), bf),
            pltpu.VMEM((LAYERS, g, rows, CTX), bf),
            pltpu.VMEM((32, 128), f32),
            pltpu.VMEM((n, 32, 128), f32),
            pltpu.VMEM((16, n * 128), bf),
            pltpu.VMEM((LAYERS * g, GROUP), f32),
            pltpu.VMEM((LAYERS * (FF // D), D), f32),
            pltpu.VMEM((MEM_ROWS, D), bf),
            pltpu.VMEM((LAYERS, D // n, g * GROUP), bf),
            pltpu.VMEM((rows, D), bf),
            pltpu.VMEM((rows, D), bf),
            pltpu.VMEM((8, span), f32),
            pltpu.VMEM((rows, D), bf),
            dma((4 * LAYERS, 6)),
            dma((4 * LAYERS, 6)),
            dma((4 * LAYERS, 7)),
            dma((4 * LAYERS, 7)),
            dma((4 * LAYERS,)),
            dma((LAYERS, 3)),
            dma((LAYERS, 3)),
            dma((LAYERS, 4, 2)),
            dma((LAYERS, 4, 2)),
            dma((LAYERS, g)),
            dma((LAYERS, g)),
            dma((8 * LAYERS,)),
            dma((n - 1,)),
            dma((n - 1,)),
            dma((3,)),
            dma((3,)),
            dma(()),
        ],
        compiler_params=pltpu.CompilerParams(
            collective_id=0, has_side_effects=True, vmem_limit_bytes=62 * 1024 * 1024
        ),
    )(lengths, tokens, memory, *vectors, cotangent, sq, so, su, sd)


def norm_rows(values, gain_vec, shift_vec):
    row_mean = jnp.mean(values, axis=-1, keepdims=True)
    centred = values - row_mean
    variance = jnp.mean(centred * centred, axis=-1, keepdims=True)
    return centred * lax.rsqrt(variance + norm_eps) * gain_vec + shift_vec


def gelu_exact(values):
    return jax.nn.gelu(values, approximate=False)


def gather_layer(stacks, layer_index):
    (
        w_qkv,
        b_qv,
        w_out,
        b_out,
        gain_attn,
        shift_attn,
        w_up,
        b_up,
        w_down,
        b_down,
        gain_ffn,
        shift_ffn,
    ) = tuple((stacked[layer_index] for stacked in stacks))
    return (
        lax.all_gather(w_qkv, "fsdp", axis=0, tiled=True),
        lax.all_gather(b_qv, "fsdp", axis=0, tiled=True),
        lax.all_gather(w_out, "fsdp", axis=0, tiled=True),
        lax.all_gather(b_out, "fsdp", axis=0, tiled=True),
        lax.all_gather(gain_attn, "fsdp", axis=0, tiled=True),
        lax.all_gather(shift_attn, "fsdp", axis=0, tiled=True),
        lax.all_gather(w_up, "fsdp", axis=0, tiled=True),
        lax.all_gather(b_up, "fsdp", axis=0, tiled=True),
        lax.all_gather(w_down, "fsdp", axis=0, tiled=True),
        lax.all_gather(b_down, "fsdp", axis=0, tiled=True),
        lax.all_gather(gain_ffn, "fsdp", axis=0, tiled=True),
        lax.all_gather(shift_ffn, "fsdp", axis=0, tiled=True),
    )


def attend_forward(queries, keys_all, values_all, key_live):
    total_rows, local_heads = (queries.shape[0], queries.shape[1])
    block_rows = math.gcd(total_rows, 512)
    block_count = total_rows // block_rows
    score_scale = HD ** (-0.5)

    def one_block(query_block):
        scores = (
            jnp.einsum("qhd,khd->hqk", query_block, keys_all, preferred_element_type=jnp.float32)
            * score_scale
        )
        scores = jnp.where(key_live[None, None, :], scores, masked_score)
        top_score = jnp.max(scores, axis=-1, keepdims=True)
        exponent = jnp.exp(scores - top_score)
        row_total = jnp.sum(exponent, axis=-1, keepdims=True)
        probability = (exponent / row_total).astype(jnp.bfloat16)
        context = jnp.einsum(
            "hqk,khd->qhd", probability, values_all, preferred_element_type=jnp.float32
        )
        return (context.astype(jnp.bfloat16), (top_score + jnp.log(row_total))[..., 0])

    blocks = queries.reshape(block_count, block_rows, local_heads, HD)
    context, log_total = lax.map(one_block, blocks)
    return (context.reshape(total_rows, local_heads, HD), log_total)


def attend_backward(queries, keys_all, values_all, grad_context, log_total, key_live):
    total_rows, local_heads = (queries.shape[0], queries.shape[1])
    block_rows = math.gcd(total_rows, 512)
    block_count = total_rows // block_rows
    score_scale = HD ** (-0.5)

    def one_block(running, inputs):
        grad_keys, grad_values = running
        query_block, grad_block, log_block = inputs
        scores = (
            jnp.einsum("qhd,khd->hqk", query_block, keys_all, preferred_element_type=jnp.float32)
            * score_scale
        )
        scores = jnp.where(key_live[None, None, :], scores, masked_score)
        probability = jnp.exp(scores - log_block[:, :, None])
        grad_prob = jnp.einsum(
            "qhd,khd->hqk", grad_block, values_all, preferred_element_type=jnp.float32
        )
        grad_values = grad_values + jnp.einsum(
            "hqk,qhd->khd",
            probability.astype(jnp.bfloat16),
            grad_block,
            preferred_element_type=jnp.float32,
        )
        inner_sum = jnp.sum(grad_prob * probability, axis=-1, keepdims=True)
        grad_scores = (probability * (grad_prob - inner_sum)).astype(jnp.bfloat16)
        grad_query = (
            jnp.einsum("hqk,khd->qhd", grad_scores, keys_all, preferred_element_type=jnp.float32)
            * score_scale
        )
        grad_keys = (
            grad_keys
            + jnp.einsum(
                "hqk,qhd->khd", grad_scores, query_block, preferred_element_type=jnp.float32
            )
            * score_scale
        )
        return ((grad_keys, grad_values), grad_query)

    zero_keys = jnp.zeros((total_rows, local_heads, HD), jnp.float32)
    shaped = (
        queries.reshape(block_count, block_rows, local_heads, HD),
        grad_context.reshape(block_count, block_rows, local_heads, HD),
        log_total,
    )
    (grad_keys, grad_values), grad_queries = lax.scan(one_block, (zero_keys, zero_keys), shaped)
    return (grad_queries.reshape(total_rows, local_heads, HD), grad_keys, grad_values)


def layer_forward(hidden, weights, key_live):
    (
        w_qkv,
        b_qv,
        w_out,
        b_out,
        gain_attn,
        shift_attn,
        w_up,
        b_up,
        w_down,
        b_down,
        gain_ffn,
        shift_ffn,
    ) = weights
    local_rows = hidden.shape[0]
    groups = lax.axis_size("seq")
    local_heads = HEADS // groups
    bias_qv = b_qv.astype(jnp.float32)
    bias_full = jnp.concatenate([bias_qv[:D], jnp.zeros((D,), jnp.float32), bias_qv[D:]])
    hidden_low = hidden.astype(jnp.bfloat16)
    projected = (jnp.dot(hidden_low, w_qkv, preferred_element_type=jnp.float32) + bias_full).astype(
        jnp.bfloat16
    )
    by_head = lax.all_to_all(
        projected.reshape(local_rows, 3, groups, local_heads, HD),
        "seq",
        split_axis=2,
        concat_axis=0,
        tiled=True,
    )
    context, log_total = attend_forward(
        by_head[:, 0, 0], by_head[:, 1, 0], by_head[:, 2, 0], key_live
    )
    ctx_rows = lax.all_to_all(
        context.reshape(local_rows * groups, 1, local_heads, HD),
        "seq",
        split_axis=0,
        concat_axis=1,
        tiled=True,
    ).reshape(local_rows, D)
    attended = jnp.dot(ctx_rows, w_out, preferred_element_type=jnp.float32) + b_out.astype(
        jnp.float32
    )
    residual_one = hidden + attended
    normed = norm_rows(residual_one, gain_attn.astype(jnp.float32), shift_attn.astype(jnp.float32))
    pre_gelu = jnp.dot(
        normed.astype(jnp.bfloat16), w_up, preferred_element_type=jnp.float32
    ) + b_up.astype(jnp.float32)
    active = gelu_exact(pre_gelu).astype(jnp.bfloat16)
    branch_out = jnp.dot(active, w_down, preferred_element_type=jnp.float32) + b_down.astype(
        jnp.float32
    )
    residual_two = normed + branch_out
    output = norm_rows(residual_two, gain_ffn.astype(jnp.float32), shift_ffn.astype(jnp.float32))
    stored = (
        hidden,
        by_head,
        log_total,
        ctx_rows,
        residual_one,
        normed,
        pre_gelu,
        active,
        residual_two,
    )
    return (output, stored)


def layer_backward(grad_output, weights, stored, key_live):
    (
        w_qkv,
        b_qv,
        w_out,
        b_out,
        gain_attn,
        shift_attn,
        w_up,
        b_up,
        w_down,
        b_down,
        gain_ffn,
        shift_ffn,
    ) = weights
    hidden, by_head, log_total, ctx_rows, residual_one, normed, pre_gelu, active, residual_two = (
        stored
    )
    local_rows = hidden.shape[0]
    groups = lax.axis_size("seq")
    local_heads = HEADS // groups
    ffn_pull = jax.vjp(
        norm_rows, residual_two, gain_ffn.astype(jnp.float32), shift_ffn.astype(jnp.float32)
    )[1]
    grad_two, grad_gain_ffn, grad_shift_ffn = ffn_pull(grad_output)
    grad_branch = grad_two.astype(jnp.bfloat16)
    grad_b_down = jnp.sum(grad_branch.astype(jnp.float32), axis=0)
    grad_w_down = jnp.einsum("rf,rd->fd", active, grad_branch, preferred_element_type=jnp.float32)
    grad_active = jnp.einsum("rd,fd->rf", grad_branch, w_down, preferred_element_type=jnp.float32)
    gelu_pull = jax.vjp(gelu_exact, pre_gelu)[1]
    grad_pre = gelu_pull(grad_active)[0].astype(jnp.bfloat16)
    grad_b_up = jnp.sum(grad_pre.astype(jnp.float32), axis=0)
    normed_low = normed.astype(jnp.bfloat16)
    grad_w_up = jnp.einsum("rd,rf->df", normed_low, grad_pre, preferred_element_type=jnp.float32)
    grad_normed = (
        jnp.einsum("rf,df->rd", grad_pre, w_up, preferred_element_type=jnp.float32) + grad_two
    )
    attn_pull = jax.vjp(
        norm_rows, residual_one, gain_attn.astype(jnp.float32), shift_attn.astype(jnp.float32)
    )[1]
    grad_one, grad_gain_attn, grad_shift_attn = attn_pull(grad_normed)
    grad_attended = grad_one.astype(jnp.bfloat16)
    grad_b_out = jnp.sum(grad_attended.astype(jnp.float32), axis=0)
    grad_w_out = jnp.einsum(
        "rk,rd->kd", ctx_rows, grad_attended, preferred_element_type=jnp.float32
    )
    grad_ctx = jnp.einsum(
        "rd,kd->rk", grad_attended, w_out, preferred_element_type=jnp.float32
    ).astype(jnp.bfloat16)
    grad_heads = lax.all_to_all(
        grad_ctx.reshape(local_rows, groups, local_heads, HD),
        "seq",
        split_axis=1,
        concat_axis=0,
        tiled=True,
    )
    grad_queries, grad_keys, grad_values = attend_backward(
        by_head[:, 0, 0], by_head[:, 1, 0], by_head[:, 2, 0], grad_heads[:, 0], log_total, key_live
    )
    grad_stack = jnp.stack([grad_queries, grad_keys, grad_values], axis=1).astype(jnp.bfloat16)[
        :, :, None
    ]
    grad_projected = lax.all_to_all(
        grad_stack, "seq", split_axis=0, concat_axis=2, tiled=True
    ).reshape(local_rows, 3 * D)
    grad_sums = jnp.sum(grad_projected.astype(jnp.float32), axis=0)
    grad_b_qv = jnp.concatenate([grad_sums[:D], grad_sums[2 * D :]])
    hidden_low = hidden.astype(jnp.bfloat16)
    grad_w_qkv = jnp.einsum(
        "rd,re->de", hidden_low, grad_projected, preferred_element_type=jnp.float32
    )
    grad_hidden = (
        jnp.einsum("re,de->rd", grad_projected, w_qkv, preferred_element_type=jnp.float32)
        + grad_one
    )
    weight_grads = (
        grad_w_qkv,
        grad_b_qv,
        grad_w_out,
        grad_b_out,
        grad_gain_attn,
        grad_shift_attn,
        grad_w_up,
        grad_b_up,
        grad_w_down,
        grad_b_down,
        grad_gain_ffn,
        grad_shift_ffn,
    )
    return (grad_hidden, weight_grads)


def fsdp_layer_sum(weight_grads):
    (
        grad_w_qkv,
        grad_b_qv,
        grad_w_out,
        grad_b_out,
        grad_gain_attn,
        grad_shift_attn,
        grad_w_up,
        grad_b_up,
        grad_w_down,
        grad_b_down,
        grad_gain_ffn,
        grad_shift_ffn,
    ) = weight_grads
    return (
        lax.psum_scatter(grad_w_qkv.astype(jnp.bfloat16), "fsdp", scatter_dimension=0, tiled=True),
        lax.psum_scatter(grad_b_qv.astype(jnp.bfloat16), "fsdp", scatter_dimension=0, tiled=True),
        lax.psum_scatter(grad_w_out.astype(jnp.bfloat16), "fsdp", scatter_dimension=0, tiled=True),
        lax.psum_scatter(grad_b_out.astype(jnp.bfloat16), "fsdp", scatter_dimension=0, tiled=True),
        lax.psum_scatter(grad_gain_attn.astype(jnp.bfloat16), "fsdp", scatter_dimension=0, tiled=True),
        lax.psum_scatter(grad_shift_attn.astype(jnp.bfloat16), "fsdp", scatter_dimension=0, tiled=True),
        lax.psum_scatter(grad_w_up.astype(jnp.bfloat16), "fsdp", scatter_dimension=0, tiled=True),
        lax.psum_scatter(grad_b_up.astype(jnp.bfloat16), "fsdp", scatter_dimension=0, tiled=True),
        lax.psum_scatter(grad_w_down.astype(jnp.bfloat16), "fsdp", scatter_dimension=0, tiled=True),
        lax.psum_scatter(grad_b_down.astype(jnp.bfloat16), "fsdp", scatter_dimension=0, tiled=True),
        lax.psum_scatter(grad_gain_ffn.astype(jnp.bfloat16), "fsdp", scatter_dimension=0, tiled=True),
        lax.psum_scatter(grad_shift_ffn.astype(jnp.bfloat16), "fsdp", scatter_dimension=0, tiled=True),
    )


def seq_total_sum(shard_grads, grad_memory):
    (
        grad_w_qkv,
        grad_b_qv,
        grad_w_out,
        grad_b_out,
        grad_gain_attn,
        grad_shift_attn,
        grad_w_up,
        grad_b_up,
        grad_w_down,
        grad_b_down,
        grad_gain_ffn,
        grad_shift_ffn,
    ) = shard_grads
    pieces = (
        lax.psum_scatter(
            grad_w_qkv.astype(jnp.bfloat16), "seq", scatter_dimension=2, tiled=True
        ).astype(jnp.float32),
        lax.psum_scatter(
            grad_w_out.astype(jnp.bfloat16), "seq", scatter_dimension=2, tiled=True
        ).astype(jnp.float32),
        lax.psum_scatter(
            grad_w_up.astype(jnp.bfloat16), "seq", scatter_dimension=2, tiled=True
        ).astype(jnp.float32),
        lax.psum_scatter(
            grad_w_down.astype(jnp.bfloat16), "seq", scatter_dimension=2, tiled=True
        ).astype(jnp.float32),
    )
    matrices = (
        lax.all_gather(pieces[0].astype(jnp.bfloat16), "seq", axis=2, tiled=True).astype(
            jnp.float32
        ),
        lax.all_gather(pieces[1].astype(jnp.bfloat16), "seq", axis=2, tiled=True).astype(
            jnp.float32
        ),
        lax.all_gather(pieces[2].astype(jnp.bfloat16), "seq", axis=2, tiled=True).astype(
            jnp.float32
        ),
        lax.all_gather(pieces[3].astype(jnp.bfloat16), "seq", axis=2, tiled=True).astype(
            jnp.float32
        ),
    )
    smalls = (
        lax.psum(grad_b_qv.astype(jnp.bfloat16), "seq").astype(jnp.float32),
        lax.psum(grad_b_out.astype(jnp.bfloat16), "seq").astype(jnp.float32),
        lax.psum(grad_gain_attn.astype(jnp.bfloat16), "seq").astype(jnp.float32),
        lax.psum(grad_shift_attn.astype(jnp.bfloat16), "seq").astype(jnp.float32),
        lax.psum(grad_b_up.astype(jnp.bfloat16), "seq").astype(jnp.float32),
        lax.psum(grad_b_down.astype(jnp.bfloat16), "seq").astype(jnp.float32),
        lax.psum(grad_gain_ffn.astype(jnp.bfloat16), "seq").astype(jnp.float32),
        lax.psum(grad_shift_ffn.astype(jnp.bfloat16), "seq").astype(jnp.float32),
        lax.psum(grad_memory.astype(jnp.bfloat16), "seq").astype(jnp.float32),
    )
    weights_sum = (
        matrices[0],
        smalls[0],
        matrices[1],
        smalls[1],
        smalls[2],
        smalls[3],
        matrices[2],
        smalls[4],
        matrices[3],
        smalls[5],
        smalls[6],
        smalls[7],
    )
    return (weights_sum, smalls[8])


def plain_body(
    tokens,
    memory,
    lengths,
    w_qkv,
    b_qv,
    w_out,
    b_out,
    gain_attn,
    shift_attn,
    w_up,
    b_up,
    w_down,
    b_down,
    gain_ffn,
    shift_ffn,
    cotangent,
):
    local_rows = tokens.shape[0]
    groups = lax.axis_size("seq")
    seq_place = lax.axis_index("seq")
    length = lengths[0]
    positions = seq_place * local_rows + jnp.arange(local_rows, dtype=jnp.int32)
    key_live = jnp.arange(local_rows * groups, dtype=jnp.int32) < length + 2 * MEM
    row_live = (positions < length + 2 * MEM)[:, None]
    token_live = ((positions >= MEM) & (positions < length + MEM))[:, None]
    memory_slots = jnp.arange(2 * MEM, dtype=jnp.int32)
    targets = jnp.where(memory_slots < MEM, memory_slots, length + memory_slots)
    select = positions[:, None] == targets[None, :]
    hidden = jnp.where(token_live, tokens.astype(jnp.float32), 0.0) + jnp.dot(
        select.astype(jnp.bfloat16), memory[0], preferred_element_type=jnp.float32
    )
    stacks = (
        w_qkv,
        b_qv,
        w_out,
        b_out,
        gain_attn,
        shift_attn,
        w_up,
        b_up,
        w_down,
        b_down,
        gain_ffn,
        shift_ffn,
    )
    kept = []
    for layer_index in range(LAYERS):
        weights = gather_layer(stacks, layer_index)
        hidden, stored = layer_forward(hidden, weights, key_live)
        kept.append((weights, stored))
    result = jnp.where(row_live, hidden, 0.0)
    grad_hidden = jnp.where(row_live, cotangent, 0.0)
    collected = []
    for layer_index in reversed(range(LAYERS)):
        weights, stored = kept[layer_index]
        grad_hidden, weight_grads = layer_backward(grad_hidden, weights, stored, key_live)
        collected.insert(0, fsdp_layer_sum(weight_grads))
    stacked_grads = tuple((jnp.stack(member) for member in zip(*collected)))
    grad_tokens = jnp.where(token_live, grad_hidden, 0.0)
    grad_memory = jnp.dot(
        select.astype(jnp.float32).T, grad_hidden, precision=lax.Precision.HIGHEST
    )[None]
    summed, memory_sum = seq_total_sum(stacked_grads, grad_memory)
    return (result, grad_tokens, memory_sum) + tuple(summed)


SMALL_OUT = SMALL * LAYERS


def backward_kernel(n, g, *refs):
    (
        len_ref, mask_ref, vec, cot_ref, y_ref, fq_ref, fo_ref, fu_ref, fd_ref, xb_ref, heads_ref, lse_ref, ctx_ref, r1_ref, slope_ref, act_ref, r2_ref,
        result_ref, tokens_ref, small_ref, memory_ref, oq_ref, oo_ref, ou_ref, od_ref,
        wq, wo, wu, wd, slope, act, xb, hd, lse, ctx, r1, r2,
        p_o, p_u, p_d, pair_o, pair_u, pair_d, half_o, half_u, half_d, plane_o, plane_u, plane_d,
        sum_o, sum_u, sum_d, whole_o, whole_u, whole_d, part_o, part_u, part_d, p_q, half_q, plane_q, sum_q, line_q, done_q,
        gx, gn, norm_t, low, live, home, gc_send, gctx, key_t, acc_k, acc_v, acc_d, acc_e, grad_p, aside_send, aside_in, across_in,
        small_a, small_b, small_c, land_a, land_b, land_c, memory_part, memory_land,
        load_sem, stream_sem, pair_send, pair_recv, up_send, up_recv, half_send, half_recv, uh_send, uh_recv, plane_send, plane_recv, z_send, z_recv, out_send, out_recv, out_own,
        c_send, c_recv, x_send, x_recv, qh_send, qh_recv, qp_send, qp_recv, ql_send, ql_recv, qo_send, qo_recv, qo_own, sa_send, sa_recv, sb_send, sb_recv, sc_send, sc_recv, home_send, home_recv, store_sem,
        pair_credit, half_credit, plane_credit, z_credit,
    ) = refs
    place = Place(n, g)
    f, s, me, core = place.f, place.s, place.me, place.core
    rows = gx.shape[0]
    span = rows * g
    half = n // 2
    partner = place.on_plane(place.partner)
    bf, f32 = jnp.bfloat16, jnp.float32
    pairs = (pair_o, pair_u, pair_d)
    halves = (half_o, half_u, half_d)
    planes = (plane_o, plane_u, plane_d)
    sums = (sum_o, sum_u, sum_d)
    wholes = (whole_o, whole_u, whole_d)
    inners = (part_o, part_u, part_d)
    outs = (oo_ref, ou_ref, od_ref)
    O, U, DN = 0, 1, 2
    width = D // n
    inner = jnp.logical_and(s > 0, s < g - 1)
    outer = jnp.logical_not(inner)
    side = s // 2
    inner_chip = place.at(f, 1 + side)
    other_inner = place.at(f, 3 - s)
    end_chip = place.at(f, 3 * side)

    def member(i):
        return place.member(lax.rem(me + i, g))

    def depth(m):
        return pairs[m].shape[1]

    def part(layer, m):
        return (p_o.at[layer], p_u.at[layer], p_d)[m]

    def part_rows(layer, m, owner):
        return part(layer, m).at[aligned(owner * depth(m), depth(m), 32)]

    def part_half(layer, m, owner, which):
        return part(layer, m).at[aligned(owner * depth(m) + which * (depth(m) // 2), depth(m) // 2, 16)]

    def half_rows(ref, m, which):
        return ref.at[aligned(which * (depth(m) // 2), depth(m) // 2, 16)]

    def chunk(c):
        bit = lax.rem(f // 2 + 3 - c, 2)
        return bit + 2 * lax.rem(f // 4 + (3 - c) // 2, 2)

    def ff_columns(c):
        return aligned(chunk(c) * D, D, 128)

    names = {}

    def load(name, src, dst):
        index = {"xb": 0, "hd": 1, "lse": 2, "ctx": 3, "r1": 4, "r2": 5, "wq": 6, "wo": 7, "cot": 8, "y": 9}[name]
        copy = pltpu.make_async_copy(src, dst, load_sem.at[index])
        copy.start()
        names[name] = copy

    def loaded(name):
        names.pop(name).wait()

    def stream(layer, c, slot):
        columns = ff_columns(c)
        return [
            pltpu.make_async_copy(fd_ref.at[layer, columns, :], wd.at[slot], stream_sem.at[0, slot]),
            pltpu.make_async_copy(fu_ref.at[layer, :, columns], wu.at[slot], stream_sem.at[1, slot]),
            pltpu.make_async_copy(slope_ref.at[layer, :, columns], slope.at[slot], stream_sem.at[2, slot]),
            pltpu.make_async_copy(act_ref.at[layer, :, columns], act.at[slot], stream_sem.at[3, slot]),
        ]

    last = LAYERS - 1
    for copy in stream(last, 0, 0):
        copy.start()
    load("cot", cot_ref, low.at[0])
    load("y", y_ref, gn)
    load("r2", r2_ref.at[last], r2)
    load("r1", r1_ref.at[last], r1)
    load("wo", fo_ref.at[last], wo)
    load("ctx", ctx_ref.at[last], ctx)
    load("hd", heads_ref.at[last], hd)
    load("lse", lse_ref.at[last], lse)
    load("xb", xb_ref.at[last], xb)
    load("wq", fq_ref.at[last], wq)

    place.barrier()

    def pair_copy(layer, m, c):
        return remote(part_rows(layer, m, 2 * c + 1 - core), pairs[m].at[c], pair_send.at[layer, m, c], pair_recv.at[layer, m, c], partner)

    def up_block(layer, c, start, count):
        return p_u.at[layer, aligned(start, count, 16), ff_columns(c)]

    def up_pair(layer, c, k):
        source = up_block(layer, c, (2 * k + 1 - core) * width, width)
        return remote(source, pair_u.at[k, :, ff_columns(c)], up_send.at[layer, c, k], up_recv.at[layer, c, k], partner)

    def up_half(layer, c, way):
        source = up_block(layer, c, place.fd * width + way * (width // 2), width // 2)
        device = place.on_plane((place.fx, place.fy)[way])
        return remote(source, half_u.at[way, :, ff_columns(c)], uh_send.at[layer, c, way], uh_recv.at[layer, c, way], device)

    def half_copy(layer, m, way):
        device = place.on_plane((place.fx, place.fy)[way])
        return remote(part_half(layer, m, place.fd, way), halves[m].at[way], half_send.at[layer, m, way], half_recv.at[layer, m, way], device)

    def plane_copy(layer, m, way):
        owner = (place.fx, place.fy)[way]
        return remote(part_rows(layer, m, owner), planes[m].at[way], plane_send.at[layer, m, way], plane_recv.at[layer, m, way], place.on_plane(owner))

    def end_copy(layer, m, h):
        return remote(half_rows(sums[m].at[layer], m, h), half_rows(wholes[m].at[layer], m, h), z_send.at[layer, m, h], z_recv.at[layer, m, h], inner_chip)

    def inner_copy(layer, m, h):
        return remote(half_rows(sums[m].at[layer], m, h), half_rows(inners[m], m, h), z_send.at[layer, m, 2 + h], z_recv.at[layer, m, 2 + h], other_inner)

    def out_end(layer, m, h):
        return remote(half_rows(wholes[m].at[layer], m, h), half_rows(outs[m].at[layer], m, h), out_send.at[layer, m, h], out_recv.at[layer, m, h], end_chip)

    def out_local(layer, m, h):
        return pltpu.make_async_copy(half_rows(wholes[m].at[layer], m, h), half_rows(outs[m].at[layer], m, h), out_own.at[layer, m, h])

    def pair_ready(layer, m):
        if layer != last:
            pl.semaphore_wait(pair_credit.at[m], 1)

    def each(count, step, body):
        def go(k, carry):
            body(k * step)
            return carry

        lax.fori_loop(0, count // step, go, 0)

    def add(target, start, source, count):
        step = 48 if count % 32 else 32

        def body(at):
            mine, theirs = aligned(start + at, step, 16), aligned(at, step, 16)
            target[mine, :] = target[mine, :] + source[theirs, :]

        each(count, step, body)

    def half_start(layer, m):
        for way in range(2):
            if layer != last:
                pl.semaphore_wait(half_credit.at[m, way], 1)
            half_copy(layer, m, way).start()

    def pair_used(layer, m):
        if layer:
            pl.semaphore_signal(pair_credit.at[m], 1, device_id=partner, device_id_type=MESH)

    def sum_pair(layer, m):
        for c in range(half):
            pair_copy(layer, m, c).wait_recv()
        for c in range(half):
            pair_copy(layer, m, c).wait_send()
        for owner in (place.fd, place.fx, place.fy, f):
            add(part(layer, m), owner * depth(m), pairs[m].at[owner // 2], depth(m))
            if owner is place.fd:
                half_start(layer, m)
        pair_used(layer, m)

    def sum_chunk(layer, c):
        now = chunk(c)
        pair_copy(layer, DN, now).wait_recv()
        pair_copy(layer, DN, now).wait_send()
        add(p_d, (2 * now + core) * depth(DN), pair_d.at[now], depth(DN))

        @pl.when(c == 0)
        def _():
            half_start(layer, DN)

        for k in range(half):
            up_pair(layer, c, k).wait_recv()
            up_pair(layer, c, k).wait_send()
            columns = ff_columns(c)
            mine = aligned((2 * k + core) * width, width, 32)
            p_u[layer, mine, columns] = p_u[layer, mine, columns] + pair_u[k, :, columns]
        if layer != last:
            @pl.when(c == 0)
            def _():
                for way in range(2):
                    pl.semaphore_wait(half_credit.at[U, way], 1)

        for way in range(2):
            up_half(layer, c, way).start()

    def sum_half(layer, m):
        for way in range(2):
            if m == U:
                for c in range(half):
                    up_half(layer, c, way).wait_recv()
            else:
                half_copy(layer, m, way).wait_recv()
            owner = (place.fy, place.fx)[way]
            add(part(layer, m), owner * depth(m) + way * (depth(m) // 2), halves[m].at[way], depth(m) // 2)
            if layer != last:
                pl.semaphore_wait(plane_credit.at[m, 1 - way], 1)
            plane_copy(layer, m, 1 - way).start()
        for way in range(2):
            if layer:
                pl.semaphore_signal(
                    half_credit.at[m, way], 1, device_id=place.on_plane((place.fx, place.fy)[way]), device_id_type=MESH)
            if m == U:
                for c in range(half):
                    up_half(layer, c, way).wait_send()
            else:
                half_copy(layer, m, way).wait_send()

    def sum_plane(layer, m):
        for way in range(2):
            plane_copy(layer, m, way).wait_recv()

        def body(at):
            mine, theirs = aligned(f * depth(m) + at, 32, 32), aligned(at, 32, 32)
            total = part(layer, m)[mine, :].astype(f32) + planes[m][0, theirs, :].astype(f32) + planes[m][1, theirs, :].astype(f32)
            sums[m][layer, theirs, :] = total.astype(bf)

        each(depth(m), 32, body)
        for way in range(2):
            if layer:
                pl.semaphore_signal(
                    plane_credit.at[m, way], 1, device_id=place.on_plane((place.fx, place.fy)[way]), device_id_type=MESH)
            plane_copy(layer, m, way).wait_send()

        @pl.when(outer)
        def _():
            for h in range(2):
                end_copy(layer, m, h).start()

    def sum_end(layer, m):
        @pl.when(inner)
        def _():
            if layer != last:
                pl.semaphore_wait(z_credit.at[m, 1], 1)
            for h in range(2):
                end_copy(layer, m, h).wait_recv()
                add(sums[m].at[layer], h * (depth(m) // 2), half_rows(wholes[m].at[layer], m, h), depth(m) // 2)
                inner_copy(layer, m, h).start()

    def sum_line(layer, m):
        @pl.when(inner)
        def _():
            for h in range(2):
                inner_copy(layer, m, h).wait_recv()

                def body(at, h=h):
                    rows_now = aligned(h * (depth(m) // 2) + at, 16, 16)
                    wholes[m][layer, rows_now, :] = sums[m][layer, rows_now, :] + inners[m][rows_now, :]

                each(depth(m) // 2, 16, body)
                out_end(layer, m, h).start()
                out_local(layer, m, h).start()
            if layer:
                pl.semaphore_signal(z_credit.at[m, 1], 1, device_id=other_inner, device_id_type=MESH)

    def line_done(layer, m):
        @pl.when(inner)
        def _():
            for h in range(2):
                inner_copy(layer, m, h).wait_send()
                out_end(layer, m, h).wait_send()
                out_local(layer, m, h).wait()

    neighbours = (place.fx, place.fy)

    def q_rows(owner, start=0, count=2 * width):
        return p_q.at[aligned((owner // 2) * (2 * width) + start, count, 32)]

    def q_half_copy(layer, way):
        return remote(q_rows(place.fd, way * width, width), half_q.at[layer, way], qh_send.at[layer, way], qh_recv.at[layer, way], place.on_plane(neighbours[way]))

    def q_plane_copy(layer, way):
        return remote(q_rows(neighbours[way]), plane_q.at[layer, way], qp_send.at[layer, way], qp_recv.at[layer, way], place.on_plane(neighbours[way]))

    def q_line_copy(layer):
        return remote(sum_q.at[layer], line_q.at[layer], ql_send.at[layer], ql_recv.at[layer], place.at(f, lax.rem(s + 2, g)))

    def q_columns(layer, group):
        return oq_ref.at[layer, :, aligned(group * GROUP, GROUP, 128)]

    def q_out(layer, to_core, near):
        to = s + 1 - 2 * lax.rem(s, 2) if near else s
        source = done_q.at[layer, aligned(to_core * width, width, 32)]
        slot = 0 if not near else 1 if to_core is core else 2
        return remote(source, q_columns(layer, me), qo_send.at[layer, slot], qo_recv.at[layer, me], place.at(f - core + to_core, to))

    def q_out_local(layer):
        return pltpu.make_async_copy(done_q.at[layer, aligned(core * width, width, 32)], q_columns(layer, me), qo_own.at[layer])

    def q_start(layer):
        for way in range(2):
            q_half_copy(layer, way).start()

    def q_sum_half(layer):
        for way in range(2):
            q_half_copy(layer, way).wait_recv()
            owner = (place.fy, place.fx)[way]
            add(p_q, (owner // 2) * (2 * width) + way * width, half_q.at[layer, way], width)
            q_plane_copy(layer, 1 - way).start()

    def q_sum_plane(layer):
        for way in range(2):
            q_plane_copy(layer, way).wait_recv()

        def body(at):
            mine, theirs = aligned((f // 2) * (2 * width) + at, 32, 32), aligned(at, 32, 32)
            total = p_q[mine, :].astype(f32) + plane_q[layer, 0, theirs, :].astype(f32) + plane_q[layer, 1, theirs, :].astype(f32)
            sum_q[layer, theirs, :] = total.astype(bf)

        each(2 * width, 32, body)
        q_line_copy(layer).start()
        for way in range(2):
            q_half_copy(layer, way).wait_send()
            q_plane_copy(layer, way).wait_send()

    def q_sum_line(layer):
        q_line_copy(layer).wait_recv()

        def body(at):
            rows_now = aligned(at, 32, 32)
            done_q[layer, rows_now, :] = sum_q[layer, rows_now, :] + line_q[layer, rows_now, :]

        each(2 * width, 32, body)
        other = 1 - core
        for to_core, near in ((core, True), (other, True), (other, False)):
            q_out(layer, to_core, near).start()
        q_out_local(layer).start()

    def q_finish(layer):
        q_line_copy(layer).wait_send()
        other = 1 - core
        for to_core, near in ((core, True), (other, True), (other, False)):
            q_out(layer, to_core, near).wait_send()
        q_out_local(layer).wait()
        for group in range(g):
            @pl.when(me != group)
            def _(group=group):
                source = done_q.at[layer, aligned(core * width, width, 32)]
                remote(source, q_columns(layer, group), qo_send.at[layer, 0], qo_recv.at[layer, group], partner).wait_recv()

    lane = lax.broadcasted_iota(jnp.int32, (rows, 128), 1)
    low_lane = lane < 64

    def vector(kind, layer):
        row = 2 * WIDE.index(kind) + layer
        return vec[row : row + 1, :]

    def norm_back(grad, residual, layer, gain_row, shift_row):
        standard, scale = standardize(residual)
        small_a[layer * SMALL + gain_row : layer * SMALL + gain_row + 1, :] = jnp.sum(grad * standard, axis=0, keepdims=True)
        small_a[layer * SMALL + shift_row : layer * SMALL + shift_row + 1, :] = jnp.sum(grad, axis=0, keepdims=True)
        inner = grad * vector(gain_row, layer)
        back = scale * (inner - jnp.mean(inner, -1, keepdims=True) - standard * jnp.mean(inner * standard, -1, keepdims=True))
        return back, standard

    def row_sum(layer, row, values):
        small_a[layer * SMALL + row : layer * SMALL + row + 1, : values.shape[1]] = jnp.sum(values.astype(f32), axis=0, keepdims=True)

    def go_home(slot, device):
        return remote(low.at[1], home.at[slot], home_send.at[slot], home_recv.at[slot], device)

    def send_home(slot):
        @pl.when(jnp.logical_not(place.stays))
        def _():
            go_home(slot, place.away_home).start()

        @pl.when(place.stays)
        def _():
            home[slot] = low[1]

    def sent_home(slot):
        @pl.when(jnp.logical_not(place.stays))
        def _():
            go_home(slot, place.away_home).wait_send()

    def came_home(slot):
        @pl.when(jnp.logical_not(place.stays))
        def _():
            go_home(slot, place.away_home).wait_recv()

    small_a[...] = jnp.zeros_like(small_a)
    live[...] = jnp.where(jnp.broadcast_to(mask_ref[0:1, :], (128, span)) < 0.0, 0.0, 1.0).T.astype(bf)
    loaded("y")
    low[1] = gn[...].astype(bf)
    send_home(1)
    loaded("cot")
    gx[...] = low[0].astype(f32)

    for layer in reversed(range(LAYERS)):
        loaded("r2")
        grad_two, _ = norm_back(gx[...], r2[...], layer, GAIN_F, SHIFT_F)
        gn[...] = grad_two
        low[0] = grad_two.astype(bf)
        row_sum(layer, B_DOWN, low[0])
        loaded("r1")
        normed = standardize(r1[...])[0] * vector(GAIN_A, layer) + vector(SHIFT_A, layer)
        norm_t[...] = normed.astype(bf).T
        if layer != last:
            sum_plane(last, U)
        pair_ready(layer, DN)
        pair_ready(layer, U)

        def ffn(c, carry):
            slot = lax.rem(c, 2)

            @pl.when(c + 1 < FF // D)
            def _():
                for copy in stream(layer, c + 1, 1 - slot):
                    copy.start()

            for copy in stream(layer, c, slot):
                copy.wait()
            branch = low[0]
            if layer != last:
                @pl.when(c == 1)
                def _():
                    q_sum_half(last)

                @pl.when(c == 3)
                def _():
                    sum_end(last, DN)

            grad_pre = (dot_t(branch, wd[slot]) * slope[slot].astype(f32)).astype(bf)
            now = chunk(c)
            small_a[pl.ds(layer * SMALL + B_UP + now, 1), :] = jnp.sum(grad_pre.astype(f32), axis=0, keepdims=True)
            columns = ff_columns(c)
            p_d[columns, :] = t_dot(act[slot], branch).astype(bf)
            pair_copy(layer, DN, now).start()
            p_u[layer, :, columns] = dot(norm_t[...], grad_pre).astype(bf)
            for k in range(half):
                up_pair(layer, c, k).start()
            gn[...] += dot_t(grad_pre, wu[slot])

            @pl.when(c > 0)
            def _():
                sum_chunk(layer, c - 1)

            return carry

        lax.fori_loop(0, FF // D, ffn, 0)
        if layer:
            for copy in stream(layer - 1, 0, 0):
                copy.start()
            load("r2", r2_ref.at[layer - 1], r2)
        sum_chunk(layer, FF // D - 1)
        pair_used(layer, DN)
        pair_used(layer, U)

        grad_one, _ = norm_back(gn[...], r1[...], layer, GAIN_A, SHIFT_A)
        gx[...] = grad_one
        if layer == last:
            sent_home(1)
        low[1] = grad_one.astype(bf)
        row_sum(layer, B_OUT, low[1])
        if layer:
            load("r1", r1_ref.at[layer - 1], r1)
        loaded("wo")

        def c_copy(i):
            return remote(gc_send.at[i - 1], gctx.at[me], c_send.at[layer, i], c_recv.at[layer, i], member(i))

        if layer != last:
            for i in range(1, g):
                remote(gc_send.at[i - 1], gctx.at[me], c_send.at[last, i], c_recv.at[last, i], member(i)).wait_send()

        def out_back(k, carry):
            b = lax.rem(me + k, g)
            base = b * (3 * HD)
            first = dot_t(low[1], wo[pl.ds(pl.multiple_of(base, 64), 128), :]).astype(bf)
            second = dot_t(low[1], wo[pl.ds(pl.multiple_of(base + 64, 64), 128), :]).astype(bf)
            second = jnp.where(low_lane, jnp.zeros_like(second), second)

            @pl.when(k < g)
            def _():
                gc_send[k - 1, :, 0:128] = first
                gc_send[k - 1, :, 128:256] = second
                c_copy(k).start()

            @pl.when(k == g)
            def _():
                gctx[me, :, 0:128] = first
                gctx[me, :, 128:256] = second

            return carry

        lax.fori_loop(1, g + 1, out_back, 0)
        if layer != last:
            sum_plane(last, O)
            q_sum_plane(last)
        loaded("ctx")
        for grp in range(g):
            base = grp * 3 * HD
            p_o[layer, base : base + 128, :] = t_dot(ctx[grp, :, 0:128], low[1]).astype(bf)
            p_o[layer, base + 128 : base + 192, :] = t_dot(ctx[grp, :, 128:256], low[1])[64:].astype(bf)
        if layer:
            load("wo", fo_ref.at[layer - 1], wo)
            load("ctx", ctx_ref.at[layer - 1], ctx)
        pair_ready(layer, O)
        for c in range(half):
            pair_copy(layer, O, c).start()
        sum_pair(layer, O)
        sum_half(layer, DN)
        if layer != last:
            sum_line(last, DN)

        loaded("hd")
        loaded("lse")
        for tile in range(1, 5):
            columns = slice(tile * 128, tile * 128 + 128)
            if tile == 3:
                full = hd[:, columns]
                wide_low = lax.broadcasted_iota(jnp.int32, full.shape, 1) < 64
                hd[:, columns] = jnp.where(wide_low, full, full * live[...])
            else:
                hd[:, columns] = hd[:, columns] * live[...]
        key_t[0:128, :] = hd[:, 128:256].T
        key_t[128:256, :] = hd[:, 512:640].T
        for acc in (acc_k, acc_v, acc_d, acc_e):
            acc[...] = jnp.zeros_like(acc)
        for i in range(1, g):
            c_copy(i).wait_recv()

        def attend(k, carry):
            if layer != last:
                @pl.when(k == 1)
                def _():
                    sum_end(last, U)

                @pl.when(k == 3)
                def _():
                    sum_end(last, O)

            @pl.when(k == 2)
            def _():
                sum_half(layer, U)

            b = lax.rem(me + k, g)
            block = pl.ds(pl.multiple_of(b * rows, rows), rows)
            q_a = hd[block, 0:128] * bf(HD**-0.5)
            q_d = hd[block, 384:512] * bf(HD**-0.5)
            g_a = gctx[b, :, 0:128]
            g_d = gctx[b, :, 128:256]
            zero = jnp.zeros_like(q_a)
            queries = (jnp.where(low_lane, q_a, zero), jnp.where(low_lane, zero, q_a), jnp.where(low_lane, q_d, zero))
            grads = (jnp.where(low_lane, g_a, zero), jnp.where(low_lane, zero, g_a), g_d)
            turned = []
            for h in range(3):
                keys = slice(512, 640) if h == 2 else slice(128, 256)
                values = slice(384, 512) if h == 2 else slice(256, 384)
                scores = dot_t(hd[:, keys], queries[h])
                prob = jnp.exp(jnp.minimum(scores - lse[h : h + 1, block], 0.0))
                grad_prob = dot_t(hd[:, values], grads[h])
                inner = jnp.sum(grad_prob * prob, axis=0, keepdims=True)
                grad_scores = (prob * (grad_prob - inner)).astype(bf)
                acc_value, acc_key = (acc_d, acc_e) if h == 2 else (acc_v, acc_k)
                acc_value[...] += dot(prob.astype(bf), grads[h])
                acc_key[...] += dot(grad_scores, queries[h])
                turned.append(dot(key_t[h * 64 : h * 64 + 64, :], grad_scores))
            grad_p[block, 0:128] = (jnp.concatenate(turned[:2], axis=0).T * HD**-0.5).astype(bf)
            acc_d[block, :] += jnp.concatenate([turned[2], jnp.zeros_like(turned[2])], axis=0).T * HD**-0.5
            return carry

        lax.fori_loop(1, g + 1, attend, 0)

        if layer:
            load("hd", heads_ref.at[layer - 1], hd)
            load("lse", lse_ref.at[layer - 1], lse)
        wide_low = lax.broadcasted_iota(jnp.int32, (span, 128), 1) < 64
        alive = live[...].astype(f32)
        grad_p[:, 128:256] = (acc_k[...] * alive).astype(bf)
        grad_p[:, 256:384] = (acc_v[...] * alive).astype(bf)
        grad_p[:, 384:512] = jnp.where(wide_low, acc_d[...], acc_d[...] * alive).astype(bf)
        grad_p[:, 512:640] = (acc_e[...] * alive).astype(bf)

        loaded("wq")
        across, aside = lax.rem(me + 2, g), me + 1 - 2 * core

        def back(quarter):
            return dot_t(grad_p[aligned(quarter * rows, rows, rows), :], wq[...])

        def aside_copy(k):
            return remote(aside_send.at[k], aside_in.at[k], x_send.at[layer, k], x_recv.at[layer, k], partner)

        aside_copies = [aside_copy(k) for k in range(2)]
        across_copy = remote(low.at[0], across_in, x_send.at[layer, 2], x_recv.at[layer, 2], place.member(across))
        for k, quarter in ((1, lax.rem(aside + 2, g)), (0, aside)):
            aside_send[k] = back(quarter).astype(bf)
            aside_copies[k].start()
        if layer == 0:
            sum_plane(layer, DN)
        crossing = back(across)
        aside_copies[1].wait_recv()
        low[0] = (crossing + aside_in[1].astype(f32)).astype(bf)
        across_copy.start()
        if layer:
            sum_plane(layer, DN)
        loaded("xb")
        p_q[...] = t_dot(xb[...], grad_p[...]).astype(bf)
        q_start(layer)
        small_a[pl.ds(layer * SMALL + VECS + me, 1), 0:GROUP] = jnp.sum(grad_p[...].astype(f32), axis=0, keepdims=True)
        sum_half(layer, O)
        gx[...] += back(me)
        aside_copies[0].wait_recv()
        gx[...] += aside_in[0].astype(f32)
        if layer != last:
            sum_line(last, U)
            sum_line(last, O)
            sum_end(layer, DN)
            q_sum_line(last)
        across_copy.wait_recv()
        gx[...] += across_in[...].astype(f32)
        if layer:
            across_copy.wait_send()
            for copy in aside_copies:
                copy.wait_send()
            load("xb", xb_ref.at[layer - 1], xb)
            load("wq", fq_ref.at[layer - 1], wq)

    low[1] = gx[...].astype(bf)
    send_home(0)
    a_copy = remote(small_a, land_a, sa_send, sa_recv, partner)
    a_copy.start()
    sum_plane(0, U)
    sum_line(0, DN)
    q_sum_half(0)
    a_copy.wait()
    small_b[...] = small_a[...] + land_a[...]
    b_copies = [
        remote(small_b, land_b.at[j], sb_send.at[j], sb_recv.at[j], place.on_plane(owner))
        for j, owner in enumerate((place.fx, place.fy, place.fd))
    ]
    for copy in b_copies:
        copy.start()
    sum_end(0, U)
    sum_plane(0, O)
    q_sum_plane(0)
    position = s * rows + lax.broadcasted_iota(jnp.int32, (rows, 1), 0)
    length = len_ref[0]
    came_home(0)
    memory_part[0] = dot(selection(place, rows, length).astype(bf), home[0]).astype(bf)
    for copy in b_copies:
        copy.wait()
    total = small_b[...] + land_b[0] + land_b[1] + land_b[2]
    small_a[...] = total
    from_lane = lax.broadcasted_iota(jnp.int32, (D, 128), 0)
    to_lane = lax.broadcasted_iota(jnp.int32, (D, 128), 1)
    pick = jnp.where(jnp.logical_and(from_lane == to_lane + f * width, to_lane < width), 1.0, 0.0)
    small_c[0] = jnp.zeros(small_c.shape[1:], f32)
    small_c[0, 0:SMALL_OUT, :] = jnp.dot(total, pick, precision=lax.Precision.HIGHEST, preferred_element_type=f32)
    for layer in range(LAYERS):
        base, row = layer * SMALL, SMALL_OUT + layer * 8
        up_row = small_a[pl.ds(base + B_UP + f // 2, 1), aligned(core * 384, 384, 128)]
        for t in range(3):
            small_c[0, row + t : row + t + 1, :] = up_row[:, 128 * t : 128 * t + 128]
        group_row = small_a[pl.ds(base + VECS + lax.rem(f, g), 1), :]
        turned = swap_halves(jnp.broadcast_to(group_row[:, 384:512], (8, 128)))[0:1]
        queries = f < g
        small_c[0, row + 3 : row + 4, :] = jnp.where(queries, group_row[:, 0:128], group_row[:, 256:384])
        small_c[0, row + 4 : row + 5, :] = jnp.where(queries, group_row[:, 384:512], turned)
    near = place.at(f, s + 1 - 2 * lax.rem(s, 2))
    far = place.at(f, lax.rem(s + 2, g))

    def c_stage(k, device):
        return [
            remote(small_c.at[k], land_c.at[k], sc_send.at[k, 0], sc_recv.at[k, 0], device),
            remote(memory_part.at[k], memory_land.at[k], sc_send.at[k, 1], sc_recv.at[k, 1], device),
        ]

    c_near, c_far = c_stage(0, near), c_stage(1, far)
    for copy in c_near:
        copy.start()
    is_token = jnp.logical_and(position >= MEM, position < length + MEM)
    home[0] = jnp.where(is_token, home[0], jnp.zeros_like(home[0]))
    tokens_copy = pltpu.make_async_copy(home.at[0], tokens_ref, store_sem.at[0])
    tokens_copy.start()
    came_home(1)
    home[1] = jnp.where(position < length + 2 * MEM, home[1], jnp.zeros_like(home[1]))
    result_copy = pltpu.make_async_copy(home.at[1], result_ref, store_sem.at[1])
    result_copy.start()
    sum_end(0, O)
    sum_line(0, U)
    for copy in c_near:
        copy.wait()
    small_c[1] = small_c[0] + land_c[0]
    memory_part[1] = memory_part[0] + memory_land[0]
    for copy in c_far:
        copy.start()
    sum_line(0, O)
    q_sum_line(0)
    for copy in c_far:
        copy.wait()
    small_ref[...] = small_c[1] + land_c[1]
    memory_ref[...] = memory_part[1].astype(f32) + memory_land[1].astype(f32)

    for i in range(1, g):
        remote(gc_send.at[i - 1], gctx.at[me], c_send.at[0, i], c_recv.at[0, i], member(i)).wait_send()
    sent_home(0)
    across_copy.wait_send()
    for copy in aside_copies:
        copy.wait_send()
    for layer in range(LAYERS):
        q_finish(layer)

    for layer in range(LAYERS):
        for m in range(3):
            line_done(layer, m)

    @pl.when(outer)
    def _():
        for layer in range(LAYERS):
            for m in range(3):
                for h in range(2):
                    end_copy(layer, m, h).wait_send()
                    out_end(layer, m, h).wait_recv()

    tokens_copy.wait()
    result_copy.wait()


def run_backward(n, g, lengths, mask, vec, cot, y, fq, fo, fu, fd, stored):
    rows, span = y.shape[0], y.shape[0] * g
    any_spec = pl.BlockSpec(memory_space=pl.ANY)
    vmem = pl.BlockSpec(memory_space=pltpu.VMEM)
    bf, f32 = jnp.bfloat16, jnp.float32
    half = n // 2
    wide = g * GROUP
    dims = ((D, D), (D, FF), (FF, D))
    width = D // n
    small = SMALL * LAYERS
    shapes = [((rows, D), bf, any_spec), ((rows, D), bf, any_spec), ((SMALL_OUT + 8 * LAYERS, 128), f32, vmem), ((MEM_ROWS, D), f32, vmem)]
    shapes += [((LAYERS, a // n, b), bf, any_spec) for a, b in ((D, wide),) + dims]
    dma, regular = pltpu.SemaphoreType.DMA, pltpu.SemaphoreType.REGULAR
    scratch = [
        pltpu.VMEM((D, GROUP), bf), pltpu.VMEM((D, D), bf), pltpu.VMEM((2, D, D), bf), pltpu.VMEM((2, D, D), bf),
        pltpu.VMEM((2, rows, D), bf), pltpu.VMEM((2, rows, D), bf), pltpu.VMEM((span, D), bf), pltpu.VMEM((span, GROUP), bf),
        pltpu.VMEM((8, span), f32), pltpu.VMEM((g, rows, CTX), bf), pltpu.VMEM((rows, D), f32), pltpu.VMEM((rows, D), f32),
    ]
    scratch += [pltpu.VMEM((LAYERS,) + shape, bf) for shape in dims[:2]] + [pltpu.VMEM(dims[2], bf)]
    scratch += [pltpu.VMEM((half, a // n, b), bf) for a, b in dims]
    scratch += [pltpu.VMEM((2, a // n // 2, b), bf) for a, b in dims]
    scratch += [pltpu.VMEM((2, a // n, b), bf) for a, b in dims]
    scratch += [pltpu.VMEM((LAYERS, a // n, b), bf) for a, b in dims]
    scratch += [pltpu.VMEM((LAYERS, a // n, b), bf) for a, b in dims]
    scratch += [pltpu.VMEM((a // n, b), bf) for a, b in dims]
    scratch += [
        pltpu.VMEM((D, GROUP), bf), pltpu.VMEM((LAYERS, 2, width, GROUP), bf), pltpu.VMEM((LAYERS, 2, 2 * width, GROUP), bf),
        pltpu.VMEM((LAYERS, 2 * width, GROUP), bf), pltpu.VMEM((LAYERS, 2 * width, GROUP), bf), pltpu.VMEM((LAYERS, 2 * width, GROUP), bf),
    ]
    scratch += [
        pltpu.VMEM((rows, D), f32), pltpu.VMEM((rows, D), f32), pltpu.VMEM((D, rows), bf), pltpu.VMEM((2, rows, D), bf),
        pltpu.VMEM((span, 128), bf), pltpu.VMEM((2, rows, D), bf),
        pltpu.VMEM((g - 1, rows, CTX), bf), pltpu.VMEM((g, rows, CTX), bf), pltpu.VMEM((256, span), bf),
        pltpu.VMEM((span, 128), f32), pltpu.VMEM((span, 128), f32), pltpu.VMEM((span, 128), f32), pltpu.VMEM((span, 128), f32),
        pltpu.VMEM((span, GROUP), bf), pltpu.VMEM((2, rows, D), bf), pltpu.VMEM((2, rows, D), bf), pltpu.VMEM((rows, D), bf),
        pltpu.VMEM((small, D), f32), pltpu.VMEM((small, D), f32), pltpu.VMEM((2, small + 8 * LAYERS, 128), f32),
        pltpu.VMEM((small, D), f32), pltpu.VMEM((3, small, D), f32), pltpu.VMEM((2, small + 8 * LAYERS, 128), f32),
        pltpu.VMEM((2, MEM_ROWS, D), bf), pltpu.VMEM((2, MEM_ROWS, D), bf),
        dma((10,)), dma((4, 2)), dma((LAYERS, 3, half)), dma((LAYERS, 3, half)), dma((LAYERS, half, half)), dma((LAYERS, half, half)), dma((LAYERS, 3, 2)), dma((LAYERS, 3, 2)), dma((LAYERS, half, 2)), dma((LAYERS, half, 2)),
        dma((LAYERS, 3, 2)), dma((LAYERS, 3, 2)), dma((LAYERS, 3, 4)), dma((LAYERS, 3, 4)), dma((LAYERS, 3, 2)), dma((LAYERS, 3, 2)), dma((LAYERS, 3, 2)),
        dma((LAYERS, g)), dma((LAYERS, g)), dma((LAYERS, 3)), dma((LAYERS, 3)), dma((LAYERS, 2)), dma((LAYERS, 2)), dma((LAYERS, 2)), dma((LAYERS, 2)),
        dma((LAYERS,)), dma((LAYERS,)), dma((LAYERS, 3)), dma((LAYERS, g)), dma((LAYERS,)), dma(()), dma(()),
        dma((3,)), dma((3,)), dma((2, 2)), dma((2, 2)), dma((2,)), dma((2,)), dma((2,)),
        regular((3,)), regular((3, 2)), regular((3, 2)), regular((3, 2)),
    ]
    return pl.pallas_call(
        functools.partial(backward_kernel, n, g),
        name="backward",
        out_shape=[jax.ShapeDtypeStruct(a, b) for a, b, _ in shapes],
        in_specs=[pl.BlockSpec(memory_space=pltpu.SMEM)] + [vmem] * 2 + [any_spec] * 14,
        out_specs=[c for _, _, c in shapes],
        scratch_shapes=scratch,
        compiler_params=pltpu.CompilerParams(
            collective_id=1, has_side_effects=True, vmem_limit_bytes=64 * 1024 * 1024 - 65536
        ),
    )(lengths, mask, vec, cot, y, fq, fo, fu, fd, *stored)


def finish_kernel(n, g, result_ref, tokens_ref, small_ref, memory_ref, oq_ref, oo_ref, ou_ref, od_ref, *outs):
    result, tokens, memory, q, bqv, o, bout, ga, sa, u, bup, d, bdown, gf, sf = outs
    f32 = jnp.float32
    result[...] = result_ref[...].astype(f32)
    tokens[...] = tokens_ref[...].astype(f32)
    o[...] = oo_ref[...].astype(f32)
    u[...] = ou_ref[...].astype(f32)
    d[...] = od_ref[...].astype(f32)
    low = lax.broadcasted_iota(jnp.int32, (q.shape[1], 128), 1) < 64

    def take(group, tile):
        at = group * GROUP + tile * 128
        return oq_ref[0, :, at : at + 128].astype(f32)

    def give(kind, tile, values):
        at = kind * D + tile * 128
        q[0, :, at : at + 128] = values

    ungroup_tiles(take, give, low)
    width = D // n
    for row in range(2 * MEM):
        memory[row] = memory_ref[row : row + 1, :]
    for layer in range(LAYERS):
        row = slice(layer, layer + 1)
        for ref, kind in ((bout, B_OUT), (ga, GAIN_A), (sa, SHIFT_A), (bdown, B_DOWN), (gf, GAIN_F), (sf, SHIFT_F)):
            at = layer * SMALL + kind
            ref[row, :] = small_ref[at : at + 1, 0:width]
        at = SMALL_OUT + layer * 8
        for t in range(3):
            bup[row, 128 * t : 128 * t + 128] = small_ref[at + t : at + t + 1, :]
        bqv[row, 0:128] = small_ref[at + 3 : at + 4, :]
        bqv[row, 128:192] = small_ref[at + 4 : at + 5, 0:64]


def run_finish(n, g, result, tokens, small, memory, oq, oo, ou, od):
    f32 = jnp.float32
    rows = result.shape[0]
    steps = 4

    def by_rows(width):
        return pl.BlockSpec((rows // (LAYERS * steps), width), lambda layer, k: (layer * steps + k, 0))

    def by_layer(depth, width):
        return pl.BlockSpec((1, depth // steps, width), lambda layer, k: (layer, k, 0))

    def whole(shape):
        return pl.BlockSpec(shape, lambda layer, k: (0,) * len(shape))

    width = D // n
    wide, deep = (LAYERS, width), FF // n
    shapes = [
        ((rows, D), by_rows(D)), ((rows, D), by_rows(D)), ((2 * MEM, 1, D), None), ((LAYERS, width, 3 * D), by_layer(width, 3 * D)),
        ((LAYERS, 2 * width), None), ((LAYERS, width, D), by_layer(width, D)), (wide, None), (wide, None), (wide, None),
        ((LAYERS, width, FF), by_layer(width, FF)), ((LAYERS, deep), None), ((LAYERS, deep, D), by_layer(deep, D)), (wide, None), (wide, None), (wide, None),
    ]
    return pl.pallas_call(
        functools.partial(finish_kernel, n, g),
        name="finish",
        grid=(LAYERS, steps),
        out_shape=[jax.ShapeDtypeStruct(shape, f32) for shape, _ in shapes],
        in_specs=[by_rows(D), by_rows(D), whole(small.shape), whole(memory.shape), by_layer(width, g * GROUP), by_layer(width, D), by_layer(width, FF), by_layer(deep, D)],
        out_specs=[spec or whole(shape) for shape, spec in shapes],
        compiler_params=pltpu.CompilerParams(vmem_limit_bytes=60 * 1024 * 1024),
    )(result, tokens, small, memory, oq, oo, ou, od)


def kernel_body(
    tokens, memory, lengths, w_qkv, b_qv, w_out, b_out, gain_attn, shift_attn, w_up, b_up, w_down, b_down, gain_ffn, shift_ffn, cotangent,
):
    n, g = lax.axis_size("fsdp"), lax.axis_size("seq")
    vectors = (b_qv, b_out, gain_attn, shift_attn, b_up, b_down, gain_ffn, shift_ffn)
    y, cot, mask, vec, fq, fo, fu, fd, *stored = run_forward(n, g, lengths, tokens, memory, vectors, cotangent, w_qkv, w_out, w_up, w_down)
    result, grad_tokens, grad_memory, *rest = run_finish(n, g, *run_backward(n, g, lengths, mask, vec, cot, y, fq, fo, fu, fd, stored))
    return (result, grad_tokens, grad_memory.transpose(1, 0, 2), *rest)


def pick_body(mesh):
    return kernel_body if mesh.shape["fsdp"] == 8 and mesh.shape["seq"] == 4 else plain_body


def solution(mesh):
    in_specs = (
        P(("fsdp", "seq"), None),
        P("fsdp", None, None),
        P("fsdp"),
        P(None, "fsdp", None),
        P(None, "fsdp"),
        P(None, "fsdp", None),
        P(None, "fsdp"),
        P(None, "fsdp"),
        P(None, "fsdp"),
        P(None, "fsdp", None),
        P(None, "fsdp"),
        P(None, "fsdp", None),
        P(None, "fsdp"),
        P(None, "fsdp"),
        P(None, "fsdp"),
        P(("fsdp", "seq"), None),
    )
    out_specs = (
        P(("fsdp", "seq"), None),
        P(("fsdp", "seq"), None),
        P("fsdp", None, None),
        P(None, "fsdp", None),
        P(None, "fsdp"),
        P(None, "fsdp", None),
        P(None, "fsdp"),
        P(None, "fsdp"),
        P(None, "fsdp"),
        P(None, "fsdp", None),
        P(None, "fsdp"),
        P(None, "fsdp", None),
        P(None, "fsdp"),
        P(None, "fsdp"),
        P(None, "fsdp"),
    )
    return jax.shard_map(pick_body(mesh), mesh=mesh, in_specs=in_specs, out_specs=out_specs, check_vma=False)
```
